32 devices in a mesh: scene: 2 (over x), tile: 8 (over z, y), date: 2 (over core).
Axes of the slice: x: 2, y: 2, z: 4, core: 2. Of those that a mesh axis runs over, the one named last changes fastest.
Arguments:
- slc_real: bfloat16 [32, 512, 256], P('date', ('scene', 'tile')), parts along dimension 1, may hold values from -4.5 to 4.5
- slc_imag: bfloat16 [32, 512, 256], P('date', ('scene', 'tile')), parts along dimension 1, may hold values from -4.5 to 4.5
- pair_offset: int32 [32, 4], replicated, may hold values from 1 to 5, as said below
- pair_weight: int32 [128, 512, 256], P(None, ('scene', 'tile', 'date')), parts along dimension 1, may hold values from 1 to 255
Outputs:
- increments: float32 [31, 512, 256], P(None, ('scene', 'tile', 'date')), parts along dimension 1
The draws below stay inside these ranges and needn't reach their ends.
There are 2 independent parts, one for each index of `scene`. The reference program is written for one: setup_inputs(seed, part) draws one part's arguments, and reference() takes and returns one part's arrays. A program takes and returns all parts, laid end to end along the dimension named above; an argument that names none is the same for every part. Nothing has to cross between parts.
Inputs may be any that keep to these rules, and one draw needn't show every extreme that they name: `pair_offset`: each row holds 4 different offsets in increasing order; 1 and 5 are in every row.
All inputs are finite; a program needn't handle non-finite values.
Results may differ from the reference program's by a relative error of at most 0.0003.
Values may be sent and summed in bfloat16 or wider, within the bound.
No kernel may reach another device: no remote copies, remote signals or barrier semaphores. Data moves between devices by JAX's collectives and lax.ppermute only.
A program may use at most 128 MiB of HBM per device.

```python
import math
import jax
import jax.numpy as jnp
from jax import lax

COLS = 256
K = 4
SPAN = 5
SWEEPS = 8
PASSES = 3
STEPS = 2
DATES = 32
PAIRS = 128
INCR = 31
ROWS = 256


def draw_pair_offset(key, part):
    dropped = jax.random.randint(key, (DATES, 1), 2, SPAN).astype(jnp.int32)
    ladder = jnp.arange(1, K + 1, dtype=jnp.int32)[None, :]
    return (ladder + (ladder >= dropped).astype(jnp.int32)).astype(jnp.int32)


def scene_images(key):
    keys = jax.random.split(jax.random.fold_in(key, 9173), 5)
    shape = (DATES, ROWS, COLS)
    scatter = jax.random.uniform(keys[1], (1, ROWS, COLS), jnp.float32, -math.pi, math.pi)
    amplitude = jnp.exp(jax.random.uniform(keys[0], (1, ROWS, COLS), jnp.float32, 0.0, math.log(3.0)))
    motion = 0.5 * jax.random.truncated_normal(keys[2], -3.0, 3.0, shape, jnp.float32)
    noise_re = 0.4 * jax.random.truncated_normal(keys[3], -3.0, 3.0, shape, jnp.float32)
    noise_im = 0.4 * jax.random.truncated_normal(keys[4], -3.0, 3.0, shape, jnp.float32)
    phase = scatter + jnp.cumsum(motion, axis=0)
    real_part = amplitude * jnp.cos(phase) + noise_re
    imag_part = amplitude * jnp.sin(phase) + noise_im
    return (real_part, imag_part)


def draw_slc_real(key, part):
    return scene_images(key)[0].astype(jnp.bfloat16)


def draw_slc_imag(key, part):
    return scene_images(key)[1].astype(jnp.bfloat16)


def set_ends(drawn, key, least, high):
    place = [jax.random.randint(jax.random.fold_in(key, axis), (), 0, length) for axis, length in enumerate(drawn.shape)]
    widest = drawn.shape.index(max(drawn.shape))
    neighbour = place[:widest] + [(place[widest] + 1) % drawn.shape[widest]] + place[widest + 1:]
    return drawn.at[tuple(place)].set(least).at[tuple(neighbour)].set(high)


def setup_inputs(seed: int = 0, part: int = 0) -> dict:
    streams_of = jax.random.split(jax.random.key(seed), 5)
    part_splits = jax.random.split(jax.random.fold_in(streams_of[4], part), 5)
    slc_real = draw_slc_real(jax.random.fold_in(jax.random.fold_in(streams_of[4], part), 71), part)
    slc_imag = draw_slc_imag(jax.random.fold_in(jax.random.fold_in(streams_of[4], part), 71), part)
    pair_offset = draw_pair_offset(jax.random.fold_in(streams_of[4], 71), part)
    pair_weight = set_ends(jax.random.randint(part_splits[3], (PAIRS, ROWS, COLS), 1, 256), jax.random.fold_in(part_splits[3], 1), 1, 255).astype(jnp.int32)
    return {"slc_real": slc_real, "slc_imag": slc_imag, "pair_offset": pair_offset, "pair_weight": pair_weight}


unwrap_damping = 0.08
column_weight = 0.15
solve_damping = 0.1
residual_scale = 0.3

def from_left(values):
    widths = [(0, 0)] * (values.ndim - 1) + [(1, 0)]
    return jnp.pad(values[..., :-1], widths)

def from_right(values):
    widths = [(0, 0)] * (values.ndim - 1) + [(0, 1)]
    return jnp.pad(values[..., 1:], widths)

def coupling(here_re, here_im, there_re, there_im, weight):
    magnitude = jnp.sqrt((here_re * here_re + here_im * here_im) * (there_re * there_re + there_im * there_im))
    link_value = weight * magnitude / (magnitude + 1.0)
    slope_value = (here_im * there_re - here_re * there_im) / (magnitude + 1.0)
    return (link_value, slope_value)

def box_mean(values):
    row_sum = values[..., :-2, :] + values[..., 1:-1, :] + values[..., 2:, :]
    return (from_left(row_sum) + row_sum + from_right(row_sum)) / 9.0

def cell_terms(smooth_re, smooth_im):
    centre_re = smooth_re[..., 1:-1, :]
    centre_im = smooth_im[..., 1:-1, :]
    link_up, slope_up = coupling(centre_re, centre_im, smooth_re[..., :-2, :], smooth_im[..., :-2, :], 1.0)
    link_down, slope_down = coupling(centre_re, centre_im, smooth_re[..., 2:, :], smooth_im[..., 2:, :], 1.0)
    link_left, slope_left = coupling(centre_re, centre_im, from_left(centre_re), from_left(centre_im), column_weight)
    link_right, slope_right = coupling(centre_re, centre_im, from_right(centre_re), from_right(centre_im), column_weight)
    denominator = link_up + link_down + link_left + link_right + unwrap_damping
    source = link_up * slope_up + link_down * slope_down + link_left * slope_left + link_right * slope_right
    return (link_up, link_down, link_left, link_right, denominator, source)

def relax_once(unwrapped, above, below, stencil):
    link_up, link_down, link_left, link_right, denominator, source = stencil
    summed = source + link_up * above + link_down * below + link_left * from_left(unwrapped) + link_right * from_right(unwrapped)
    return summed / denominator

def pair_tables(pair_offset):
    date_count = pair_offset.shape[0]
    per_date = pair_offset.shape[1]
    first_date = jnp.arange(date_count * per_date, dtype=jnp.int32) // per_date
    second = first_date + pair_offset.reshape(-1)
    validity = (second < date_count).astype(jnp.float32)
    unknown = jnp.arange(date_count - 1, dtype=jnp.int32)
    design = ((unknown[None, :] >= first_date[:, None]) & (unknown[None, :] < second[:, None])).astype(jnp.float32)
    return (validity, design)

def forward(design, values):
    return jnp.dot(design, values, precision=lax.Precision.HIGHEST, preferred_element_type=jnp.float32)

def backward(design, values):
    return jnp.dot(design.T, values, precision=lax.Precision.HIGHEST, preferred_element_type=jnp.float32)

def invert(phases, base_weight, design):
    increments = jnp.zeros((design.shape[1], phases.shape[1]), jnp.float32)
    for pass_index in range(PASSES):
        scaled = (phases - forward(design, increments)) / residual_scale
        weights = base_weight / (1.0 + scaled * scaled)
        diagonal = backward(design, weights) + solve_damping
        for step_index in range(STEPS):
            gradient = backward(design, weights * (phases - forward(design, increments))) - solve_damping * increments
            increments = increments + 1.0 / SPAN * gradient / diagonal
    return increments

def reference(slc_real, slc_imag, pair_offset, pair_weight):
    validity, design = pair_tables(pair_offset)
    date_count = pair_offset.shape[0]

    def unwrap_one(pair_number):
        first_date = pair_number // K
        second = first_date + pair_offset[first_date, pair_number % K]
        kept = validity[pair_number]
        clipped = jnp.minimum(second, date_count - 1).astype(jnp.int32)
        first_re = lax.dynamic_index_in_dim(slc_real, first_date, 0, keepdims=False).astype(jnp.float32)
        first_im = lax.dynamic_index_in_dim(slc_imag, first_date, 0, keepdims=False).astype(jnp.float32)
        second_re = lax.dynamic_index_in_dim(slc_real, clipped, 0, keepdims=False).astype(jnp.float32)
        second_im = lax.dynamic_index_in_dim(slc_imag, clipped, 0, keepdims=False).astype(jnp.float32)
        pair_real = kept * (first_re * second_re + first_im * second_im)
        pair_imag = kept * (first_im * second_re - first_re * second_im)
        smooth_re = box_mean(jnp.pad(pair_real, ((1, 1), (0, 0))))
        smooth_im = box_mean(jnp.pad(pair_imag, ((1, 1), (0, 0))))
        stencil = cell_terms(jnp.pad(smooth_re, ((1, 1), (0, 0))), jnp.pad(smooth_im, ((1, 1), (0, 0))))
        unwrapped = jnp.zeros_like(smooth_re)
        for sweep_index in range(SWEEPS):
            above = jnp.pad(unwrapped[:-1], ((1, 0), (0, 0)))
            below = jnp.pad(unwrapped[1:], ((0, 1), (0, 0)))
            unwrapped = relax_once(unwrapped, above, below, stencil)
        return unwrapped
    phases = lax.map(unwrap_one, jnp.arange(PAIRS, dtype=jnp.int32))
    base_weight = pair_weight.astype(jnp.float32) / 255.0 * validity[:, None, None]
    increments = invert(phases.reshape(PAIRS, -1), base_weight.reshape(PAIRS, -1), design)
    return increments.reshape(INCR, ROWS, COLS)
```

```python
import functools

import jax
import jax.numpy as jnp
from jax import lax
from jax.experimental import pallas as pl
from jax.experimental.pallas import tpu as pltpu
from jax.sharding import PartitionSpec as P

K = 4
SPAN = 5
SWEEPS = 8
PASSES = 3
STEPS = 2

unwrap_damping = 0.08
column_weight = 0.15
solve_damping = 0.1
residual_scale = 0.3

LANES = 128
SUB = 8
HALO = SWEEPS + 1
F32 = jnp.float32
BF16 = jnp.bfloat16


def al(x):
    return pl.multiple_of(x, SUB)


def vreg(ref, row):
    return ref[pl.ds(row, SUB), :]


def perm_matrix(transpose):
    n = 2 * LANES
    a = lax.broadcasted_iota(jnp.int32, (n, n), 0)
    b = lax.broadcasted_iota(jnp.int32, (n, n), 1)
    col, place = (b, a) if transpose else (a, b)
    target = (col % 2) * LANES + col // 2
    return jnp.where(place == target, 1.0, 0.0).astype(BF16)


def pack_kernel(halo, re_ref, im_ref, all_ref, same_ref, cross_ref, flat):
    dates, rows, columns = re_ref.shape
    side = lax.axis_index("date")
    perm = perm_matrix(False)
    for part, ref in enumerate((re_ref, im_ref)):
        block = ref[...].reshape(dates * rows, columns)
        out = jnp.dot(block, perm, preferred_element_type=F32)
        for half in range(2):
            flat[part, half] = out[:, half * LANES : (half + 1) * LANES]
    for row in range(rows):
        for part in range(2):
            for half in range(2):
                tile = flat[part, half, pl.ds(row, dates, stride=rows), :]
                all_ref[row, part, half] = tile.astype(BF16)
    last = rows - halo
    same_ref[...] = all_ref[pl.ds(last * (1 - side), halo)]
    cross_ref[...] = all_ref[pl.ds(last * side, halo)]


def pack(slc_real, slc_imag):
    dates, rows, columns = slc_real.shape
    shape = lambda count: jax.ShapeDtypeStruct((count, 2, 2, dates, LANES), BF16)
    vm = pl.BlockSpec(memory_space=pltpu.VMEM)
    return pl.pallas_call(
        functools.partial(pack_kernel, HALO),
        out_shape=(shape(rows), shape(HALO), shape(HALO)),
        in_specs=[vm, vm],
        out_specs=(vm, vm, vm),
        scratch_shapes=[pltpu.VMEM((2, 2, dates * rows, LANES), F32)],
        name="pack",
    )(slc_real, slc_imag)


def main_kernel(
    own_ref, partner_ref, same_ref, cross_ref, offset_ref, weight_hbm, out_hbm,
    img, cre, cim, zre, zim, mag, hle, hlo, dh, sh, rr, ss, aa, ya, yb,
    yy, wraw, wf, vv, aw, ag, wk, msk, vfin, obuf, wsem, osem,
):
    half_dates = own_ref.shape[3]
    dates = 2 * half_dates
    tile_rows = own_ref.shape[0]
    R = tile_rows // 2
    H = HALO
    NR = R + 2 * H
    NZ = NR - 2
    DP = dates + SUB
    NF = dates // SUB
    side = lax.axis_index("date")
    tile = lax.axis_index("tile")
    tiles = lax.axis_size("tile")

    copies = []
    for half in range(2):
        copies.append(
            pltpu.make_async_copy(
                weight_hbm.at[:, :, pl.ds(half * LANES, LANES)], wraw.at[half], wsem.at[half]
            )
        )
    for copy in copies:
        copy.start()

    offsets = offset_ref[...]
    m1 = jnp.where(offsets[:, 1:2] == 2, 1.0, 0.0).astype(F32)
    m2 = jnp.where(offsets[:, 2:3] == 4, 1.0, 0.0).astype(F32)
    msk[0] = jnp.broadcast_to(m1, (dates, LANES))
    msk[1] = jnp.broadcast_to(m2, (dates, LANES))
    first = lax.broadcasted_iota(jnp.int32, (dates, 1), 0)
    for k in range(K):
        ok = jnp.where(first + offsets[:, k : k + 1] < dates, 1.0, 0.0).astype(F32)
        msk[2 + k] = jnp.broadcast_to(ok, (dates, LANES))

    lane = lax.broadcasted_iota(jnp.int32, (SUB, LANES), 1)
    at_first = lane == 0
    at_last = lane == LANES - 1
    zero = jnp.zeros((SUB, LANES), F32)

    third = 1.0 / 3.0
    o_date = al(half_dates * side)
    p_date = al(half_dates * (1 - side))

    def put(rho, o_tile_ref, o_row, p_tile_ref, p_row):
        for part in range(2):
            for half in range(2):
                base = ((rho * 2 + part) * 2 + half) * DP
                img[pl.ds(al(base + o_date), half_dates), :] = (
                    o_tile_ref[o_row, part, half].astype(F32) * third
                )
                img[pl.ds(al(base + p_date), half_dates), :] = (
                    p_tile_ref[p_row, part, half].astype(F32) * third
                )
                img[pl.ds(al(base + dates), SUB), :] = zero

    base_row = (R - H) * side
    base_rho = H * (1 - side)

    def put_tile(i, c):
        put(base_rho + i, own_ref, base_row + i, partner_ref, base_row + i)
        return c

    lax.fori_loop(0, R + H, put_tile, 0)
    halo_rho = (R + H) * side

    def put_halo(i, c):
        put(halo_rho + i, same_ref, i, cross_ref, i)
        return c

    lax.fori_loop(0, H, put_halo, 0)

    def roll_right(x):
        return pltpu.roll(x, 1, 1)

    def roll_left(x):
        return pltpu.roll(x, LANES - 1, 1)

    def gix(row, k, half):
        return al(((row * K + k) * 2 + half) * SUB)

    def block(ft, carry):
        f0 = al(ft * SUB)
        sel1 = vreg(msk.at[0], f0) > 0.5
        sel2 = vreg(msk.at[1], f0) > 0.5

        def form(rho):
            def image(part, half, shift):
                return vreg(img, ((rho * 2 + part) * 2 + half) * DP + f0 + shift)

            pair = {}
            for half in range(2):
                a_re, a_im = image(0, half, 0), image(1, half, 0)
                second = [(image(0, half, o), image(1, half, o)) for o in range(1, SPAN + 1)]
                pick = lambda mask, i, j: tuple(
                    jnp.where(mask, x, y) for x, y in zip(second[i - 1], second[j - 1])
                )
                chosen = (second[0], pick(sel1, 2, 3), pick(sel2, 4, 3), second[4])
                for k in range(K):
                    b_re, b_im = chosen[k]
                    pair[0, k, half] = a_re * b_re + a_im * b_im
                    pair[1, k, half] = a_im * b_re - a_re * b_im
            for part, ref in enumerate((cre, cim)):
                for k in range(K):
                    even, odd = pair[part, k, 0], pair[part, k, 1]
                    both = even + odd
                    ref[pl.ds(gix(rho, k, 0), SUB), :] = both + jnp.where(at_first, 0.0, roll_right(odd))
                    ref[pl.ds(gix(rho, k, 1), SUB), :] = both + jnp.where(at_last, 0.0, roll_left(even))

        UA = 2

        def phase_a(i, c):
            for u in range(UA):
                form(i * UA + u)
            return c

        lax.fori_loop(0, NR // UA, phase_a, 0)

        def edge(m, cross, scale):
            q = 1.0 / (m + 1.0)
            link = m * q
            if scale is not None:
                link = link * scale
            return link, link * (cross * q)

        def smooth(j):
            z = {}
            for k in range(K):
                for half in range(2):
                    i0, i1, i2 = (gix(j + d, k, half) for d in range(3))
                    re = vreg(cre, i0) + vreg(cre, i1) + vreg(cre, i2)
                    im = vreg(cim, i0) + vreg(cim, i1) + vreg(cim, i2)
                    sq = re * re + im * im
                    mg = sq * lax.rsqrt(jnp.maximum(sq, 1e-30))
                    zre[pl.ds(i0, SUB), :] = re
                    zim[pl.ds(i0, SUB), :] = im
                    mag[pl.ds(i0, SUB), :] = mg
                    z[k, half] = re, im, mg
            for k in range(K):
                e_re, e_im, e_mg = z[k, 0]
                o_re, o_im, o_mg = z[k, 1]
                le, ge = edge(e_mg * o_mg, e_im * o_re - e_re * o_im, column_weight)
                n_re, n_im, n_mg = roll_left(e_re), roll_left(e_im), roll_left(e_mg)
                m = jnp.where(at_last, 0.0, o_mg * n_mg)
                lo, go = edge(m, o_im * n_re - o_re * n_im, column_weight)
                i0, i1 = gix(j, k, 0), gix(j, k, 1)
                damped = le + unwrap_damping
                hle[pl.ds(i0, SUB), :] = le
                hle[pl.ds(i1, SUB), :] = lo
                dh[pl.ds(i0, SUB), :] = damped + roll_right(lo)
                dh[pl.ds(i1, SUB), :] = damped + lo
                sh[pl.ds(i0, SUB), :] = ge - roll_right(go)
                sh[pl.ds(i1, SUB), :] = go - ge

        UB = 2

        def phase_b(i, c):
            for u in range(UB):
                smooth(i * UB + u)
            return c

        lax.fori_loop(0, NZ // UB, phase_b, 0)

        @pl.when((tile == 0) & (side == 0))
        def _():
            for k in range(K):
                for half in range(2):
                    mag[pl.ds(gix(H - 2, k, half), SUB), :] = zero

        @pl.when((tile == tiles - 1) & (side == 1))
        def _():
            for k in range(K):
                for half in range(2):
                    mag[pl.ds(gix(H - 1 + R, k, half), SUB), :] = zero

        def vertical(j, k, half):
            i0, i1 = gix(j, k, half), gix(j + 1, k, half)
            m = vreg(mag, i0) * vreg(mag, i1)
            return edge(m, vreg(zim, i0) * vreg(zre, i1) - vreg(zre, i0) * vreg(zim, i1), None)

        start = []
        for k in range(K):
            for half in range(2):
                start += [*vertical(0, k, half), zero]

        def stencil(j, before):
            after = []
            for k in range(K):
                root = {}
                for half in range(2):
                    i0 = gix(j, k, half)
                    v, f = vertical(j, k, half)
                    n = (k * 2 + half) * 3
                    vm, fm, rm = before[n : n + 3]
                    den = vreg(dh, i0) + vm + v
                    src = vreg(sh, i0) + f - fm
                    r = lax.rsqrt(den)
                    rr[pl.ds(i0, SUB), :] = r
                    ss[pl.ds(i0, SUB), :] = src * r
                    aa[pl.ds(i0, SUB), :] = vm * (r * rm)
                    root[half] = r
                    after += [v, f, r]
                i0, i1 = gix(j, k, 0), gix(j, k, 1)
                hlo[pl.ds(i0, SUB), :] = vreg(hle, i0) * (root[0] * root[1])
                hlo[pl.ds(i1, SUB), :] = vreg(hle, i1) * (root[1] * roll_left(root[0]))
            return after

        UC = 2

        def phase_c(i, c):
            for u in range(UC):
                c = stencil(1 + i * UC + u, c)
            return tuple(c)

        lax.fori_loop(0, (NZ - 2) // UC, phase_c, tuple(start))

        def sweeps(k, c):
            src_ref = ss
            for s in range(1, SWEEPS):
                left = SWEEPS - 1 - s
                dst_ref = (ya, yb)[s % 2]
                lo, hi = H - 1 - left, H - 1 + R + left
                for j in range(lo, hi):
                    y = [[vreg(src_ref, gix(j + d, k, half)) for half in range(2)] for d in (-1, 0, 1)]
                    i0, i1 = gix(j, k, 0), gix(j, k, 1)
                    e, o = vreg(hlo, i0), vreg(hlo, i1)
                    new = []
                    for half in range(2):
                        i = (i0, i1)[half]
                        up, dn = vreg(aa, i), vreg(aa, gix(j + 1, k, half))
                        new.append(vreg(ss, i) + up * y[0][half] + dn * y[2][half])
                    even = new[0] + e * y[1][1] + roll_right(o * y[1][1])
                    odd = new[1] + e * y[1][0] + o * roll_left(y[1][0])
                    if s < SWEEPS - 1:
                        dst_ref[pl.ds(i0, SUB), :] = even
                        dst_ref[pl.ds(i1, SUB), :] = odd
                    else:
                        row = j - (H - 1)
                        for half, value in enumerate((even, odd)):
                            r = vreg(rr, gix(j, k, half)) * (1.0 / residual_scale)
                            place = (((row * K + k) * NF + ft) * 2 + half) * SUB
                            yy[pl.ds(al(place), SUB), :] = value * r
                src_ref = dst_ref
            return c

        lax.fori_loop(0, K, sweeps, 0)
        return carry

    lax.fori_loop(0, NF, block, 0)

    for copy in copies:
        copy.wait()
    perm = perm_matrix(False)

    def weights(row, c):
        rows = []
        for k in range(K):
            halves = [
                wraw.at[half].reshape(K * dates * R, LANES)[pl.ds(k * R + row, dates, stride=K * R), :]
                for half in range(2)
            ]
            rows.append(jnp.concatenate(halves, axis=1).astype(F32).astype(BF16))
        out = jnp.dot(jnp.concatenate(rows, axis=0), perm, preferred_element_type=F32)
        for k in range(K):
            for t in range(NF):
                for half in range(2):
                    place = (((row * K + k) * NF + t) * 2 + half) * SUB
                    x = out[(k * NF + t) * SUB : (k * NF + t + 1) * SUB, half * LANES : (half + 1) * LANES]
                    if (t + 1) * SUB + SPAN - 1 >= dates:
                        x = x * msk[2 + k, pl.ds(t * SUB, SUB), :]
                    wf[pl.ds(al(place), SUB), :] = x
        return c

    lax.fori_loop(0, R, weights, 0)

    damping = solve_damping * 255.0
    inv_span = 1.0 / SPAN
    VP = dates + SUB
    for u in range(vv.shape[0]):
        for half in range(2):
            vv[u, half, pl.ds(dates, SUB), :] = zero
            for m in range(SPAN):
                aw[u, half, m, pl.ds(0, SUB), :] = zero
                ag[u, half, m, pl.ds(0, SUB), :] = zero

    groups = [(t, half) for t in range(NF) for half in range(2)]

    def spread(ref, u, t, half, q):
        m_1 = vreg(msk.at[0], t * SUB)
        m_2 = vreg(msk.at[1], t * SUB)
        q0, q1, q2, q3 = q
        two = q2 + q3
        a1 = two + q1
        for m, value in enumerate(
            (a1 + q0, a1, jnp.where(m_1 > 0.5, two, a1), jnp.where(m_2 > 0.5, two, q3), q3)
        ):
            ref[u, half, m, pl.ds(SUB + t * SUB, SUB), :] = value

    def collect(ref, u, t, half):
        total = ref[u, half, 0, pl.ds(SUB + t * SUB, SUB), :]
        for m in range(1, SPAN):
            total = total + ref[u, half, m, pl.ds(SUB + t * SUB - m, SUB), :]
        return total

    def residual(u, row, t, half):
        y = [vreg(yy, al((((row * K + k) * NF + t) * 2 + half) * SUB)) for k in range(K)]
        s = [vv[u, half, pl.ds(t * SUB + m, SUB), :] for m in range(SPAN)]
        for m in range(1, SPAN):
            s[m] = s[m - 1] + s[m]
        m_1 = vreg(msk.at[0], t * SUB) > 0.5
        m_2 = vreg(msk.at[1], t * SUB) > 0.5
        model = (s[0], jnp.where(m_1, s[1], s[2]), jnp.where(m_2, s[3], s[2]), s[4])
        return [a - b for a, b in zip(y, model)]

    U = vv.shape[0]

    def invert_rows(i, c):
        rows = [(u, i * U + u) for u in range(U)]
        inverse = {}
        for p in range(PASSES):
            for step in range(STEPS):
                start = p == 0 and step == 0
                for u, row in rows:
                    for t, half in groups:
                        if start:
                            res = [
                                vreg(yy, al((((row * K + k) * NF + t) * 2 + half) * SUB)) for k in range(K)
                            ]
                        else:
                            res = residual(u, row, t, half)
                        g = []
                        w_all = []
                        for k in range(K):
                            if step == 0:
                                place = al((((row * K + k) * NF + t) * 2 + half) * SUB)
                                w = vreg(wf, place) * (1.0 / (1.0 + res[k] * res[k]))
                                wk[u, t, half, k] = w
                                w_all.append(w)
                            else:
                                w = wk[u, t, half, k]
                            g.append(w * res[k])
                        if step == 0:
                            spread(aw, u, t, half, w_all)
                        spread(ag, u, t, half, g)
                for u, row in rows:
                    for t, half in groups:
                        if step == 0:
                            inverse[u, t, half] = inv_span / (collect(aw, u, t, half) + damping)
                        grad = collect(ag, u, t, half)
                        place = pl.ds(t * SUB, SUB)
                        if start:
                            v = grad * inverse[u, t, half]
                        else:
                            old = vv[u, half, place, :]
                            v = old + (grad - damping * old) * inverse[u, t, half]
                        if p == PASSES - 1 and step == STEPS - 1:
                            vfin[row, half, place, :] = v * residual_scale
                        else:
                            vv[u, half, place, :] = v
        return c

    lax.fori_loop(0, R // U, invert_rows, 0)

    back = perm_matrix(True)
    unknowns = dates - 1

    def finish(row, c):
        value = jnp.concatenate([vfin[row, 0], vfin[row, 1]], axis=1)
        high = value.astype(BF16)
        rest = value - high.astype(F32)
        mid = rest.astype(BF16)
        low = (rest - mid.astype(F32)).astype(BF16)
        stack = jnp.concatenate([high, mid, low], axis=0)
        out = jnp.dot(stack, back, preferred_element_type=F32)
        out = out[:dates] + out[dates : 2 * dates] + out[2 * dates :]
        for half in range(2):
            obuf.at[half].reshape(dates * R, LANES)[pl.ds(row, dates, stride=R), :] = out[
                :, half * LANES : (half + 1) * LANES
            ]
        return c

    lax.fori_loop(0, R, finish, 0)
    outs = []
    for half in range(2):
        outs.append(
            pltpu.make_async_copy(
                obuf.at[half, pl.ds(0, unknowns)],
                out_hbm.at[:, :, pl.ds(half * LANES, LANES)],
                osem.at[half],
            )
        )
    for copy in outs:
        copy.start()
    for copy in outs:
        copy.wait()


def solve(own, partner, same, cross, pair_offset, pair_weight):
    tile_rows = own.shape[0]
    dates = 2 * own.shape[3]
    pairs, R, columns = pair_weight.shape
    H = HALO
    NR = R + 2 * H
    NZ = NR - 2
    NF = dates // SUB
    group = K * 2 * SUB
    vm = pl.BlockSpec(memory_space=pltpu.VMEM)
    hbm = pl.BlockSpec(memory_space=pl.ANY)
    U = 1
    v2 = lambda rows: pltpu.VMEM((rows, LANES), F32)
    scratch = [
        v2(NR * 4 * (dates + SUB)),
        v2(NR * group), v2(NR * group),
        v2(NZ * group), v2(NZ * group), v2(NZ * group),
        v2(NZ * group), v2(NZ * group),
        v2(NZ * group), v2(NZ * group),
        v2(NZ * group), v2(NZ * group), v2(NZ * group),
        v2(NZ * group), v2(NZ * group),
        v2(R * NF * group),
        pltpu.VMEM((2, pairs, R, LANES), jnp.int32),
        v2(R * NF * group),
        pltpu.VMEM((U, 2, dates + SUB, LANES), F32),
        pltpu.VMEM((U, 2, SPAN, dates + SUB, LANES), F32),
        pltpu.VMEM((U, 2, SPAN, dates + SUB, LANES), F32),
        pltpu.VMEM((U, NF, 2, K, SUB, LANES), F32),
        pltpu.VMEM((2 + K, dates, LANES), F32),
        pltpu.VMEM((R, 2, dates, LANES), F32),
        pltpu.VMEM((2, dates, R, LANES), F32),
        pltpu.SemaphoreType.DMA((2,)),
        pltpu.SemaphoreType.DMA((2,)),
    ]
    return pl.pallas_call(
        main_kernel,
        out_shape=jax.ShapeDtypeStruct((dates - 1, R, columns), F32),
        in_specs=[vm, vm, vm, vm, vm, hbm],
        out_specs=hbm,
        scratch_shapes=scratch,
        name="solve",
        compiler_params=pltpu.CompilerParams(vmem_limit_bytes=60 * 1024 * 1024),
    )(own, partner, same, cross, pair_offset, pair_weight)


def local(slc_real, slc_imag, pair_offset, pair_weight):
    tiles = lax.axis_size("tile")
    own, same, cross = pack(slc_real, slc_imag)
    axes = ("tile", "date")
    place = lambda t, d: 2 * t + d
    to_same = [(place(t, 0), place(t + 1, 0)) for t in range(tiles - 1)] + [
        (place(t + 1, 1), place(t, 1)) for t in range(tiles - 1)
    ]
    to_cross = [(place(t, 1), place(t + 1, 0)) for t in range(tiles - 1)] + [
        (place(t + 1, 0), place(t, 1)) for t in range(tiles - 1)
    ]
    same = lax.ppermute(same, axes, to_same)
    cross = lax.ppermute(cross, axes, to_cross)
    partner = lax.ppermute(own, "date", [(0, 1), (1, 0)])
    return solve(own, partner, same, cross, pair_offset, pair_weight)


def solution(mesh):
    placed = (
        P("date", ("scene", "tile"), None),
        P("date", ("scene", "tile"), None),
        P(),
        P(None, ("scene", "tile", "date"), None),
    )
    return jax.shard_map(
        local,
        mesh=mesh,
        in_specs=placed,
        out_specs=P(None, ("scene", "tile", "date"), None),
        check_vma=False,
    )
```

```python
import functools

import jax
import jax.numpy as jnp
from jax import lax
from jax.experimental import pallas as pl
from jax.experimental.pallas import tpu as pltpu
from jax.sharding import PartitionSpec as P

K = 4
SPAN = 5
SWEEPS = 8
PASSES = 3
STEPS = 2

unwrap_damping = 0.08
column_weight = 0.15
solve_damping = 0.1
residual_scale = 0.3

LANES = 128
SUB = 8
CLASSES = 4
GROUPS = 64
UA, UB, UC, CK = 2, 2, 5, 2
HALO = SWEEPS + 1
F32 = jnp.float32
BF16 = jnp.bfloat16


def al(x):
    return pl.multiple_of(x, SUB)


def vreg(ref, row):
    return ref[pl.ds(row, SUB), :]


def perm_matrix(transpose, swap=0):
    n = CLASSES * GROUPS
    a = lax.broadcasted_iota(jnp.int32, (n, n), 0)
    b = lax.broadcasted_iota(jnp.int32, (n, n), 1)
    col, place = (b, a) if transpose else (a, b)
    target = ((col % CLASSES) ^ swap) * GROUPS + col // CLASSES
    return jnp.where(place == target, 1.0, 0.0).astype(BF16)


def pack_kernel(halo, re_ref, im_ref, all_ref, same_ref, cross_ref, flat):
    dates, rows, columns = re_ref.shape
    side = lax.axis_index("date")
    perm = perm_matrix(False, side)
    CH = 4

    def permute(i, c):
        for part, ref in enumerate((re_ref, im_ref)):
            block = ref[pl.ds(i * CH, CH)].reshape(CH * rows, columns)
            out = jnp.dot(block, perm, preferred_element_type=F32)
            for half in range(2):
                flat[part, half, pl.ds(al(i * CH * rows), CH * rows), :] = out[:, half * LANES : (half + 1) * LANES]
        return c

    lax.fori_loop(0, dates // CH, permute, 0)
    RW = 4

    def turn(i, c):
        for u in range(RW):
            row = i * RW + u
            for part in range(2):
                for half in range(2):
                    tile = flat[part, half, pl.ds(row, dates, stride=rows), :]
                    all_ref[row, part, half] = tile.astype(BF16)
        return c

    lax.fori_loop(0, rows // RW, turn, 0)
    last = rows - halo

    def send(i, c):
        same_ref[i] = all_ref[last * (1 - side) + i]
        cross_ref[i] = all_ref[last * side + i]
        return c

    lax.fori_loop(0, halo, send, 0)


def pack(slc_real, slc_imag):
    dates, rows, columns = slc_real.shape
    shape = lambda count: jax.ShapeDtypeStruct((count, 2, 2, dates, LANES), BF16)
    vm = pl.BlockSpec(memory_space=pltpu.VMEM)
    return pl.pallas_call(
        functools.partial(pack_kernel, HALO),
        out_shape=(shape(rows), shape(HALO), shape(HALO)),
        in_specs=[vm, vm],
        out_specs=(vm, vm, vm),
        scratch_shapes=[pltpu.VMEM((2, 2, dates * rows, LANES), F32)],
        name="pack",
    )(slc_real, slc_imag)


def main_kernel(
    own_ref, partner_ref, same_ref, cross_ref, offset_ref, weight_hbm, out_hbm,
    img, cre, cim, zre, zim, mag, hle, hlo, dh, sh, rr, ss, aa, ya, yb, yc,
    yy, wraw, wf, vv, aw, ag, wk, msk, lmsk, vfin, obuf, wsem, osem,
):
    half_dates = own_ref.shape[3]
    dates = 2 * half_dates
    tile_rows = own_ref.shape[0]
    R = tile_rows // 2
    H = HALO
    NR = R + 2 * H
    NZ = NR - 2
    DP = half_dates + SUB
    NF = dates // SUB
    NB = NF // 2
    side = lax.axis_index("date")
    tile = lax.axis_index("tile")
    tiles = lax.axis_size("tile")

    copies = []
    for half in range(2):
        copies.append(
            pltpu.make_async_copy(
                weight_hbm.at[:, :, pl.ds(half * LANES, LANES)], wraw.at[half], wsem.at[half]
            )
        )
    for copy in copies:
        copy.start()

    offsets = offset_ref[...]
    m1 = jnp.where(offsets[:, 1:2] == 2, 1.0, 0.0).astype(F32)
    m2 = jnp.where(offsets[:, 2:3] == 4, 1.0, 0.0).astype(F32)
    msk[0] = jnp.broadcast_to(m1, (dates, LANES))
    msk[1] = jnp.broadcast_to(m2, (dates, LANES))
    first = lax.broadcasted_iota(jnp.int32, (dates, 1), 0)
    for k in range(K):
        ok = jnp.where(first + offsets[:, k : k + 1] < dates, 1.0, 0.0).astype(F32)
        msk[2 + k] = jnp.broadcast_to(ok, (dates, LANES))

    lane = lax.broadcasted_iota(jnp.int32, (SUB, LANES), 1)
    at_first = lane % GROUPS == 0
    at_last = lane % GROUPS == GROUPS - 1
    low = lane < GROUPS
    zero = jnp.zeros((SUB, LANES), F32)
    low2 = lax.broadcasted_iota(jnp.int32, (half_dates, LANES), 1) < GROUPS
    for n in range(2):
        lmsk[n] = jnp.where(low2, msk[n, :half_dates], msk[n, half_dates:])
    own2 = (lax.broadcasted_iota(jnp.int32, (half_dates, LANES), 1) // GROUPS) == side

    def swap_halves(x):
        return pltpu.roll(x, GROUPS, 1)

    third = 1.0 / 3.0

    def put(rho, o_tile_ref, o_row, p_tile_ref, p_row):
        for part in range(2):
            for pair in range(2):
                mine = o_tile_ref[o_row, part, pair].astype(F32) * third
                other = p_tile_ref[p_row, part, pair].astype(F32) * third
                for odd in range(2):
                    if odd:
                        x = swap_halves(jnp.where(own2, other, mine))
                    else:
                        x = jnp.where(own2, mine, other)
                    base = ((rho * 2 + part) * CLASSES + pair * 2 + odd) * DP
                    img[pl.ds(al(base), half_dates), :] = x
                    img[pl.ds(al(base + half_dates), SUB), :] = jnp.where(low, swap_halves(x[:SUB]), 0.0)

    base_row = (R - H) * side
    base_rho = H * (1 - side)

    def put_tile(i, c):
        put(base_rho + i, own_ref, base_row + i, partner_ref, base_row + i)
        return c

    lax.fori_loop(0, R + H, put_tile, 0)
    halo_rho = (R + H) * side

    def put_halo(i, c):
        put(halo_rho + i, same_ref, i, cross_ref, i)
        return c

    lax.fori_loop(0, H, put_halo, 0)

    def roll_right(x):
        return pltpu.roll(x, 1, 1)

    def roll_left(x):
        return pltpu.roll(x, LANES - 1, 1)

    def gix(row, k, cls):
        return al(((row * K + k) * CLASSES + cls) * SUB)

    def block(ft, carry):
        f0 = al(ft * SUB)

        def form(rho):
            sel1 = vreg(lmsk.at[0], f0) > 0.5
            sel2 = vreg(lmsk.at[1], f0) > 0.5

            def image(part, cls, shift):
                return vreg(img, ((rho * 2 + part) * CLASSES + cls) * DP + f0 + shift)

            pair = {}
            for cls in range(CLASSES):
                a_re, a_im = image(0, cls, 0), image(1, cls, 0)
                second = [(image(0, cls, o), image(1, cls, o)) for o in range(1, SPAN + 1)]
                pick = lambda mask, i, j: tuple(
                    jnp.where(mask, x, y) for x, y in zip(second[i - 1], second[j - 1])
                )
                chosen = (second[0], pick(sel1, 2, 3), pick(sel2, 4, 3), second[4])
                for k in range(K):
                    b_re, b_im = chosen[k]
                    pair[0, k, cls] = a_re * b_re + a_im * b_im
                    pair[1, k, cls] = a_im * b_re - a_re * b_im
            for part, ref in enumerate((cre, cim)):
                for k in range(K):
                    x = [pair[part, k, cls] for cls in range(CLASSES)]
                    x01, x23 = x[0] + x[1], x[2] + x[3]
                    sums = (
                        x01 + jnp.where(at_first, 0.0, roll_right(x[3])),
                        x01 + x[2],
                        x[1] + x23,
                        x23 + jnp.where(at_last, 0.0, roll_left(x[0])),
                    )
                    for cls in range(CLASSES):
                        ref[pl.ds(gix(rho, k, cls), SUB), :] = sums[cls]

        def phase_a(i, c):
            for u in range(UA):
                form(i * UA + u)
            return c

        lax.fori_loop(0, NR // UA, phase_a, 0)

        def edge(m, cross, scale):
            q = 1.0 / (m + 1.0)
            link = m * q
            if scale is not None:
                link = link * scale
            return link, link * (cross * q)

        def smooth(j):
            for k in range(K):
                re, im, mg = [], [], []
                for cls in range(CLASSES):
                    i0, i1, i2 = (gix(j + d, k, cls) for d in range(3))
                    x = vreg(cre, i0) + vreg(cre, i1) + vreg(cre, i2)
                    y = vreg(cim, i0) + vreg(cim, i1) + vreg(cim, i2)
                    sq = x * x + y * y
                    m = sq * lax.rsqrt(jnp.maximum(sq, 1e-30))
                    zre[pl.ds(i0, SUB), :] = x
                    zim[pl.ds(i0, SUB), :] = y
                    mag[pl.ds(i0, SUB), :] = m
                    re.append(x)
                    im.append(y)
                    mg.append(m)
                links, flows = [], []
                for cls in range(CLASSES):
                    if cls < CLASSES - 1:
                        n_re, n_im, m = re[cls + 1], im[cls + 1], mg[cls] * mg[cls + 1]
                    else:
                        n_re, n_im = roll_left(re[0]), roll_left(im[0])
                        m = jnp.where(at_last, 0.0, mg[cls] * roll_left(mg[0]))
                    link, flow = edge(m, im[cls] * n_re - re[cls] * n_im, column_weight)
                    hle[pl.ds(gix(j, k, cls), SUB), :] = link
                    links.append(link)
                    flows.append(flow)
                mid = links[1] + unwrap_damping
                end = links[3] + unwrap_damping
                dens = (links[0] + roll_right(end), links[0] + mid, mid + links[2], links[2] + end)
                srcs = (
                    flows[0] - roll_right(flows[3]),
                    flows[1] - flows[0],
                    flows[2] - flows[1],
                    flows[3] - flows[2],
                )
                for cls in range(CLASSES):
                    dh[pl.ds(gix(j, k, cls), SUB), :] = dens[cls]
                    sh[pl.ds(gix(j, k, cls), SUB), :] = srcs[cls]

        def phase_b(i, c):
            for u in range(UB):
                smooth(i * UB + u)
            return c

        lax.fori_loop(0, NZ // UB, phase_b, 0)

        @pl.when((tile == 0) & (side == 0))
        def _():
            for k in range(K):
                for cls in range(CLASSES):
                    mag[pl.ds(gix(H - 2, k, cls), SUB), :] = zero

        @pl.when((tile == tiles - 1) & (side == 1))
        def _():
            for k in range(K):
                for cls in range(CLASSES):
                    mag[pl.ds(gix(H - 1 + R, k, cls), SUB), :] = zero

        def vertical(j, k, cls):
            i0, i1 = gix(j, k, cls), gix(j + 1, k, cls)
            m = vreg(mag, i0) * vreg(mag, i1)
            return edge(m, vreg(zim, i0) * vreg(zre, i1) - vreg(zre, i0) * vreg(zim, i1), None)

        def stencil(j, ks, before):
            after = []
            n = 0
            for k in ks:
                root = []
                for cls in range(CLASSES):
                    i0 = gix(j, k, cls)
                    v, f = vertical(j, k, cls)
                    vm, fm, rm = before[n : n + 3]
                    n += 3
                    den = vreg(dh, i0) + vm + v
                    src = vreg(sh, i0) + f - fm
                    r = lax.rsqrt(den)
                    rr[pl.ds(i0, SUB), :] = r
                    ss[pl.ds(i0, SUB), :] = src * r
                    aa[pl.ds(i0, SUB), :] = vm * (r * rm)
                    root.append(r)
                    after += [v, f, r]
                for cls in range(CLASSES):
                    other = root[cls + 1] if cls < CLASSES - 1 else roll_left(root[0])
                    i0 = gix(j, k, cls)
                    hlo[pl.ds(i0, SUB), :] = vreg(hle, i0) * (root[cls] * other)
            return after

        def phase_c(ks):
            def body(i, c):
                for u in range(UC):
                    c = stencil(1 + i * UC + u, ks, c)
                return tuple(c)

            start = []
            for k in ks:
                for cls in range(CLASSES):
                    start += [*vertical(0, k, cls), zero]
            lax.fori_loop(0, (NZ - 2) // UC, body, tuple(start))

        for k in range(0, K, CK):
            phase_c(range(k, k + CK))

        def sweeps(k, c):
            steps = []
            buffers = [ya, yb, yc]
            held = ss
            power = SWEEPS // 2
            while power >= 1:
                source = held
                for n in range(power):
                    free = [x for x in buffers if x is not source and x is not held]
                    steps.append((source, held if n == power - 1 else None, free[0]))
                    source = free[0]
                held = source
                power //= 2
            for n, (source, added, target) in enumerate(steps):
                left = len(steps) - 1 - n
                for j in range(H - 1 - left, H - 1 + R + left):
                    y = [
                        [vreg(source, gix(j + d, k, cls)) for cls in range(CLASSES)] for d in (-1, 0, 1)
                    ]
                    h = [vreg(hlo, gix(j, k, cls)) for cls in range(CLASSES)]
                    right = [h[cls] * y[1][cls + 1] for cls in range(CLASSES - 1)] + [h[3] * roll_left(y[1][0])]
                    back = [roll_right(h[3] * y[1][3])] + [h[cls] * y[1][cls] for cls in range(CLASSES - 1)]
                    new = []
                    for cls in range(CLASSES):
                        i0 = gix(j, k, cls)
                        x = vreg(aa, i0) * y[0][cls] + vreg(aa, gix(j + 1, k, cls)) * y[2][cls]
                        if added is not None:
                            x = x + (y[1][cls] if added is source else vreg(added, i0))
                        if cls in (0, CLASSES - 1):
                            x = (x + right[cls]) + back[cls] if cls == 0 else (x + back[cls]) + right[cls]
                        else:
                            x = x + (right[cls] + back[cls])
                        new.append(x)
                    if left:
                        for cls in range(CLASSES):
                            target[pl.ds(gix(j, k, cls), SUB), :] = new[cls]
                    else:
                        row = j - (H - 1)
                        u = [
                            new[cls] * (vreg(rr, gix(j, k, cls)) * (1.0 / residual_scale))
                            for cls in range(CLASSES)
                        ]
                        for pair in range(2):
                            even, odd = u[2 * pair], u[2 * pair + 1]
                            first = jnp.where(low, even, swap_halves(odd))
                            second = jnp.where(low, swap_halves(even), odd)
                            for upper, value in enumerate((first, second)):
                                place = (((row * K + k) * NF + upper * NB + ft) * 2 + pair) * SUB
                                yy[pl.ds(al(place), SUB), :] = value
            return c

        lax.fori_loop(0, K, sweeps, 0)
        return carry

    lax.fori_loop(0, NB, block, 0)

    for copy in copies:
        copy.wait()
    perm = perm_matrix(False)

    def weights(row, c):
        rows = []
        for k in range(K):
            halves = [
                wraw.at[half].reshape(K * dates * R, LANES)[pl.ds(k * R + row, dates, stride=K * R), :]
                for half in range(2)
            ]
            rows.append(jnp.concatenate(halves, axis=1).astype(F32).astype(BF16))
        out = jnp.dot(jnp.concatenate(rows, axis=0), perm, preferred_element_type=F32)
        for k in range(K):
            for t in range(NF):
                for half in range(2):
                    place = (((row * K + k) * NF + t) * 2 + half) * SUB
                    x = out[(k * NF + t) * SUB : (k * NF + t + 1) * SUB, half * LANES : (half + 1) * LANES]
                    if (t + 1) * SUB + SPAN - 1 >= dates:
                        x = x * msk[2 + k, pl.ds(t * SUB, SUB), :]
                    wf[pl.ds(al(place), SUB), :] = x
        return c

    lax.fori_loop(0, R, weights, 0)

    damping = solve_damping * 255.0
    inv_span = 1.0 / SPAN
    VP = dates + SUB
    for u in range(vv.shape[0]):
        for half in range(2):
            vv[u, half, pl.ds(dates, SUB), :] = zero
            for m in range(SPAN):
                aw[u, half, m, pl.ds(0, SUB), :] = zero
                ag[u, half, m, pl.ds(0, SUB), :] = zero

    groups = [(t, half) for t in range(NF) for half in range(2)]

    def spread(ref, u, t, half, q):
        m_1 = vreg(msk.at[0], t * SUB)
        m_2 = vreg(msk.at[1], t * SUB)
        q0, q1, q2, q3 = q
        two = q2 + q3
        a1 = two + q1
        for m, value in enumerate(
            (a1 + q0, a1, jnp.where(m_1 > 0.5, two, a1), jnp.where(m_2 > 0.5, two, q3), q3)
        ):
            ref[u, half, m, pl.ds(SUB + t * SUB, SUB), :] = value

    def collect(ref, u, t, half):
        total = ref[u, half, 0, pl.ds(SUB + t * SUB, SUB), :]
        for m in range(1, SPAN):
            total = total + ref[u, half, m, pl.ds(SUB + t * SUB - m, SUB), :]
        return total

    def residual(u, row, t, half):
        y = [vreg(yy, al((((row * K + k) * NF + t) * 2 + half) * SUB)) for k in range(K)]
        s = [vv[u, half, pl.ds(t * SUB + m, SUB), :] for m in range(SPAN)]
        for m in range(1, SPAN):
            s[m] = s[m - 1] + s[m]
        m_1 = vreg(msk.at[0], t * SUB) > 0.5
        m_2 = vreg(msk.at[1], t * SUB) > 0.5
        model = (s[0], jnp.where(m_1, s[1], s[2]), jnp.where(m_2, s[3], s[2]), s[4])
        return [a - b for a, b in zip(y, model)]

    U = vv.shape[0]

    def invert_rows(i, c):
        rows = [(u, i * U + u) for u in range(U)]
        inverse = {}
        for p in range(PASSES):
            for step in range(STEPS):
                start = p == 0 and step == 0
                for u, row in rows:
                    for t, half in groups:
                        if start:
                            res = [
                                vreg(yy, al((((row * K + k) * NF + t) * 2 + half) * SUB)) for k in range(K)
                            ]
                        else:
                            res = residual(u, row, t, half)
                        g = []
                        w_all = []
                        for k in range(K):
                            if step == 0:
                                place = al((((row * K + k) * NF + t) * 2 + half) * SUB)
                                w = vreg(wf, place) * (1.0 / (1.0 + res[k] * res[k]))
                                wk[u, t, half, k] = w
                                w_all.append(w)
                            else:
                                w = wk[u, t, half, k]
                            g.append(w * res[k])
                        if step == 0:
                            spread(aw, u, t, half, w_all)
                        spread(ag, u, t, half, g)
                for u, row in rows:
                    for t, half in groups:
                        if step == 0:
                            inverse[u, t, half] = inv_span / (collect(aw, u, t, half) + damping)
                        grad = collect(ag, u, t, half)
                        place = pl.ds(t * SUB, SUB)
                        if start:
                            v = grad * inverse[u, t, half]
                        else:
                            old = vv[u, half, place, :]
                            v = old + (grad - damping * old) * inverse[u, t, half]
                        if p == PASSES - 1 and step == STEPS - 1:
                            vfin[row, half, place, :] = v * residual_scale
                        else:
                            vv[u, half, place, :] = v
        return c

    lax.fori_loop(0, R // U, invert_rows, 0)

    back = perm_matrix(True)
    unknowns = dates - 1

    def finish(row, c):
        value = jnp.concatenate([vfin[row, 0], vfin[row, 1]], axis=1)
        high = value.astype(BF16)
        rest = value - high.astype(F32)
        mid = rest.astype(BF16)
        low = (rest - mid.astype(F32)).astype(BF16)
        stack = jnp.concatenate([high, mid, low], axis=0)
        out = jnp.dot(stack, back, preferred_element_type=F32)
        out = out[:dates] + out[dates : 2 * dates] + out[2 * dates :]
        for half in range(2):
            obuf.at[half].reshape(dates * R, LANES)[pl.ds(row, dates, stride=R), :] = out[
                :, half * LANES : (half + 1) * LANES
            ]
        return c

    lax.fori_loop(0, R, finish, 0)
    outs = []
    for half in range(2):
        outs.append(
            pltpu.make_async_copy(
                obuf.at[half, pl.ds(0, unknowns)],
                out_hbm.at[:, :, pl.ds(half * LANES, LANES)],
                osem.at[half],
            )
        )
    for copy in outs:
        copy.start()
    for copy in outs:
        copy.wait()


def solve(own, partner, same, cross, pair_offset, pair_weight):
    tile_rows = own.shape[0]
    dates = 2 * own.shape[3]
    pairs, R, columns = pair_weight.shape
    H = HALO
    NR = R + 2 * H
    NZ = NR - 2
    NF = dates // SUB
    group = K * CLASSES * SUB
    vm = pl.BlockSpec(memory_space=pltpu.VMEM)
    hbm = pl.BlockSpec(memory_space=pl.ANY)
    U = 1
    v2 = lambda rows: pltpu.VMEM((rows, LANES), F32)
    scratch = [
        v2(NR * 2 * CLASSES * (dates // 2 + SUB)),
        v2(NR * group), v2(NR * group),
        v2(NZ * group), v2(NZ * group), v2(NZ * group),
        v2(NZ * group), v2(NZ * group),
        v2(NZ * group), v2(NZ * group),
        v2(NZ * group), v2(NZ * group), v2(NZ * group),
        v2(NZ * group), v2(NZ * group), v2(NZ * group),
        v2(R * NF * K * 2 * SUB),
        pltpu.VMEM((2, pairs, R, LANES), jnp.int32),
        v2(R * NF * K * 2 * SUB),
        pltpu.VMEM((U, 2, dates + SUB, LANES), F32),
        pltpu.VMEM((U, 2, SPAN, dates + SUB, LANES), F32),
        pltpu.VMEM((U, 2, SPAN, dates + SUB, LANES), F32),
        pltpu.VMEM((U, NF, 2, K, SUB, LANES), F32),
        pltpu.VMEM((2 + K, dates, LANES), F32),
        pltpu.VMEM((2, dates // 2, LANES), F32),
        pltpu.VMEM((R, 2, dates, LANES), F32),
        pltpu.VMEM((2, dates, R, LANES), F32),
        pltpu.SemaphoreType.DMA((2,)),
        pltpu.SemaphoreType.DMA((2,)),
    ]
    return pl.pallas_call(
        main_kernel,
        out_shape=jax.ShapeDtypeStruct((dates - 1, R, columns), F32),
        in_specs=[vm, vm, vm, vm, vm, hbm],
        out_specs=hbm,
        scratch_shapes=scratch,
        name="solve",
        compiler_params=pltpu.CompilerParams(vmem_limit_bytes=60 * 1024 * 1024),
    )(own, partner, same, cross, pair_offset, pair_weight)


def local(slc_real, slc_imag, pair_offset, pair_weight):
    tiles = lax.axis_size("tile")
    own, same, cross = pack(slc_real, slc_imag)
    axes = ("tile", "date")
    place = lambda t, d: 2 * t + d
    to_same = [(place(t, 0), place(t + 1, 0)) for t in range(tiles - 1)] + [
        (place(t + 1, 1), place(t, 1)) for t in range(tiles - 1)
    ]
    to_cross = [(place(t, 1), place(t + 1, 0)) for t in range(tiles - 1)] + [
        (place(t + 1, 0), place(t, 1)) for t in range(tiles - 1)
    ]
    same = lax.ppermute(same, axes, to_same)
    cross = lax.ppermute(cross, axes, to_cross)
    partner = lax.ppermute(own, "date", [(0, 1), (1, 0)])
    return solve(own, partner, same, cross, pair_offset, pair_weight)


def solution(mesh):
    placed = (
        P("date", ("scene", "tile"), None),
        P("date", ("scene", "tile"), None),
        P(),
        P(None, ("scene", "tile", "date"), None),
    )
    return jax.shard_map(
        local,
        mesh=mesh,
        in_specs=placed,
        out_specs=P(None, ("scene", "tile", "date"), None),
        check_vma=False,
    )
```

```python
import functools

import jax
import jax.numpy as jnp
from jax import lax
from jax.experimental import pallas as pl
from jax.experimental.pallas import tpu as pltpu
from jax.sharding import PartitionSpec as P

K = 4
SPAN = 5
SWEEPS = 8
PASSES = 3
STEPS = 2

unwrap_damping = 0.08
column_weight = 0.15
solve_damping = 0.1
residual_scale = 0.3

LANES = 128
SUB = 8
CLASSES = 4
GROUPS = 64
UI, UH, UW, UO = 5, 3, 8, 4
UA, UB, UC, CK = 2, 2, 5, 2
HALO = SWEEPS + 1
F32 = jnp.float32
BF16 = jnp.bfloat16


def al(x):
    return pl.multiple_of(x, SUB)


def vreg(ref, row):
    return ref[pl.ds(row, SUB), :]


def perm_matrix(transpose, swap=0):
    n = CLASSES * GROUPS
    a = lax.broadcasted_iota(jnp.int32, (n, n), 0)
    b = lax.broadcasted_iota(jnp.int32, (n, n), 1)
    col, place = (b, a) if transpose else (a, b)
    target = ((col % CLASSES) ^ swap) * GROUPS + col // CLASSES
    return jnp.where(place == target, 1.0, 0.0).astype(BF16)


def pack_kernel(halo, re_ref, im_ref, all_ref, same_ref, cross_ref, flat, perm_ref):
    dates, rows, columns = re_ref.shape
    side = lax.axis_index("date")
    perm_ref[...] = perm_matrix(False, side)
    CH = 4
    pitch = rows + 1

    def permute(i, c):
        for part, ref in enumerate((re_ref, im_ref)):
            block = ref[pl.ds(i * CH, CH)].reshape(CH * rows, columns)
            out = jnp.dot(block, perm_ref[...], preferred_element_type=F32)
            for n in range(CH):
                for half in range(2):
                    flat[part, half, pl.ds((i * CH + n) * pitch, rows), :] = out[
                        n * rows : (n + 1) * rows, half * LANES : (half + 1) * LANES
                    ]
        return c

    lax.fori_loop(0, dates // CH, permute, 0)
    RW = 4

    def turn(i, c):
        for u in range(RW):
            row = i * RW + u
            for part in range(2):
                for half in range(2):
                    tile = flat[part, half, pl.ds(row, dates, stride=pitch), :]
                    all_ref[row, part, half] = tile.astype(BF16)
        return c

    lax.fori_loop(0, rows // RW, turn, 0)
    last = rows - halo

    def send(i, c):
        same_ref[i] = all_ref[last * (1 - side) + i]
        cross_ref[i] = all_ref[last * side + i]
        return c

    lax.fori_loop(0, halo, send, 0)


def pack(slc_real, slc_imag):
    dates, rows, columns = slc_real.shape
    shape = lambda count: jax.ShapeDtypeStruct((count, 2, 2, dates, LANES), BF16)
    vm = pl.BlockSpec(memory_space=pltpu.VMEM)
    return pl.pallas_call(
        functools.partial(pack_kernel, HALO),
        out_shape=(shape(rows), shape(HALO), shape(HALO)),
        in_specs=[vm, vm],
        out_specs=(vm, vm, vm),
        scratch_shapes=[pltpu.VMEM((2, 2, dates * (rows + 1), LANES), F32), pltpu.VMEM((columns, columns), BF16)],
        name="pack",
    )(slc_real, slc_imag)


def main_kernel(
    own_ref, partner_ref, same_ref, cross_ref, offset_ref, weight_hbm, out_hbm,
    img, cre, cim, zre, zim, mag, hle, hlo, dh, sh, rr, ss, aa, ya, yb, yc,
    yy, wraw, wf, vv, aw, ag, wk, msk, lmsk, vfin, fbuf, obuf, perm_ref, wsem, osem,
):
    half_dates = own_ref.shape[3]
    dates = 2 * half_dates
    tile_rows = own_ref.shape[0]
    R = tile_rows // 2
    H = HALO
    NR = R + 2 * H
    NZ = NR - 2
    DP = half_dates + SUB
    NF = dates // SUB
    NB = NF // 2
    side = lax.axis_index("date")
    tile = lax.axis_index("tile")
    tiles = lax.axis_size("tile")

    copies = []
    for half in range(2):
        copies.append(
            pltpu.make_async_copy(
                weight_hbm.at[:, :, pl.ds(half * LANES, LANES)], wraw.at[half], wsem.at[half]
            )
        )
    for copy in copies:
        copy.start()

    offsets = offset_ref[...]
    m1 = jnp.where(offsets[:, 1:2] == 2, 1.0, 0.0).astype(F32)
    m2 = jnp.where(offsets[:, 2:3] == 4, 1.0, 0.0).astype(F32)
    msk[0] = jnp.broadcast_to(m1, (dates, LANES))
    msk[1] = jnp.broadcast_to(m2, (dates, LANES))
    first = lax.broadcasted_iota(jnp.int32, (dates, 1), 0)
    for k in range(K):
        ok = jnp.where(first + offsets[:, k : k + 1] < dates, 1.0, 0.0).astype(F32)
        msk[2 + k] = jnp.broadcast_to(ok, (dates, LANES))

    lane = lax.broadcasted_iota(jnp.int32, (SUB, LANES), 1)
    at_first = lane % GROUPS == 0
    at_last = lane % GROUPS == GROUPS - 1
    low = lane < GROUPS
    zero = jnp.zeros((SUB, LANES), F32)
    low2 = lax.broadcasted_iota(jnp.int32, (half_dates, LANES), 1) < GROUPS
    for n in range(2):
        lmsk[n] = jnp.where(low2, msk[n, :half_dates], msk[n, half_dates:])
    own2 = (lax.broadcasted_iota(jnp.int32, (half_dates, LANES), 1) // GROUPS) == side

    def swap_halves(x):
        return pltpu.roll(x, GROUPS, 1)

    third = 1.0 / 3.0

    def put(rho, o_tile_ref, o_row, p_tile_ref, p_row):
        for part in range(2):
            for pair in range(2):
                mine = o_tile_ref[o_row, part, pair].astype(F32) * third
                other = p_tile_ref[p_row, part, pair].astype(F32) * third
                for odd in range(2):
                    if odd:
                        x = swap_halves(jnp.where(own2, other, mine))
                    else:
                        x = jnp.where(own2, mine, other)
                    base = ((rho * 2 + part) * CLASSES + pair * 2 + odd) * DP
                    img[pl.ds(al(base), half_dates), :] = x
                    img[pl.ds(al(base + half_dates), SUB), :] = jnp.where(low, swap_halves(x[:SUB]), 0.0)

    base_row = (R - H) * side
    base_rho = H * (1 - side)

    def put_tile(i, c):
        for u in range(UI):
            n = i * UI + u
            put(base_rho + n, own_ref, base_row + n, partner_ref, base_row + n)
        return c

    lax.fori_loop(0, (R + H) // UI, put_tile, 0)
    halo_rho = (R + H) * side

    def put_halo(i, c):
        for u in range(UH):
            n = i * UH + u
            put(halo_rho + n, same_ref, n, cross_ref, n)
        return c

    lax.fori_loop(0, H // UH, put_halo, 0)

    def roll_right(x):
        return pltpu.roll(x, 1, 1)

    def roll_left(x):
        return pltpu.roll(x, LANES - 1, 1)

    def gix(row, k, cls):
        return al(((row * K + k) * CLASSES + cls) * SUB)

    def block(ft, carry):
        f0 = al(ft * SUB)

        def form(rho):
            sel1 = vreg(lmsk.at[0], f0) > 0.5
            sel2 = vreg(lmsk.at[1], f0) > 0.5

            def image(part, cls, shift):
                return vreg(img, ((rho * 2 + part) * CLASSES + cls) * DP + f0 + shift)

            pair = {}
            for cls in range(CLASSES):
                a_re, a_im = image(0, cls, 0), image(1, cls, 0)
                second = [(image(0, cls, o), image(1, cls, o)) for o in range(1, SPAN + 1)]
                pick = lambda mask, i, j: tuple(
                    jnp.where(mask, x, y) for x, y in zip(second[i - 1], second[j - 1])
                )
                chosen = (second[0], pick(sel1, 2, 3), pick(sel2, 4, 3), second[4])
                for k in range(K):
                    b_re, b_im = chosen[k]
                    pair[0, k, cls] = a_re * b_re + a_im * b_im
                    pair[1, k, cls] = a_im * b_re - a_re * b_im
            for part, ref in enumerate((cre, cim)):
                for k in range(K):
                    x = [pair[part, k, cls] for cls in range(CLASSES)]
                    x01, x23 = x[0] + x[1], x[2] + x[3]
                    sums = (
                        x01 + jnp.where(at_first, 0.0, roll_right(x[3])),
                        x01 + x[2],
                        x[1] + x23,
                        x23 + jnp.where(at_last, 0.0, roll_left(x[0])),
                    )
                    for cls in range(CLASSES):
                        ref[pl.ds(gix(rho, k, cls), SUB), :] = sums[cls]

        def phase_a(i, c):
            for u in range(UA):
                form(i * UA + u)
            return c

        lax.fori_loop(0, NR // UA, phase_a, 0)

        def edge(m, cross, scale):
            q = 1.0 / (m + 1.0)
            link = m * q
            if scale is not None:
                link = link * scale
            return link, link * (cross * q)

        def smooth(j):
            for k in range(K):
                re, im, mg = [], [], []
                for cls in range(CLASSES):
                    i0, i1, i2 = (gix(j + d, k, cls) for d in range(3))
                    x = vreg(cre, i0) + vreg(cre, i1) + vreg(cre, i2)
                    y = vreg(cim, i0) + vreg(cim, i1) + vreg(cim, i2)
                    sq = x * x + y * y
                    m = sq * lax.rsqrt(jnp.maximum(sq, 1e-30))
                    zre[pl.ds(i0, SUB), :] = x
                    zim[pl.ds(i0, SUB), :] = y
                    mag[pl.ds(i0, SUB), :] = m
                    re.append(x)
                    im.append(y)
                    mg.append(m)
                links, flows = [], []
                for cls in range(CLASSES):
                    if cls < CLASSES - 1:
                        n_re, n_im, m = re[cls + 1], im[cls + 1], mg[cls] * mg[cls + 1]
                    else:
                        n_re, n_im = roll_left(re[0]), roll_left(im[0])
                        m = jnp.where(at_last, 0.0, mg[cls] * roll_left(mg[0]))
                    link, flow = edge(m, im[cls] * n_re - re[cls] * n_im, column_weight)
                    hle[pl.ds(gix(j, k, cls), SUB), :] = link
                    links.append(link)
                    flows.append(flow)
                mid = links[1] + unwrap_damping
                end = links[3] + unwrap_damping
                dens = (links[0] + roll_right(end), links[0] + mid, mid + links[2], links[2] + end)
                srcs = (
                    flows[0] - roll_right(flows[3]),
                    flows[1] - flows[0],
                    flows[2] - flows[1],
                    flows[3] - flows[2],
                )
                for cls in range(CLASSES):
                    dh[pl.ds(gix(j, k, cls), SUB), :] = dens[cls]
                    sh[pl.ds(gix(j, k, cls), SUB), :] = srcs[cls]

        def phase_b(i, c):
            for u in range(UB):
                smooth(i * UB + u)
            return c

        lax.fori_loop(0, NZ // UB, phase_b, 0)

        @pl.when((tile == 0) & (side == 0))
        def _():
            for k in range(K):
                for cls in range(CLASSES):
                    mag[pl.ds(gix(H - 2, k, cls), SUB), :] = zero

        @pl.when((tile == tiles - 1) & (side == 1))
        def _():
            for k in range(K):
                for cls in range(CLASSES):
                    mag[pl.ds(gix(H - 1 + R, k, cls), SUB), :] = zero

        def vertical(j, k, cls):
            i0, i1 = gix(j, k, cls), gix(j + 1, k, cls)
            m = vreg(mag, i0) * vreg(mag, i1)
            return edge(m, vreg(zim, i0) * vreg(zre, i1) - vreg(zre, i0) * vreg(zim, i1), None)

        def stencil(j, ks, before):
            after = []
            n = 0
            for k in ks:
                root = []
                for cls in range(CLASSES):
                    i0 = gix(j, k, cls)
                    v, f = vertical(j, k, cls)
                    vm, fm, rm = before[n : n + 3]
                    n += 3
                    den = vreg(dh, i0) + vm + v
                    src = vreg(sh, i0) + f - fm
                    r = lax.rsqrt(den)
                    rr[pl.ds(i0, SUB), :] = r
                    ss[pl.ds(i0, SUB), :] = src * r
                    aa[pl.ds(i0, SUB), :] = vm * (r * rm)
                    root.append(r)
                    after += [v, f, r]
                for cls in range(CLASSES):
                    other = root[cls + 1] if cls < CLASSES - 1 else roll_left(root[0])
                    i0 = gix(j, k, cls)
                    hlo[pl.ds(i0, SUB), :] = vreg(hle, i0) * (root[cls] * other)
            return after

        def phase_c(ks):
            def body(i, c):
                for u in range(UC):
                    c = stencil(1 + i * UC + u, ks, c)
                return tuple(c)

            start = []
            for k in ks:
                for cls in range(CLASSES):
                    start += [*vertical(0, k, cls), zero]
            lax.fori_loop(0, (NZ - 2) // UC, body, tuple(start))

        for k in range(0, K, CK):
            phase_c(range(k, k + CK))

        def sweeps(k, c):
            steps = []
            buffers = [ya, yb, yc]
            held = ss
            power = SWEEPS // 2
            while power >= 1:
                source = held
                for n in range(power):
                    free = [x for x in buffers if x is not source and x is not held]
                    steps.append((source, held if n == power - 1 else None, free[0]))
                    source = free[0]
                held = source
                power //= 2
            for n, (source, added, target) in enumerate(steps):
                left = len(steps) - 1 - n
                classes = range(CLASSES)
                get = lambda ref, row: [vreg(ref, gix(row, k, cls)) for cls in classes]
                top = H - 1 - left
                y = [None, get(source, top - 1), get(source, top)]
                links = [None, get(aa, top)]
                for j in range(H - 1 - left, H - 1 + R + left):
                    y = [y[1], y[2], get(source, j + 1)]
                    links = [links[1], get(aa, j + 1)]
                    h = [vreg(hlo, gix(j, k, cls)) for cls in range(CLASSES)]
                    right = [h[cls] * y[1][cls + 1] for cls in range(CLASSES - 1)] + [h[3] * roll_left(y[1][0])]
                    back = [roll_right(h[3] * y[1][3])] + [h[cls] * y[1][cls] for cls in range(CLASSES - 1)]
                    new = []
                    for cls in range(CLASSES):
                        i0 = gix(j, k, cls)
                        x = links[0][cls] * y[0][cls] + links[1][cls] * y[2][cls]
                        if added is not None:
                            x = x + (y[1][cls] if added is source else vreg(added, i0))
                        if cls in (0, CLASSES - 1):
                            x = (x + right[cls]) + back[cls] if cls == 0 else (x + back[cls]) + right[cls]
                        else:
                            x = x + (right[cls] + back[cls])
                        new.append(x)
                    if left:
                        for cls in range(CLASSES):
                            target[pl.ds(gix(j, k, cls), SUB), :] = new[cls]
                    else:
                        row = j - (H - 1)
                        u = [
                            new[cls] * (vreg(rr, gix(j, k, cls)) * (1.0 / residual_scale))
                            for cls in range(CLASSES)
                        ]
                        for pair in range(2):
                            even, odd = u[2 * pair], u[2 * pair + 1]
                            first = jnp.where(low, even, swap_halves(odd))
                            second = jnp.where(low, swap_halves(even), odd)
                            for upper, value in enumerate((first, second)):
                                place = (((row * K + k) * NF + upper * NB + ft) * 2 + pair) * SUB
                                yy[pl.ds(al(place), SUB), :] = value
            return c

        lax.fori_loop(0, K, sweeps, 0)
        return carry

    lax.fori_loop(0, NB, block, 0)

    for copy in copies:
        copy.wait()
    perm_ref[...] = perm_matrix(False)
    pairs = K * dates
    WR = K * NF * 2 * SUB + 1

    def weights(i, c):
        p0 = i * UW
        rows = [
            wraw[half, pl.ds(p0, UW)].reshape(UW * R, LANES).astype(F32).astype(BF16) for half in range(2)
        ]
        out = jnp.dot(jnp.concatenate(rows, axis=1), perm_ref[...], preferred_element_type=F32)
        for n in range(UW):
            f, k = i * (UW // K) + n // K, n % K
            t, sub = f // SUB, f % SUB
            for block in range(R // SUB):
                for half in range(2):
                    x = out[n * R + block * SUB : n * R + (block + 1) * SUB, half * LANES : (half + 1) * LANES]
                    place = ((k * NF + t) * 2 + half) * SUB + sub + block * SUB * WR
                    wf[pl.ds(place, SUB, stride=WR), :] = x
        return c

    lax.fori_loop(0, pairs // UW, weights, 0)
    for row in range(R):
        for k in range(K):
            for t in range(NF):
                if (t + 1) * SUB + SPAN - 1 >= dates:
                    for half in range(2):
                        place = row * WR + ((k * NF + t) * 2 + half) * SUB
                        wf[pl.ds(place, SUB), :] = wf[pl.ds(place, SUB), :] * msk[2 + k, pl.ds(t * SUB, SUB), :]

    damping = solve_damping * 255.0
    inv_span = 1.0 / SPAN
    VP = dates + SUB
    for u in range(vv.shape[0]):
        for half in range(2):
            vv[u, half, pl.ds(dates, SUB), :] = zero
            for m in range(SPAN):
                aw[u, half, m, pl.ds(0, SUB), :] = zero
                ag[u, half, m, pl.ds(0, SUB), :] = zero

    groups = [(t, half) for t in range(NF) for half in range(2)]

    def spread(ref, u, t, half, q):
        m_1 = vreg(msk.at[0], t * SUB)
        m_2 = vreg(msk.at[1], t * SUB)
        q0, q1, q2, q3 = q
        two = q2 + q3
        a1 = two + q1
        for m, value in enumerate(
            (a1 + q0, a1, jnp.where(m_1 > 0.5, two, a1), jnp.where(m_2 > 0.5, two, q3), q3)
        ):
            ref[u, half, m, pl.ds(SUB + t * SUB, SUB), :] = value

    def collect(ref, u, t, half):
        total = ref[u, half, 0, pl.ds(SUB + t * SUB, SUB), :]
        for m in range(1, SPAN):
            total = total + ref[u, half, m, pl.ds(SUB + t * SUB - m, SUB), :]
        return total

    def residual(u, row, t, half):
        y = [vreg(yy, al((((row * K + k) * NF + t) * 2 + half) * SUB)) for k in range(K)]
        s = [vv[u, half, pl.ds(t * SUB + m, SUB), :] for m in range(SPAN)]
        for m in range(1, SPAN):
            s[m] = s[m - 1] + s[m]
        m_1 = vreg(msk.at[0], t * SUB) > 0.5
        m_2 = vreg(msk.at[1], t * SUB) > 0.5
        model = (s[0], jnp.where(m_1, s[1], s[2]), jnp.where(m_2, s[3], s[2]), s[4])
        return [a - b for a, b in zip(y, model)]

    U = vv.shape[0]

    def invert_rows(i, c):
        rows = [(u, i * U + u) for u in range(U)]
        inverse = {}
        for p in range(PASSES):
            for step in range(STEPS):
                start = p == 0 and step == 0
                for u, row in rows:
                    for t, half in groups:
                        if start:
                            res = [
                                vreg(yy, al((((row * K + k) * NF + t) * 2 + half) * SUB)) for k in range(K)
                            ]
                        else:
                            res = residual(u, row, t, half)
                        g = []
                        w_all = []
                        for k in range(K):
                            if step == 0:
                                place = row * WR + ((k * NF + t) * 2 + half) * SUB
                                w = vreg(wf, place) * (1.0 / (1.0 + res[k] * res[k]))
                                wk[u, t, half, k] = w
                                w_all.append(w)
                            else:
                                w = wk[u, t, half, k]
                            g.append(w * res[k])
                        if step == 0:
                            spread(aw, u, t, half, w_all)
                        spread(ag, u, t, half, g)
                for u, row in rows:
                    for t, half in groups:
                        if step == 0:
                            inverse[u, t, half] = inv_span / (collect(aw, u, t, half) + damping)
                        grad = collect(ag, u, t, half)
                        place = pl.ds(t * SUB, SUB)
                        if start:
                            v = grad * inverse[u, t, half]
                        else:
                            old = vv[u, half, place, :]
                            v = old + (grad - damping * old) * inverse[u, t, half]
                        if p == PASSES - 1 and step == STEPS - 1:
                            vfin[row, half, place, :] = v * residual_scale
                        else:
                            vv[u, half, place, :] = v
        return c

    lax.fori_loop(0, R // U, invert_rows, 0)

    perm_ref[...] = perm_matrix(True)
    unknowns = dates - 1
    OP = dates + 1

    def finish(i, c):
        split = [[], [], []]
        for u in range(UO):
            rest = jnp.concatenate([vfin[i * UO + u, 0], vfin[i * UO + u, 1]], axis=1)
            for part in split:
                part.append(rest.astype(BF16))
                rest = rest - part[-1].astype(F32)
        stack = jnp.concatenate(split[0] + split[1] + split[2], axis=0)
        out = jnp.dot(stack, perm_ref[...], preferred_element_type=F32)
        n = UO * dates
        out = out[:n] + (out[n : 2 * n] + out[2 * n :])
        for u in range(UO):
            for half in range(2):
                fbuf[half, pl.ds((i * UO + u) * OP, dates), :] = out[
                    u * dates : (u + 1) * dates, half * LANES : (half + 1) * LANES
                ]
        return c

    lax.fori_loop(0, R // UO, finish, 0)
    for j in range(unknowns):
        for half in range(2):
            for block in range(R // SUB):
                obuf[half, j, pl.ds(block * SUB, SUB), :] = fbuf[
                    half, pl.ds(block * SUB * OP + j, SUB, stride=OP), :
                ]
    outs = []
    for half in range(2):
        outs.append(
            pltpu.make_async_copy(
                obuf.at[half, pl.ds(0, unknowns)],
                out_hbm.at[:, :, pl.ds(half * LANES, LANES)],
                osem.at[half],
            )
        )
    for copy in outs:
        copy.start()
    for copy in outs:
        copy.wait()


def solve(own, partner, same, cross, pair_offset, pair_weight):
    tile_rows = own.shape[0]
    dates = 2 * own.shape[3]
    pairs, R, columns = pair_weight.shape
    H = HALO
    NR = R + 2 * H
    NZ = NR - 2
    NF = dates // SUB
    group = K * CLASSES * SUB
    vm = pl.BlockSpec(memory_space=pltpu.VMEM)
    hbm = pl.BlockSpec(memory_space=pl.ANY)
    U = 1
    v2 = lambda rows: pltpu.VMEM((rows, LANES), F32)
    scratch = [
        v2(NR * 2 * CLASSES * (dates // 2 + SUB)),
        v2(NR * group), v2(NR * group),
        v2(NZ * group), v2(NZ * group), v2(NZ * group),
        v2(NZ * group), v2(NZ * group),
        v2(NZ * group), v2(NZ * group),
        v2(NZ * group), v2(NZ * group), v2(NZ * group),
        v2(NZ * group), v2(NZ * group), v2(NZ * group),
        v2(R * NF * K * 2 * SUB),
        pltpu.VMEM((2, pairs, R, LANES), jnp.int32),
        v2(R * (NF * K * 2 * SUB + 1)),
        pltpu.VMEM((U, 2, dates + SUB, LANES), F32),
        pltpu.VMEM((U, 2, SPAN, dates + SUB, LANES), F32),
        pltpu.VMEM((U, 2, SPAN, dates + SUB, LANES), F32),
        pltpu.VMEM((U, NF, 2, K, SUB, LANES), F32),
        pltpu.VMEM((2 + K, dates, LANES), F32),
        pltpu.VMEM((2, dates // 2, LANES), F32),
        pltpu.VMEM((R, 2, dates, LANES), F32),
        pltpu.VMEM((2, R * (dates + 1), LANES), F32),
        pltpu.VMEM((2, dates, R, LANES), F32),
        pltpu.VMEM((columns, columns), BF16),
        pltpu.SemaphoreType.DMA((2,)),
        pltpu.SemaphoreType.DMA((2,)),
    ]
    return pl.pallas_call(
        main_kernel,
        out_shape=jax.ShapeDtypeStruct((dates - 1, R, columns), F32),
        in_specs=[vm, vm, vm, vm, vm, hbm],
        out_specs=hbm,
        scratch_shapes=scratch,
        name="solve",
        compiler_params=pltpu.CompilerParams(vmem_limit_bytes=60 * 1024 * 1024),
    )(own, partner, same, cross, pair_offset, pair_weight)


def local(slc_real, slc_imag, pair_offset, pair_weight):
    tiles = lax.axis_size("tile")
    own, same, cross = pack(slc_real, slc_imag)
    axes = ("tile", "date")
    place = lambda t, d: 2 * t + d
    to_same = [(place(t, 0), place(t + 1, 0)) for t in range(tiles - 1)] + [
        (place(t + 1, 1), place(t, 1)) for t in range(tiles - 1)
    ]
    to_cross = [(place(t, 1), place(t + 1, 0)) for t in range(tiles - 1)] + [
        (place(t + 1, 0), place(t, 1)) for t in range(tiles - 1)
    ]
    same = lax.ppermute(same, axes, to_same)
    cross = lax.ppermute(cross, axes, to_cross)
    partner = lax.ppermute(own, "date", [(0, 1), (1, 0)])
    return solve(own, partner, same, cross, pair_offset, pair_weight)


def solution(mesh):
    placed = (
        P("date", ("scene", "tile"), None),
        P("date", ("scene", "tile"), None),
        P(),
        P(None, ("scene", "tile", "date"), None),
    )
    return jax.shard_map(
        local,
        mesh=mesh,
        in_specs=placed,
        out_specs=P(None, ("scene", "tile", "date"), None),
        check_vma=False,
    )
```

```python
import functools

import jax
import jax.numpy as jnp
from jax import lax
from jax.experimental import pallas as pl
from jax.experimental.pallas import tpu as pltpu
from jax.sharding import PartitionSpec as P

K = 4
SPAN = 5
SWEEPS = 8
PASSES = 3
STEPS = 2

unwrap_damping = 0.08
column_weight = 0.15
solve_damping = 0.1
residual_scale = 0.3

LANES = 128
SUB = 8
CLASSES = 4
GROUPS = 64
UI, UH, UW, UO = 5, 3, 8, 4
UNROLL_1 = (5, 4, 7)
UNROLL_2 = (7, 4, 10)
MORE = 5
HALO = SWEEPS + 1
F32 = jnp.float32
BF16 = jnp.bfloat16


def al(x):
    return pl.multiple_of(x, SUB)


def vreg(ref, row):
    return ref[pl.ds(row, SUB), :]


def perm_matrix(transpose, swap=0):
    n = CLASSES * GROUPS
    a = lax.broadcasted_iota(jnp.int32, (n, n), 0)
    b = lax.broadcasted_iota(jnp.int32, (n, n), 1)
    col, place = (b, a) if transpose else (a, b)
    target = ((col % CLASSES) ^ swap) * GROUPS + col // CLASSES
    return jnp.where(place == target, 1.0, 0.0).astype(BF16)


def pack_kernel(
    re_hbm, im_hbm, offset_hbm, weight_hbm, all_ref, msk, lmsk, wraw,
    images, offset_ref, flat, turned, perm_ref, sems,
):
    _, dates, rows, columns = images.shape
    side = lax.axis_index("date")
    copies = [
        pltpu.make_async_copy(re_hbm, images.at[0], sems.at[0]),
        pltpu.make_async_copy(im_hbm, images.at[1], sems.at[1]),
        pltpu.make_async_copy(offset_hbm, offset_ref, sems.at[2]),
    ]
    copies += [
        pltpu.make_async_copy(weight_hbm.at[:, :, pl.ds(half * LANES, LANES)], wraw.at[half], sems.at[3 + half])
        for half in range(2)
    ]
    for copy in copies:
        copy.start()
    perm_ref[...] = perm_matrix(False, side)
    CH = 4
    pitch = rows + 1
    copies[0].wait()
    copies[1].wait()

    def permute(i, c):
        for part in range(2):
            block = images[part, pl.ds(i * CH, CH)].reshape(CH * rows, columns)
            out = jnp.dot(block, perm_ref[...], preferred_element_type=F32)
            for n in range(CH):
                for half in range(2):
                    flat[part, half, pl.ds((i * CH + n) * pitch, rows), :] = out[
                        n * rows : (n + 1) * rows, half * LANES : (half + 1) * LANES
                    ]
        return c

    lax.fori_loop(0, dates // CH, permute, 0)
    RW = 8

    def turn(i, c):
        for u in range(RW):
            row = i * RW + u
            for part in range(2):
                for half in range(2):
                    tile = flat[part, half, pl.ds(row, dates, stride=pitch), :]
                    all_ref[row, part, half] = tile.astype(BF16)
        return c

    lax.fori_loop(0, rows // RW, turn, 0)
    copies[2].wait()
    offset_masks(offset_ref, msk, lmsk, turned)
    copies[3].wait()
    copies[4].wait()


def pack(slc_real, slc_imag, offsets, pair_weight):
    dates, rows, columns = slc_real.shape
    pairs, R, _ = pair_weight.shape
    inputs = [pltpu.with_memory_space_constraint(x, pltpu.HBM) for x in (slc_real, slc_imag, offsets, pair_weight)]
    vm = pl.BlockSpec(memory_space=pltpu.VMEM)
    hbm = pl.BlockSpec(memory_space=pltpu.HBM)
    per_date, all_dates = offsets.shape
    return pl.pallas_call(
        pack_kernel,
        out_shape=(
            pltpu.VMEM((rows, 2, 2, dates, LANES), BF16),
            pltpu.VMEM((2 + per_date, all_dates, LANES), F32),
            pltpu.VMEM((2, all_dates // 2, LANES), F32),
            pltpu.VMEM((2, pairs, R, LANES), jnp.int32),
        ),
        in_specs=[hbm] * 4,
        out_specs=(vm,) * 4,
        scratch_shapes=[
            pltpu.VMEM((2, dates, rows, columns), BF16),
            pltpu.VMEM(offsets.shape, jnp.int32),
            pltpu.VMEM((2, 2, dates * (rows + 1), LANES), F32),
            pltpu.VMEM((SUB, LANES), F32),
            pltpu.VMEM((columns, columns), BF16),
            pltpu.SemaphoreType.DMA((5,)),
        ],
        name="pack",
        compiler_params=pltpu.CompilerParams(vmem_limit_bytes=12 * 1024 * 1024),
    )(*inputs)


def edge_kernel(own_ref, partner_ref, _, sent_ref):
    side = lax.axis_index("date")
    first = (own_ref.shape[0] - HALO) * side
    for i in range(HALO):
        sent_ref[0, i] = own_ref[first + i]
        sent_ref[1, i] = partner_ref[first + i]


def edges(own, partner, after):
    vm = pl.BlockSpec(memory_space=pltpu.VMEM)
    return pl.pallas_call(
        edge_kernel,
        out_shape=pltpu.VMEM((2, HALO, *own.shape[1:]), own.dtype),
        in_specs=[vm, vm, pl.BlockSpec(memory_space=pl.ANY)],
        out_specs=vm,
        name="edges",
        compiler_params=pltpu.CompilerParams(vmem_limit_bytes=4 * 1024 * 1024),
    )(own, partner, after)


def gix(row, k, cls):
    return al(((row * K + k) * CLASSES + cls) * SUB)


def roll_right(x):
    return pltpu.roll(x, 1, 1)


def roll_left(x):
    return pltpu.roll(x, LANES - 1, 1)


def swap_halves(x):
    return pltpu.roll(x, GROUPS, 1)


def run(count, unroll, step):
    def body(i, c):
        for u in range(unroll):
            step(i * unroll + u)
        return c

    whole = count // unroll
    lax.fori_loop(0, whole, body, 0)
    for n in range(whole * unroll, count):
        step(n)


def lane_masks():
    lane = lax.broadcasted_iota(jnp.int32, (SUB, LANES), 1)
    return lane < GROUPS, lane % GROUPS == 0, lane % GROUPS == GROUPS - 1


def offset_masks(offset_ref, msk, lmsk, turned):
    dates = offset_ref.shape[1]
    turned[...] = jnp.zeros(turned.shape, F32)
    turned[pl.ds(0, K), pl.ds(0, dates)] = offset_ref[...].astype(F32)
    offsets = jnp.transpose(turned[...])[:dates]
    first = lax.broadcasted_iota(jnp.int32, (dates, 1), 0).astype(F32)
    tests = [offsets[:, 1:2] == 2.0, offsets[:, 2:3] == 4.0]
    tests += [first + offsets[:, k : k + 1] < dates for k in range(K)]
    for n, test in enumerate(tests[: msk.shape[0]]):
        msk[n] = jnp.broadcast_to(jnp.where(test, 1.0, 0.0).astype(F32), (dates, LANES))
    if lmsk is not None:
        half = dates // 2
        low = lax.broadcasted_iota(jnp.int32, (half, LANES), 1) < GROUPS
        for n in range(2):
            lmsk[n] = jnp.where(low, msk[n, :half], msk[n, half:])


def place_images(img, side, row, mine_ref, mine_row, other_ref, other_row):
    half_dates = mine_ref.shape[3]
    DP = half_dates + SUB
    own = (lax.broadcasted_iota(jnp.int32, (half_dates, LANES), 1) // GROUPS) == side
    low = lane_masks()[0]
    third = 1.0 / 3.0
    for part in range(2):
        for pair in range(2):
            mine = mine_ref[mine_row, part, pair].astype(F32) * third
            other = other_ref[other_row, part, pair].astype(F32) * third
            for odd in range(2):
                if odd:
                    x = swap_halves(jnp.where(own, other, mine))
                else:
                    x = jnp.where(own, mine, other)
                base = ((row * 2 + part) * CLASSES + pair * 2 + odd) * DP
                img[pl.ds(al(base), half_dates), :] = x
                img[pl.ds(al(base + half_dates), SUB), :] = jnp.where(low, swap_halves(x[:SUB]), 0.0)


def construct(img, lmsk, count, base, outside, resume, unroll, work, outs, NZ):
    cre, cim, zre, zim, mag, hle, dh, sh = work
    rr, ss, aa, hlo = outs
    DP = lmsk.shape[1] + SUB
    NB = lmsk.shape[1] // SUB
    low, at_first, at_last = lane_masks()
    ua, ub, uc = unroll
    fix = lambda ft, row, k, cls: al((((ft * NZ + row) * K + k) * CLASSES + cls) * SUB)

    def block(ft, carry):
        f0 = al(ft * SUB)

        def form(rho):
            sel1 = vreg(lmsk.at[0], f0) > 0.5
            sel2 = vreg(lmsk.at[1], f0) > 0.5

            def image(part, cls, shift):
                return vreg(img, ((rho * 2 + part) * CLASSES + cls) * DP + f0 + shift)

            pair = {}
            for cls in range(CLASSES):
                a_re, a_im = image(0, cls, 0), image(1, cls, 0)
                second = [(image(0, cls, o), image(1, cls, o)) for o in range(1, SPAN + 1)]
                pick = lambda mask, i, j: tuple(
                    jnp.where(mask, x, y) for x, y in zip(second[i - 1], second[j - 1])
                )
                chosen = (second[0], pick(sel1, 2, 3), pick(sel2, 4, 3), second[4])
                for k in range(K):
                    b_re, b_im = chosen[k]
                    pair[0, k, cls] = a_re * b_re + a_im * b_im
                    pair[1, k, cls] = a_im * b_re - a_re * b_im
            for part, ref in enumerate((cre, cim)):
                for k in range(K):
                    x = [pair[part, k, cls] for cls in range(CLASSES)]
                    x01, x23 = x[0] + x[1], x[2] + x[3]
                    sums = (
                        x01 + jnp.where(at_first, 0.0, roll_right(x[3])),
                        x01 + x[2],
                        x[1] + x23,
                        x23 + jnp.where(at_last, 0.0, roll_left(x[0])),
                    )
                    for cls in range(CLASSES):
                        ref[pl.ds(gix(rho, k, cls), SUB), :] = sums[cls]

        run(count, ua, form)

        def edge(m, cross, scale):
            q = 1.0 / (m + 1.0)
            link = m * q
            if scale is not None:
                link = link * scale
            return link, link * (cross * q)

        def smooth(j):
            for k in range(K):
                re, im, mg = [], [], []
                for cls in range(CLASSES):
                    i0, i1, i2 = (gix(j + d, k, cls) for d in range(3))
                    x = vreg(cre, i0) + vreg(cre, i1) + vreg(cre, i2)
                    y = vreg(cim, i0) + vreg(cim, i1) + vreg(cim, i2)
                    sq = x * x + y * y
                    m = sq * lax.rsqrt(jnp.maximum(sq, 1e-30))
                    zre[pl.ds(i0, SUB), :] = x
                    zim[pl.ds(i0, SUB), :] = y
                    mag[pl.ds(i0, SUB), :] = m
                    re.append(x)
                    im.append(y)
                    mg.append(m)
                links, flows = [], []
                for cls in range(CLASSES):
                    if cls < CLASSES - 1:
                        n_re, n_im, m = re[cls + 1], im[cls + 1], mg[cls] * mg[cls + 1]
                    else:
                        n_re, n_im = roll_left(re[0]), roll_left(im[0])
                        m = jnp.where(at_last, 0.0, mg[cls] * roll_left(mg[0]))
                    link, flow = edge(m, im[cls] * n_re - re[cls] * n_im, column_weight)
                    hle[pl.ds(gix(j, k, cls), SUB), :] = link
                    links.append(link)
                    flows.append(flow)
                mid = links[1] + unwrap_damping
                end = links[3] + unwrap_damping
                dens = (links[0] + roll_right(end), links[0] + mid, mid + links[2], links[2] + end)
                srcs = (
                    flows[0] - roll_right(flows[3]),
                    flows[1] - flows[0],
                    flows[2] - flows[1],
                    flows[3] - flows[2],
                )
                for cls in range(CLASSES):
                    dh[pl.ds(gix(j, k, cls), SUB), :] = dens[cls]
                    sh[pl.ds(gix(j, k, cls), SUB), :] = srcs[cls]

        run(count - 2, ub, smooth)

        for condition, row in outside:
            @pl.when(condition)
            def _():
                for k in range(K):
                    for cls in range(CLASSES):
                        mag[pl.ds(gix(row, k, cls), SUB), :] = jnp.zeros((SUB, LANES), F32)

        def vertical(j, k, cls):
            i0, i1 = gix(j, k, cls), gix(j + 1, k, cls)
            m = vreg(mag, i0) * vreg(mag, i1)
            return edge(m, vreg(zim, i0) * vreg(zre, i1) - vreg(zre, i0) * vreg(zim, i1), None)

        def stencil(j, ks, before):
            after = []
            n = 0
            for k in ks:
                root = []
                for cls in range(CLASSES):
                    i0 = gix(j, k, cls)
                    v, f = vertical(j, k, cls)
                    vm, fm, rm = before[n : n + 3]
                    n += 3
                    den = vreg(dh, i0) + vm + v
                    src = vreg(sh, i0) + f - fm
                    r = lax.rsqrt(den)
                    place = fix(ft, base + j, k, cls)
                    rr[pl.ds(place, SUB), :] = r
                    ss[pl.ds(place, SUB), :] = src * r
                    aa[pl.ds(place, SUB), :] = vm * (r * rm)
                    root.append(r)
                    after += [v, f, r]
                for cls in range(CLASSES):
                    other = root[cls + 1] if cls < CLASSES - 1 else roll_left(root[0])
                    i0 = gix(j, k, cls)
                    hlo[pl.ds(fix(ft, base + j, k, cls), SUB), :] = vreg(hle, i0) * (root[cls] * other)
            return after

        def phase_c(k):
            start = []
            for cls in range(CLASSES):
                above = jnp.zeros((SUB, LANES), F32)
                if resume is not None:
                    above = jnp.where(resume, vreg(rr, fix(ft, base, k, cls)), above)
                start += [*vertical(0, k, cls), above]

            def body(i, c):
                for u in range(uc):
                    c = stencil(1 + i * uc + u, [k], c)
                return tuple(c)

            lax.fori_loop(0, (count - 4) // uc, body, tuple(start))

        for k in range(K):
            phase_c(k)
        return carry

    lax.fori_loop(0, NB, block, 0)


def work_scratch(count):
    group = K * CLASSES * SUB
    v2 = lambda rows: pltpu.VMEM((rows, LANES), F32)
    return [v2(count * group)] * 2 + [v2((count - 2) * group)] * 6


def weight_kernel(wraw, msk, wf, perm_ref):
    dates = msk.shape[1]
    R = wraw.shape[2]
    NF = dates // SUB
    perm_ref[...] = perm_matrix(False)
    pairs = K * dates
    WR = K * NF * 2 * SUB + 1

    def weights(i, c):
        p0 = i * UW
        rows = [
            wraw[half, pl.ds(p0, UW)].reshape(UW * R, LANES).astype(F32).astype(BF16) for half in range(2)
        ]
        out = jnp.dot(jnp.concatenate(rows, axis=1), perm_ref[...], preferred_element_type=F32)
        for n in range(UW):
            f, k = i * (UW // K) + n // K, n % K
            t, sub = f // SUB, f % SUB
            for block in range(R // SUB):
                for half in range(2):
                    x = out[n * R + block * SUB : n * R + (block + 1) * SUB, half * LANES : (half + 1) * LANES]
                    place = ((k * NF + t) * 2 + half) * SUB + sub + block * SUB * WR
                    wf[pl.ds(place, SUB, stride=WR), :] = x
        return c

    lax.fori_loop(0, pairs // UW, weights, 0)
    for row in range(R):
        for k in range(K):
            for t in range(NF):
                if (t + 1) * SUB + SPAN - 1 >= dates:
                    for half in range(2):
                        place = row * WR + ((k * NF + t) * 2 + half) * SUB
                        wf[pl.ds(place, SUB), :] = wf[pl.ds(place, SUB), :] * msk[2 + k, pl.ds(t * SUB, SUB), :]


def inner_kernel(
    own_ref, partner_ref, lmsk, rr, ss, aa, hlo,
    img, cre, cim, zre, zim, mag, hle, dh, sh,
):
    R = own_ref.shape[0] // 2
    H = HALO
    NZ = R + 2 * H - 2
    side = lax.axis_index("date")
    row0 = (R - H) * side
    run(R + H, UI, lambda i: place_images(img, side, i, own_ref, row0 + i, partner_ref, row0 + i))
    construct(
        img, lmsk, R + H, H * (1 - side), (), None, UNROLL_1,
        (cre, cim, zre, zim, mag, hle, dh, sh), (rr, ss, aa, hlo), NZ,
    )


def outer_kernel(
    own_ref, partner_ref, halo_ref, msk, lmsk, rr_in, ss_in, aa_in, hlo_in, wf,
    out_hbm, rr, ss, aa, hlo,
    img, cre, cim, zre, zim, mag, hle, dh, sh, ya, yb, yc, yy,
    vv, aw, ag, wk, vfin, fbuf, obuf, perm_ref, osem,
):
    dates = 2 * own_ref.shape[3]
    R = own_ref.shape[0] // 2
    H = HALO
    NR = R + 2 * H
    NZ = NR - 2
    NF = dates // SUB
    NB = NF // 2
    side = lax.axis_index("date")
    tile = lax.axis_index("tile")
    tiles = lax.axis_size("tile")
    zero = jnp.zeros((SUB, LANES), F32)
    low = lane_masks()[0]
    WR = K * NF * 2 * SUB + 1

    count = H + MORE
    base = (NR - count) * side
    run(H, UH, lambda i: place_images(img, side, MORE * side + i, halo_ref.at[1], i, halo_ref.at[0], i))
    row0 = (2 * R - MORE) * side
    run(
        MORE, MORE,
        lambda i: place_images(img, side, H * (1 - side) + i, own_ref, row0 + i, partner_ref, row0 + i),
    )
    outside = (
        ((tile == 0) & (side == 0), H - 2),
        ((tile == tiles - 1) & (side == 1), H - 1 + R - (NR - count)),
    )
    construct(
        img, lmsk, count, base, outside, side == 1, UNROLL_2,
        (cre, cim, zre, zim, mag, hle, dh, sh), (rr, ss, aa, hlo), NZ,
    )

    def sweep_block(ft, carry):
        def at(ref, row, k, cls):
            if any(ref is x for x in (ya, yb, yc)):
                return gix(row, k, cls)
            return al((((ft * NZ + row) * K + k) * CLASSES + cls) * SUB)

        def sweeps(k, c):
            steps = []
            buffers = [ya, yb, yc]
            held = ss
            power = SWEEPS // 2
            while power >= 1:
                source = held
                for n in range(power):
                    free = [x for x in buffers if x is not source and x is not held]
                    steps.append((source, held if n == power - 1 else None, free[0]))
                    source = free[0]
                held = source
                power //= 2
            for n, (source, added, target) in enumerate(steps):
                left = len(steps) - 1 - n
                classes = range(CLASSES)
                get = lambda ref, row: [vreg(ref, at(ref, row, k, cls)) for cls in classes]
                top = H - 1 - left
                y = [None, get(source, top - 1), get(source, top)]
                links = [None, get(aa, top)]
                for j in range(H - 1 - left, H - 1 + R + left):
                    y = [y[1], y[2], get(source, j + 1)]
                    links = [links[1], get(aa, j + 1)]
                    h = get(hlo, j)
                    right = [h[cls] * y[1][cls + 1] for cls in range(CLASSES - 1)] + [h[3] * roll_left(y[1][0])]
                    back = [roll_right(h[3] * y[1][3])] + [h[cls] * y[1][cls] for cls in range(CLASSES - 1)]
                    new = []
                    for cls in range(CLASSES):
                        x = links[0][cls] * y[0][cls] + links[1][cls] * y[2][cls]
                        if added is not None:
                            x = x + (y[1][cls] if added is source else vreg(added, at(added, j, k, cls)))
                        if cls in (0, CLASSES - 1):
                            x = (x + right[cls]) + back[cls] if cls == 0 else (x + back[cls]) + right[cls]
                        else:
                            x = x + (right[cls] + back[cls])
                        new.append(x)
                    if left:
                        for cls in range(CLASSES):
                            target[pl.ds(gix(j, k, cls), SUB), :] = new[cls]
                    else:
                        row = j - (H - 1)
                        u = [
                            new[cls] * (vreg(rr, at(rr, j, k, cls)) * (1.0 / residual_scale))
                            for cls in range(CLASSES)
                        ]
                        for pair in range(2):
                            even, odd = u[2 * pair], u[2 * pair + 1]
                            first = jnp.where(low, even, swap_halves(odd))
                            second = jnp.where(low, swap_halves(even), odd)
                            for upper, value in enumerate((first, second)):
                                place = (((row * K + k) * NF + upper * NB + ft) * 2 + pair) * SUB
                                yy[pl.ds(al(place), SUB), :] = value
            return c

        lax.fori_loop(0, K, sweeps, 0)
        return carry

    lax.fori_loop(0, NB, sweep_block, 0)

    damping = solve_damping * 255.0
    inv_span = 1.0 / SPAN
    VP = dates + SUB
    for u in range(vv.shape[0]):
        for half in range(2):
            vv[u, half, pl.ds(dates, SUB), :] = zero
            for m in range(SPAN):
                aw[u, half, m, pl.ds(0, SUB), :] = zero
                ag[u, half, m, pl.ds(0, SUB), :] = zero

    groups = [(t, half) for t in range(NF) for half in range(2)]

    def spread(ref, u, t, half, q):
        m_1 = vreg(msk.at[0], t * SUB)
        m_2 = vreg(msk.at[1], t * SUB)
        q0, q1, q2, q3 = q
        two = q2 + q3
        a1 = two + q1
        for m, value in enumerate(
            (a1 + q0, a1, jnp.where(m_1 > 0.5, two, a1), jnp.where(m_2 > 0.5, two, q3), q3)
        ):
            ref[u, half, m, pl.ds(SUB + t * SUB, SUB), :] = value

    def collect(ref, u, t, half):
        total = ref[u, half, 0, pl.ds(SUB + t * SUB, SUB), :]
        for m in range(1, SPAN):
            total = total + ref[u, half, m, pl.ds(SUB + t * SUB - m, SUB), :]
        return total

    def residual(u, row, t, half):
        y = [vreg(yy, al((((row * K + k) * NF + t) * 2 + half) * SUB)) for k in range(K)]
        s = [vv[u, half, pl.ds(t * SUB + m, SUB), :] for m in range(SPAN)]
        for m in range(1, SPAN):
            s[m] = s[m - 1] + s[m]
        m_1 = vreg(msk.at[0], t * SUB) > 0.5
        m_2 = vreg(msk.at[1], t * SUB) > 0.5
        model = (s[0], jnp.where(m_1, s[1], s[2]), jnp.where(m_2, s[3], s[2]), s[4])
        return [a - b for a, b in zip(y, model)]

    U = vv.shape[0]

    def invert_rows(i, c):
        rows = [(u, i * U + u) for u in range(U)]
        inverse = {}
        for p in range(PASSES):
            for step in range(STEPS):
                start = p == 0 and step == 0
                for u, row in rows:
                    for t, half in groups:
                        if start:
                            res = [
                                vreg(yy, al((((row * K + k) * NF + t) * 2 + half) * SUB)) for k in range(K)
                            ]
                        else:
                            res = residual(u, row, t, half)
                        g = []
                        w_all = []
                        for k in range(K):
                            if step == 0:
                                place = row * WR + ((k * NF + t) * 2 + half) * SUB
                                w = vreg(wf, place) * (1.0 / (1.0 + res[k] * res[k]))
                                wk[u, t, half, k] = w
                                w_all.append(w)
                            else:
                                w = wk[u, t, half, k]
                            g.append(w * res[k])
                        if step == 0:
                            spread(aw, u, t, half, w_all)
                        spread(ag, u, t, half, g)
                for u, row in rows:
                    for t, half in groups:
                        if step == 0:
                            inverse[u, t, half] = inv_span / (collect(aw, u, t, half) + damping)
                        grad = collect(ag, u, t, half)
                        place = pl.ds(t * SUB, SUB)
                        if start:
                            v = grad * inverse[u, t, half]
                        else:
                            old = vv[u, half, place, :]
                            v = old + (grad - damping * old) * inverse[u, t, half]
                        if p == PASSES - 1 and step == STEPS - 1:
                            vfin[row, half, place, :] = v * residual_scale
                        else:
                            vv[u, half, place, :] = v
        return c

    lax.fori_loop(0, R // U, invert_rows, 0)

    perm_ref[...] = perm_matrix(True)
    unknowns = dates - 1
    OP = dates + 1

    def finish(i, c):
        split = [[], [], []]
        for u in range(UO):
            rest = jnp.concatenate([vfin[i * UO + u, 0], vfin[i * UO + u, 1]], axis=1)
            for part in split:
                part.append(rest.astype(BF16))
                rest = rest - part[-1].astype(F32)
        stack = jnp.concatenate(split[0] + split[1] + split[2], axis=0)
        out = jnp.dot(stack, perm_ref[...], preferred_element_type=F32)
        n = UO * dates
        out = out[:n] + (out[n : 2 * n] + out[2 * n :])
        for u in range(UO):
            for half in range(2):
                fbuf[half, pl.ds((i * UO + u) * OP, dates), :] = out[
                    u * dates : (u + 1) * dates, half * LANES : (half + 1) * LANES
                ]
        return c

    lax.fori_loop(0, R // UO, finish, 0)
    for j in range(unknowns):
        for half in range(2):
            for block in range(R // SUB):
                obuf[half, j, pl.ds(block * SUB, SUB), :] = fbuf[
                    half, pl.ds(block * SUB * OP + j, SUB, stride=OP), :
                ]
    outs = []
    for half in range(2):
        outs.append(
            pltpu.make_async_copy(
                obuf.at[half, pl.ds(0, unknowns)],
                out_hbm.at[:, :, pl.ds(half * LANES, LANES)],
                osem.at[half],
            )
        )
    for copy in outs:
        copy.start()
    for copy in outs:
        copy.wait()


def weigh(wraw, msk):
    _, pairs, R, _ = wraw.shape
    vm = pl.BlockSpec(memory_space=pltpu.VMEM)
    return pl.pallas_call(
        weight_kernel,
        out_shape=pltpu.VMEM((R * (2 * pairs + 1), LANES), F32),
        in_specs=[vm, vm],
        out_specs=vm,
        scratch_shapes=[pltpu.VMEM((2 * LANES, 2 * LANES), BF16)],
        name="weigh",
        compiler_params=pltpu.CompilerParams(vmem_limit_bytes=4 * 1024 * 1024),
    )(wraw, msk)


def solve(own, partner, halo, msk, lmsk, wf):
    tile_rows = own.shape[0]
    dates = 2 * own.shape[3]
    R = tile_rows // 2
    columns = 2 * LANES
    H = HALO
    NZ = R + 2 * H - 2
    NF = dates // SUB
    group = K * CLASSES * SUB
    image = 2 * CLASSES * (dates // 2 + SUB)
    vm = pl.BlockSpec(memory_space=pltpu.VMEM)
    hbm = pl.BlockSpec(memory_space=pl.ANY)
    U = 1
    v2 = lambda rows: pltpu.VMEM((rows, LANES), F32)
    stencil = [v2(NF // 2 * NZ * group)] * 4
    inner = pl.pallas_call(
        inner_kernel,
        out_shape=tuple(stencil),
        in_specs=[vm] * 3,
        out_specs=(vm,) * 4,
        scratch_shapes=[
            v2((R + H) * image),
            *work_scratch(R + H),
        ],
        name="inner",
        compiler_params=pltpu.CompilerParams(vmem_limit_bytes=24 * 1024 * 1024),
    )
    rr, ss, aa, hlo = inner(own, partner, lmsk)
    outer = pl.pallas_call(
        outer_kernel,
        out_shape=(jax.ShapeDtypeStruct((dates - 1, R, columns), F32), *stencil),
        in_specs=[vm] * 10,
        out_specs=(hbm,) + (vm,) * 4,
        input_output_aliases={5: 1, 6: 2, 7: 3, 8: 4},
        scratch_shapes=[
            v2((H + MORE) * image),
            *work_scratch(H + MORE),
            v2(NZ * group), v2(NZ * group), v2(NZ * group),
            v2(R * NF * K * 2 * SUB),
            pltpu.VMEM((U, 2, dates + SUB, LANES), F32),
            pltpu.VMEM((U, 2, SPAN, dates + SUB, LANES), F32),
            pltpu.VMEM((U, 2, SPAN, dates + SUB, LANES), F32),
            pltpu.VMEM((U, NF, 2, K, SUB, LANES), F32),
            pltpu.VMEM((R, 2, dates, LANES), F32),
            pltpu.VMEM((2, R * (dates + 1), LANES), F32),
            pltpu.VMEM((2, dates, R, LANES), F32),
            pltpu.VMEM((columns, columns), BF16),
            pltpu.SemaphoreType.DMA((2,)),
        ],
        name="outer",
        compiler_params=pltpu.CompilerParams(vmem_limit_bytes=28 * 1024 * 1024),
    )
    return outer(own, partner, halo, msk, lmsk, rr, ss, aa, hlo, wf)[0]


def local(slc_real, slc_imag, pair_offset, pair_weight):
    tiles = lax.axis_size("tile")
    own, msk, lmsk, wraw = pack(slc_real, slc_imag, pair_offset.T, pair_weight)
    partner = lax.ppermute(own, "date", [(0, 1), (1, 0)])
    wf = weigh(wraw, msk)
    moves = [(2 * t + 1, 2 * t + 2) for t in range(tiles - 1)] + [(2 * t + 2, 2 * t + 1) for t in range(tiles - 1)]
    halo = lax.ppermute(edges(own, partner, wf), ("tile", "date"), moves)
    return solve(own, partner, halo, msk, lmsk, wf)


def solution(mesh):
    placed = (
        P("date", ("scene", "tile"), None),
        P("date", ("scene", "tile"), None),
        P(),
        P(None, ("scene", "tile", "date"), None),
    )
    return jax.shard_map(
        local,
        mesh=mesh,
        in_specs=placed,
        out_specs=P(None, ("scene", "tile", "date"), None),
        check_vma=False,
    )
```

```python
import jax
import jax.numpy as jnp
from jax import lax
from jax.experimental import pallas as pl
from jax.experimental.pallas import tpu as pltpu
from jax.sharding import PartitionSpec as P


K = 4
SPAN = 5
SWEEPS = 8
PASSES = 3
STEPS = 2

unwrap_damping = 0.08
column_weight = 0.15
solve_damping = 0.1
residual_scale = 0.3

LANES = 128
SUB = 8
CLASSES = 4
GROUPS = 64
UI, UH, UW, KS = 4, 3, 32, 1
UNROLL_1 = (25, 8, 7)
UNROLL_2 = (14, 6, 10)
MORE = 5
HALO = SWEEPS + 1
F32 = jnp.float32
BF16 = jnp.bfloat16


def al(x):
    return pl.multiple_of(x, SUB)


def vreg(ref, row):
    return ref[pl.ds(row, SUB), :]


def perm_matrix(transpose, swap=0):
    n = CLASSES * GROUPS
    a = lax.broadcasted_iota(jnp.int32, (n, n), 0)
    b = lax.broadcasted_iota(jnp.int32, (n, n), 1)
    col, place = (b, a) if transpose else (a, b)
    target = ((col % CLASSES) ^ swap) * GROUPS + col // CLASSES
    return jnp.where(place == target, 1.0, 0.0).astype(BF16)


def pack_kernel(
    re_hbm, im_hbm, offset_hbm, weight_hbm, all_ref, near_ref, rest_ref, msk, lmsk, wraw,
    images, offset_ref, flat, turned, perm_ref, sems,
):
    _, dates, rows, columns = images.shape
    side = lax.axis_index("date")
    copies = [
        pltpu.make_async_copy(re_hbm, images.at[0], sems.at[0]),
        pltpu.make_async_copy(im_hbm, images.at[1], sems.at[1]),
        pltpu.make_async_copy(offset_hbm, offset_ref, sems.at[2]),
    ]
    copies += [
        pltpu.make_async_copy(weight_hbm.at[:, :, pl.ds(half * LANES, LANES)], wraw.at[half], sems.at[3 + half])
        for half in range(2)
    ]
    for copy in copies:
        copy.start()
    perm_ref[...] = perm_matrix(False, side)
    CH = dates // 2
    pitch = rows + 1
    for part in range(2):
        copies[part].wait()
        for first in range(0, dates, CH):
            block = images[part, first : first + CH].reshape(CH * rows, columns)
            out = jnp.dot(block, perm_ref[...], preferred_element_type=F32)
            for n in range(CH):
                for half in range(2):
                    flat[part, half, pl.ds((first + n) * pitch, rows), :] = out[
                        n * rows : (n + 1) * rows, half * LANES : (half + 1) * LANES
                    ]
    RW = 8

    def turn(i, c):
        for u in range(RW):
            row = i * RW + u
            for part in range(2):
                for half in range(2):
                    tile = flat[part, half, pl.ds(row, dates, stride=pitch), :]
                    all_ref[row, part, half] = tile.astype(BF16)
        return c

    lax.fori_loop(0, rows // RW, turn, 0)
    near = near_ref.shape[0]
    rest = rest_ref.shape[0]
    for i in range(near):
        near_ref[i] = all_ref[(rows - near) * (1 - side) + i]
    for i in range(rest):
        rest_ref[i] = all_ref[near * side + (rows - near - rest) * (1 - side) + i]
    copies[2].wait()
    offset_masks(offset_ref, msk, lmsk, turned)
    copies[3].wait()
    copies[4].wait()


def pack(slc_real, slc_imag, offsets, pair_weight):
    dates, rows, columns = slc_real.shape
    pairs, R, _ = pair_weight.shape
    inputs = [pltpu.with_memory_space_constraint(x, pltpu.HBM) for x in (slc_real, slc_imag, offsets, pair_weight)]
    vm = pl.BlockSpec(memory_space=pltpu.VMEM)
    hbm = pl.BlockSpec(memory_space=pltpu.HBM)
    per_date, all_dates = offsets.shape
    return pl.pallas_call(
        pack_kernel,
        out_shape=(
            pltpu.VMEM((rows, 2, 2, dates, LANES), BF16),
            pltpu.VMEM((HALO, 2, 2, dates, LANES), BF16),
            pltpu.VMEM((rows // 2, 2, 2, dates, LANES), BF16),
            pltpu.VMEM((2 + per_date, all_dates, LANES), F32),
            pltpu.VMEM((2, all_dates // 2, LANES), F32),
            pltpu.VMEM((2, pairs, R, LANES), jnp.int32),
        ),
        in_specs=[hbm] * 4,
        out_specs=(vm,) * 6,
        scratch_shapes=[
            pltpu.VMEM((2, dates, rows, columns), BF16),
            pltpu.VMEM(offsets.shape, jnp.int32),
            pltpu.VMEM((2, 2, dates * (rows + 1), LANES), F32),
            pltpu.VMEM((SUB, LANES), F32),
            pltpu.VMEM((columns, columns), BF16),
            pltpu.SemaphoreType.DMA((5,)),
        ],
        name="pack",
        compiler_params=pltpu.CompilerParams(vmem_limit_bytes=12 * 1024 * 1024),
    )(*inputs)


def edge_kernel(own_ref, near_ref, sent_ref):
    side = lax.axis_index("date")
    first = (own_ref.shape[0] - HALO) * side
    for i in range(HALO):
        sent_ref[0, i] = own_ref[first + i]
        sent_ref[1, i] = near_ref[i]


def edges(own, near):
    vm = pl.BlockSpec(memory_space=pltpu.VMEM)
    return pl.pallas_call(
        edge_kernel,
        out_shape=pltpu.VMEM((2, HALO, *own.shape[1:]), own.dtype),
        in_specs=[vm, vm],
        out_specs=vm,
        name="edges",
        compiler_params=pltpu.CompilerParams(vmem_limit_bytes=4 * 1024 * 1024),
    )(own, near)


def gix(row, k, cls):
    return al(((row * K + k) * CLASSES + cls) * SUB)


def roll_right(x):
    return pltpu.roll(x, 1, 1)


def roll_left(x):
    return pltpu.roll(x, LANES - 1, 1)


def swap_halves(x):
    return pltpu.roll(x, GROUPS, 1)


def run(count, unroll, step):
    def body(i, c):
        for u in range(unroll):
            step(i * unroll + u)
        return c

    whole = count // unroll
    lax.fori_loop(0, whole, body, 0)
    for n in range(whole * unroll, count):
        step(n)


def lane_masks():
    lane = lax.broadcasted_iota(jnp.int32, (SUB, LANES), 1)
    return lane < GROUPS, lane % GROUPS == 0, lane % GROUPS == GROUPS - 1


def offset_masks(offset_ref, msk, lmsk, turned):
    dates = offset_ref.shape[1]
    turned[...] = jnp.zeros(turned.shape, F32)
    turned[pl.ds(0, K), pl.ds(0, dates)] = offset_ref[...].astype(F32)
    offsets = jnp.transpose(turned[...])[:dates]
    first = lax.broadcasted_iota(jnp.int32, (dates, 1), 0).astype(F32)
    tests = [offsets[:, 1:2] == 2.0, offsets[:, 2:3] == 4.0]
    tests += [first + offsets[:, k : k + 1] < dates for k in range(K)]
    for n, test in enumerate(tests[: msk.shape[0]]):
        msk[n] = jnp.broadcast_to(jnp.where(test, 1.0, 0.0).astype(F32), (dates, LANES))
    if lmsk is not None:
        half = dates // 2
        low = lax.broadcasted_iota(jnp.int32, (half, LANES), 1) < GROUPS
        for n in range(2):
            lmsk[n] = jnp.where(low, msk[n, :half], msk[n, half:])


def place_images(img, side, row, mine_ref, mine_row, other_ref, other_row):
    half_dates = mine_ref.shape[3]
    DP = half_dates + SUB
    own = (lax.broadcasted_iota(jnp.int32, (half_dates, LANES), 1) // GROUPS) == side
    low = lane_masks()[0]
    third = 1.0 / 3.0
    for part in range(2):
        for pair in range(2):
            mine = mine_ref[mine_row, part, pair].astype(F32) * third
            other = other_ref[other_row, part, pair].astype(F32) * third
            for odd in range(2):
                if odd:
                    x = swap_halves(jnp.where(own, other, mine))
                else:
                    x = jnp.where(own, mine, other)
                base = ((row * 2 + part) * CLASSES + pair * 2 + odd) * DP
                img[pl.ds(al(base), half_dates), :] = x
                img[pl.ds(al(base + half_dates), SUB), :] = jnp.where(low, swap_halves(x[:SUB]), 0.0)


def construct(img, lmsk, count, base, outside, resume, unroll, work, outs, NZ):
    cre, cim, zre, zim, mag, hle, dh, sh = work
    rr, ss, aa, hlo = outs
    DP = lmsk.shape[1] + SUB
    NB = lmsk.shape[1] // SUB
    _, at_first, at_last = lane_masks()
    ua, ub, uc = unroll
    fix = lambda ft, row, k, cls: al((((ft * NZ + row) * K + k) * CLASSES + cls) * SUB)

    def block(ft, carry):
        f0 = al(ft * SUB)

        def form(rho):
            sel1 = vreg(lmsk.at[0], f0) > 0.5
            sel2 = vreg(lmsk.at[1], f0) > 0.5

            def image(part, cls, shift):
                return vreg(img, ((rho * 2 + part) * CLASSES + cls) * DP + f0 + shift)

            pair = {}
            for cls in range(CLASSES):
                a_re, a_im = image(0, cls, 0), image(1, cls, 0)
                second = [(image(0, cls, o), image(1, cls, o)) for o in range(1, SPAN + 1)]
                pick = lambda mask, i, j: tuple(
                    jnp.where(mask, x, y) for x, y in zip(second[i - 1], second[j - 1])
                )
                chosen = (second[0], pick(sel1, 2, 3), pick(sel2, 4, 3), second[4])
                for k in range(K):
                    b_re, b_im = chosen[k]
                    pair[0, k, cls] = a_re * b_re + a_im * b_im
                    pair[1, k, cls] = a_im * b_re - a_re * b_im
            for part, ref in enumerate((cre, cim)):
                for k in range(K):
                    x = [pair[part, k, cls] for cls in range(CLASSES)]
                    x01, x23 = x[0] + x[1], x[2] + x[3]
                    sums = (
                        x01 + jnp.where(at_first, 0.0, roll_right(x[3])),
                        x01 + x[2],
                        x[1] + x23,
                        x23 + jnp.where(at_last, 0.0, roll_left(x[0])),
                    )
                    for cls in range(CLASSES):
                        ref[pl.ds(gix(rho, k, cls), SUB), :] = sums[cls]

        run(count, ua, form)

        def edge(m, cross, scale):
            q = 1.0 / (m + 1.0)
            link = m * q
            if scale is not None:
                link = link * scale
            return link, link * (cross * q)

        def smooth(j):
            for k in range(K):
                re, im, mg = [], [], []
                for cls in range(CLASSES):
                    i0, i1, i2 = (gix(j + d, k, cls) for d in range(3))
                    x = vreg(cre, i0) + vreg(cre, i1) + vreg(cre, i2)
                    y = vreg(cim, i0) + vreg(cim, i1) + vreg(cim, i2)
                    sq = x * x + y * y
                    m = sq * lax.rsqrt(jnp.maximum(sq, 1e-30))
                    zre[pl.ds(i0, SUB), :] = x
                    zim[pl.ds(i0, SUB), :] = y
                    mag[pl.ds(i0, SUB), :] = m
                    re.append(x)
                    im.append(y)
                    mg.append(m)
                links, flows = [], []
                for cls in range(CLASSES):
                    if cls < CLASSES - 1:
                        n_re, n_im, m = re[cls + 1], im[cls + 1], mg[cls] * mg[cls + 1]
                    else:
                        n_re, n_im = roll_left(re[0]), roll_left(im[0])
                        m = jnp.where(at_last, 0.0, mg[cls] * roll_left(mg[0]))
                    link, flow = edge(m, im[cls] * n_re - re[cls] * n_im, column_weight)
                    hle[pl.ds(gix(j, k, cls), SUB), :] = link
                    links.append(link)
                    flows.append(flow)
                mid = links[1] + unwrap_damping
                end = links[3] + unwrap_damping
                dens = (links[0] + roll_right(end), links[0] + mid, mid + links[2], links[2] + end)
                srcs = (
                    flows[0] - roll_right(flows[3]),
                    flows[1] - flows[0],
                    flows[2] - flows[1],
                    flows[3] - flows[2],
                )
                for cls in range(CLASSES):
                    dh[pl.ds(gix(j, k, cls), SUB), :] = dens[cls]
                    sh[pl.ds(gix(j, k, cls), SUB), :] = srcs[cls]

        run(count - 2, ub, smooth)

        for condition, row in outside:
            @pl.when(condition)
            def _():
                for k in range(K):
                    for cls in range(CLASSES):
                        mag[pl.ds(gix(row, k, cls), SUB), :] = jnp.zeros((SUB, LANES), F32)

        def vertical(j, k, cls):
            i0, i1 = gix(j, k, cls), gix(j + 1, k, cls)
            m = vreg(mag, i0) * vreg(mag, i1)
            return edge(m, vreg(zim, i0) * vreg(zre, i1) - vreg(zre, i0) * vreg(zim, i1), None)

        def stencil(j, ks, before):
            after = []
            n = 0
            for k in ks:
                root = []
                for cls in range(CLASSES):
                    i0 = gix(j, k, cls)
                    v, f = vertical(j, k, cls)
                    vm, fm, rm = before[n : n + 3]
                    n += 3
                    den = vreg(dh, i0) + vm + v
                    src = vreg(sh, i0) + f - fm
                    r = lax.rsqrt(den)
                    place = fix(ft, base + j, k, cls)
                    rr[pl.ds(place, SUB), :] = r
                    ss[pl.ds(place, SUB), :] = src * r
                    aa[pl.ds(place, SUB), :] = vm * (r * rm)
                    root.append(r)
                    after += [v, f, r]
                for cls in range(CLASSES):
                    other = root[cls + 1] if cls < CLASSES - 1 else roll_left(root[0])
                    i0 = gix(j, k, cls)
                    hlo[pl.ds(fix(ft, base + j, k, cls), SUB), :] = vreg(hle, i0) * (root[cls] * other)
            return after

        def phase_c(k):
            start = []
            for cls in range(CLASSES):
                above = jnp.zeros((SUB, LANES), F32)
                if resume is not None:
                    above = jnp.where(resume, vreg(rr, fix(ft, base, k, cls)), above)
                start += [*vertical(0, k, cls), above]

            def body(i, c):
                for u in range(uc):
                    c = stencil(1 + i * uc + u, [k], c)
                return tuple(c)

            lax.fori_loop(0, (count - 4) // uc, body, tuple(start))

        for k in range(K):
            phase_c(k)
        return carry

    lax.fori_loop(0, NB, block, 0)


def work_scratch(count):
    group = K * CLASSES * SUB
    v2 = lambda rows: pltpu.VMEM((rows, LANES), F32)
    return [v2(count * group)] * 2 + [v2((count - 2) * group)] * 6


def weight_kernel(wraw, msk, wf, perm_ref):
    dates = msk.shape[1]
    R = wraw.shape[2]
    NF = dates // SUB
    perm_ref[...] = perm_matrix(False)
    pairs = K * dates
    WR = K * NF * 2 * SUB + 1

    def weights(i, c):
        p0 = i * UW
        rows = [
            wraw[half, pl.ds(p0, UW)].reshape(UW * R, LANES).astype(F32).astype(BF16) for half in range(2)
        ]
        out = jnp.dot(jnp.concatenate(rows, axis=1), perm_ref[...], preferred_element_type=F32)
        for n in range(UW):
            f, k = i * (UW // K) + n // K, n % K
            t, sub = f // SUB, f % SUB
            for block in range(R // SUB):
                for half in range(2):
                    x = out[n * R + block * SUB : n * R + (block + 1) * SUB, half * LANES : (half + 1) * LANES]
                    place = ((k * NF + t) * 2 + half) * SUB + sub + block * SUB * WR
                    wf[pl.ds(place, SUB, stride=WR), :] = x
        return c

    lax.fori_loop(0, pairs // UW, weights, 0)
    for row in range(R):
        for k in range(K):
            for t in range(NF):
                if (t + 1) * SUB + SPAN - 1 >= dates:
                    for half in range(2):
                        place = row * WR + ((k * NF + t) * 2 + half) * SUB
                        wf[pl.ds(place, SUB), :] = wf[pl.ds(place, SUB), :] * msk[2 + k, pl.ds(t * SUB, SUB), :]


def inner_kernel(
    own_ref, near_ref, rest_ref, lmsk, rr, ss, aa, hlo,
    img, cre, cim, zre, zim, mag, hle, dh, sh,
):
    R = own_ref.shape[0] // 2
    H = HALO
    NZ = R + 2 * H - 2
    side = lax.axis_index("date")
    row0 = (R - H) * side
    far = R * side
    run(H, UH, lambda i: place_images(img, side, far + i, own_ref, row0 + far + i, near_ref, i))
    far = H * (1 - side)
    run(R, UI, lambda i: place_images(img, side, far + i, own_ref, row0 + far + i, rest_ref, i))
    construct(
        img, lmsk, R + H, H * (1 - side), (), None, UNROLL_1,
        (cre, cim, zre, zim, mag, hle, dh, sh), (rr, ss, aa, hlo), NZ,
    )


def outer_kernel(
    own_ref, near_ref, halo_ref, msk, lmsk, rr_in, ss_in, aa_in, hlo_in, wf,
    out_hbm, rr, ss, aa, hlo,
    img, cre, cim, zre, zim, mag, hle, dh, sh, ya, yb, yc, yy,
    vv, aw, ag, wk, vfin, fbuf, obuf, perm_ref, osem,
):
    dates = 2 * own_ref.shape[3]
    R = own_ref.shape[0] // 2
    H = HALO
    NR = R + 2 * H
    NZ = NR - 2
    NF = dates // SUB
    NB = NF // 2
    side = lax.axis_index("date")
    tile = lax.axis_index("tile")
    tiles = lax.axis_size("tile")
    zero = jnp.zeros((SUB, LANES), F32)
    low = lane_masks()[0]
    WR = K * NF * 2 * SUB + 1

    count = H + MORE
    base = (NR - count) * side
    run(H, UH, lambda i: place_images(img, side, MORE * side + i, halo_ref.at[1], i, halo_ref.at[0], i))
    row0 = (2 * R - MORE) * side
    run(
        MORE, MORE,
        lambda i: place_images(
            img, side, H * (1 - side) + i, own_ref, row0 + i, near_ref, (H - MORE) * side + i
        ),
    )
    outside = (
        ((tile == 0) & (side == 0), H - 2),
        ((tile == tiles - 1) & (side == 1), H - 1 + R - (NR - count)),
    )
    construct(
        img, lmsk, count, base, outside, side == 1, UNROLL_2,
        (cre, cim, zre, zim, mag, hle, dh, sh), (rr, ss, aa, hlo), NZ,
    )

    def sweep_block(ft, carry):
        def at(ref, row, k, cls):
            if any(ref is x for x in (ya, yb, yc)):
                return gix(row, k, cls)
            return al((((ft * NZ + row) * K + k) * CLASSES + cls) * SUB)

        def sweeps(i, c):
            ks = [i * KS + u for u in range(KS)]
            steps = []
            buffers = [ya, yb, yc]
            held = ss
            power = SWEEPS // 2
            while power >= 1:
                source = held
                for n in range(power):
                    free = [x for x in buffers if x is not source and x is not held]
                    steps.append((source, held if n == power - 1 else None, free[0]))
                    source = free[0]
                held = source
                power //= 2
            for n, (source, added, target) in enumerate(steps):
                left = len(steps) - 1 - n
                classes = range(CLASSES)
                get = lambda ref, row, k: [vreg(ref, at(ref, row, k, cls)) for cls in classes]
                top = H - 1 - left
                window = [
                    ([None, get(source, top - 1, k), get(source, top, k)], [None, get(aa, top, k)]) for k in ks
                ]
                for j in range(H - 1 - left, H - 1 + R + left):
                    for u, k in enumerate(ks):
                        y, links = window[u]
                        y = [y[1], y[2], get(source, j + 1, k)]
                        links = [links[1], get(aa, j + 1, k)]
                        window[u] = y, links
                        h = get(hlo, j, k)
                        right = [h[cls] * y[1][cls + 1] for cls in range(CLASSES - 1)] + [h[3] * roll_left(y[1][0])]
                        back = [roll_right(h[3] * y[1][3])] + [h[cls] * y[1][cls] for cls in range(CLASSES - 1)]
                        new = []
                        for cls in range(CLASSES):
                            x = links[0][cls] * y[0][cls] + links[1][cls] * y[2][cls]
                            if added is not None:
                                x = x + (y[1][cls] if added is source else vreg(added, at(added, j, k, cls)))
                            if cls in (0, CLASSES - 1):
                                x = (x + right[cls]) + back[cls] if cls == 0 else (x + back[cls]) + right[cls]
                            else:
                                x = x + (right[cls] + back[cls])
                            new.append(x)
                        if left:
                            for cls in range(CLASSES):
                                target[pl.ds(gix(j, k, cls), SUB), :] = new[cls]
                        else:
                            row = j - (H - 1)
                            scaled = [
                                new[cls] * (vreg(rr, at(rr, j, k, cls)) * (1.0 / residual_scale))
                                for cls in range(CLASSES)
                            ]
                            for pair in range(2):
                                even, odd = scaled[2 * pair], scaled[2 * pair + 1]
                                first = jnp.where(low, even, swap_halves(odd))
                                second = jnp.where(low, swap_halves(even), odd)
                                for upper, value in enumerate((first, second)):
                                    place = (((row * K + k) * NF + upper * NB + ft) * 2 + pair) * SUB
                                    yy[pl.ds(al(place), SUB), :] = value
            return c

        lax.fori_loop(0, K // KS, sweeps, 0)
        return carry

    lax.fori_loop(0, NB, sweep_block, 0)

    damping = solve_damping * 255.0
    inv_span = 1.0 / SPAN
    for u in range(vv.shape[0]):
        for half in range(2):
            vv[u, half, pl.ds(dates, SUB), :] = zero
            for m in range(SPAN):
                aw[u, half, m, pl.ds(0, SUB), :] = zero
                ag[u, half, m, pl.ds(0, SUB), :] = zero

    groups = [(t, half) for t in range(NF) for half in range(2)]

    def spread(ref, u, t, half, q):
        m_1 = vreg(msk.at[0], t * SUB)
        m_2 = vreg(msk.at[1], t * SUB)
        q0, q1, q2, q3 = q
        two = q2 + q3
        a1 = two + q1
        for m, value in enumerate(
            (a1 + q0, a1, jnp.where(m_1 > 0.5, two, a1), jnp.where(m_2 > 0.5, two, q3), q3)
        ):
            ref[u, half, m, pl.ds(SUB + t * SUB, SUB), :] = value

    def collect(ref, u, t, half):
        total = ref[u, half, 0, pl.ds(SUB + t * SUB, SUB), :]
        for m in range(1, SPAN):
            total = total + ref[u, half, m, pl.ds(SUB + t * SUB - m, SUB), :]
        return total

    def residual(u, row, t, half):
        y = [vreg(yy, al((((row * K + k) * NF + t) * 2 + half) * SUB)) for k in range(K)]
        s = [vv[u, half, pl.ds(t * SUB + m, SUB), :] for m in range(SPAN)]
        for m in range(1, SPAN):
            s[m] = s[m - 1] + s[m]
        m_1 = vreg(msk.at[0], t * SUB) > 0.5
        m_2 = vreg(msk.at[1], t * SUB) > 0.5
        model = (s[0], jnp.where(m_1, s[1], s[2]), jnp.where(m_2, s[3], s[2]), s[4])
        return [a - b for a, b in zip(y, model)]

    U = vv.shape[0]

    def invert_rows(i, c):
        rows = [(u, i * U + u) for u in range(U)]
        inverse = {}
        for p in range(PASSES):
            for step in range(STEPS):
                start = p == 0 and step == 0
                for u, row in rows:
                    for t, half in groups:
                        if start:
                            res = [
                                vreg(yy, al((((row * K + k) * NF + t) * 2 + half) * SUB)) for k in range(K)
                            ]
                        else:
                            res = residual(u, row, t, half)
                        g = []
                        w_all = []
                        for k in range(K):
                            if step == 0:
                                place = row * WR + ((k * NF + t) * 2 + half) * SUB
                                w = vreg(wf, place) * (1.0 / (1.0 + res[k] * res[k]))
                                wk[u, t, half, k] = w
                                w_all.append(w)
                            else:
                                w = wk[u, t, half, k]
                            g.append(w * res[k])
                        if step == 0:
                            spread(aw, u, t, half, w_all)
                        spread(ag, u, t, half, g)
                for u, row in rows:
                    for t, half in groups:
                        if step == 0:
                            inverse[u, t, half] = inv_span / (collect(aw, u, t, half) + damping)
                        grad = collect(ag, u, t, half)
                        place = pl.ds(t * SUB, SUB)
                        if start:
                            v = grad * inverse[u, t, half]
                        else:
                            old = vv[u, half, place, :]
                            v = old + (grad - damping * old) * inverse[u, t, half]
                        if p == PASSES - 1 and step == STEPS - 1:
                            vfin[row, half, place, :] = v * residual_scale
                        else:
                            vv[u, half, place, :] = v
        return c

    perm_ref[...] = perm_matrix(True)
    unknowns = dates - 1
    OP = dates + 1

    def finish(first):
        split = [[], [], []]
        for u in range(SUB):
            rest = jnp.concatenate([vfin[first + u, 0], vfin[first + u, 1]], axis=1)
            for part in split:
                part.append(rest.astype(BF16))
                rest = rest - part[-1].astype(F32)
        out = None
        for part in split:
            x = jnp.dot(jnp.concatenate(part, axis=0), perm_ref[...], preferred_element_type=F32)
            out = x if out is None else out + x
        for u in range(SUB):
            for half in range(2):
                fbuf[half, pl.ds(u * OP, dates), :] = out[
                    u * dates : (u + 1) * dates, half * LANES : (half + 1) * LANES
                ]
        for j in range(unknowns):
            for half in range(2):
                obuf[half, j, pl.ds(first, SUB), :] = fbuf[half, pl.ds(j, SUB, stride=OP), :]

    outs = []
    for first in range(0, R, SUB):
        lax.fori_loop(first // U, (first + SUB) // U, invert_rows, 0)
        finish(first)
        for half in range(2):
            copy = pltpu.make_async_copy(
                obuf.at[half, pl.ds(0, unknowns), pl.ds(first, SUB)],
                out_hbm.at[:, pl.ds(first, SUB), pl.ds(half * LANES, LANES)],
                osem.at[first // SUB, half],
            )
            copy.start()
            outs.append(copy)
    for copy in outs:
        copy.wait()


def weigh(wraw, msk):
    _, pairs, R, _ = wraw.shape
    vm = pl.BlockSpec(memory_space=pltpu.VMEM)
    return pl.pallas_call(
        weight_kernel,
        out_shape=pltpu.VMEM((R * (2 * pairs + 1), LANES), F32),
        in_specs=[vm, vm],
        out_specs=vm,
        scratch_shapes=[pltpu.VMEM((2 * LANES, 2 * LANES), BF16)],
        name="weigh",
        compiler_params=pltpu.CompilerParams(vmem_limit_bytes=4 * 1024 * 1024),
    )(wraw, msk)


def solve(own, near, rest, halo, msk, lmsk, wf):
    tile_rows = own.shape[0]
    dates = 2 * own.shape[3]
    R = tile_rows // 2
    columns = 2 * LANES
    H = HALO
    NZ = R + 2 * H - 2
    NF = dates // SUB
    group = K * CLASSES * SUB
    image = 2 * CLASSES * (dates // 2 + SUB)
    vm = pl.BlockSpec(memory_space=pltpu.VMEM)
    hbm = pl.BlockSpec(memory_space=pl.ANY)
    U = 1
    v2 = lambda rows: pltpu.VMEM((rows, LANES), F32)
    stencil = [v2(NF // 2 * NZ * group)] * 4
    inner = pl.pallas_call(
        inner_kernel,
        out_shape=tuple(stencil),
        in_specs=[vm] * 4,
        out_specs=(vm,) * 4,
        scratch_shapes=[
            v2((R + H) * image),
            *work_scratch(R + H),
        ],
        name="inner",
        compiler_params=pltpu.CompilerParams(vmem_limit_bytes=24 * 1024 * 1024),
    )
    rr, ss, aa, hlo = inner(own, near, rest, lmsk)
    outer = pl.pallas_call(
        outer_kernel,
        out_shape=(jax.ShapeDtypeStruct((dates - 1, R, columns), F32), *stencil),
        in_specs=[vm] * 10,
        out_specs=(hbm,) + (vm,) * 4,
        input_output_aliases={5: 1, 6: 2, 7: 3, 8: 4},
        scratch_shapes=[
            v2((H + MORE) * image),
            *work_scratch(H + MORE),
            v2(NZ * group), v2(NZ * group), v2(NZ * group),
            v2(R * NF * K * 2 * SUB),
            pltpu.VMEM((U, 2, dates + SUB, LANES), F32),
            pltpu.VMEM((U, 2, SPAN, dates + SUB, LANES), F32),
            pltpu.VMEM((U, 2, SPAN, dates + SUB, LANES), F32),
            pltpu.VMEM((U, NF, 2, K, SUB, LANES), F32),
            pltpu.VMEM((R, 2, dates, LANES), F32),
            pltpu.VMEM((2, SUB * (dates + 1), LANES), F32),
            pltpu.VMEM((2, dates, R, LANES), F32),
            pltpu.VMEM((columns, columns), BF16),
            pltpu.SemaphoreType.DMA((R // SUB, 2)),
        ],
        name="outer",
        compiler_params=pltpu.CompilerParams(vmem_limit_bytes=28 * 1024 * 1024),
    )
    return outer(own, near, halo, msk, lmsk, rr, ss, aa, hlo, wf)[0]


def local(slc_real, slc_imag, pair_offset, pair_weight):
    tiles = lax.axis_size("tile")
    swap = [(0, 1), (1, 0)]
    moves = [(2 * t + 1, 2 * t + 2) for t in range(tiles - 1)] + [(2 * t + 2, 2 * t + 1) for t in range(tiles - 1)]
    own, near, rest, msk, lmsk, wraw = pack(slc_real, slc_imag, pair_offset.T, pair_weight)
    near = lax.ppermute(near, "date", swap)
    rest = lax.ppermute(rest, "date", swap)
    sent = edges(own, near)
    halo = lax.ppermute(sent, ("tile", "date"), moves)
    wf = weigh(wraw, msk)
    return solve(own, near, rest, halo, msk, lmsk, wf)


def solution(mesh):
    placed = (
        P("date", ("scene", "tile"), None),
        P("date", ("scene", "tile"), None),
        P(),
        P(None, ("scene", "tile", "date"), None),
    )
    return jax.shard_map(
        local,
        mesh=mesh,
        in_specs=placed,
        out_specs=P(None, ("scene", "tile", "date"), None),
        check_vma=False,
    )
```

```python
import jax
import jax.numpy as jnp
from jax import lax
from jax.experimental import pallas as pl
from jax.experimental.pallas import tpu as pltpu
from jax.sharding import PartitionSpec as P


K = 4
SPAN = 5
SWEEPS = 8
PASSES = 3
STEPS = 2

unwrap_damping = 0.08
column_weight = 0.15
solve_damping = 0.1
residual_scale = 0.3

LANES = 128
SUB = 8
CLASSES = 4
GROUPS = 64
UI, UH, UW, KS = 4, 3, 32, 1
UNROLL_1 = (25, 4, 7)
UNROLL_2 = (14, 3, 10)
MORE = 5
HALO = SWEEPS + 1
F32 = jnp.float32
BF16 = jnp.bfloat16


def al(x):
    return pl.multiple_of(x, SUB)


def vreg(ref, row):
    return ref[pl.ds(row, SUB), :]


def perm_matrix(transpose, swap=0):
    n = CLASSES * GROUPS
    a = lax.broadcasted_iota(jnp.int32, (n, n), 0)
    b = lax.broadcasted_iota(jnp.int32, (n, n), 1)
    col, place = (b, a) if transpose else (a, b)
    target = ((col % CLASSES) ^ swap) * GROUPS + col // CLASSES
    return jnp.where(place == target, 1.0, 0.0).astype(BF16)


def pack_kernel(
    re_hbm, im_hbm, offset_hbm, weight_hbm, all_ref, near_ref, rest_ref, msk, lmsk, wraw,
    images, offset_ref, flat, turned, perm_ref, sems,
):
    _, dates, rows, columns = images.shape
    side = lax.axis_index("date")
    copies = [
        pltpu.make_async_copy(re_hbm, images.at[0], sems.at[0]),
        pltpu.make_async_copy(im_hbm, images.at[1], sems.at[1]),
        pltpu.make_async_copy(offset_hbm, offset_ref, sems.at[2]),
    ]
    copies += [
        pltpu.make_async_copy(weight_hbm.at[:, :, pl.ds(half * LANES, LANES)], wraw.at[half], sems.at[3 + half])
        for half in range(2)
    ]
    for copy in copies:
        copy.start()
    perm_ref[...] = perm_matrix(False, side)
    CH = dates // 2
    pitch = rows + 1
    for part in range(2):
        copies[part].wait()
        for first in range(0, dates, CH):
            block = images[part, first : first + CH].reshape(CH * rows, columns)
            out = jnp.dot(block, perm_ref[...], preferred_element_type=F32)
            for n in range(CH):
                for half in range(2):
                    flat[part, half, pl.ds((first + n) * pitch, rows), :] = out[
                        n * rows : (n + 1) * rows, half * LANES : (half + 1) * LANES
                    ]
    RW = 8

    def turn(i, c):
        for u in range(RW):
            row = i * RW + u
            for part in range(2):
                for half in range(2):
                    tile = flat[part, half, pl.ds(row, dates, stride=pitch), :]
                    all_ref[row, part, half] = tile.astype(BF16)
        return c

    lax.fori_loop(0, rows // RW, turn, 0)
    near = near_ref.shape[0]
    rest = rest_ref.shape[0]
    for i in range(near):
        near_ref[i] = all_ref[(rows - near) * (1 - side) + i]
    for i in range(rest):
        rest_ref[i] = all_ref[near * side + (rows - near - rest) * (1 - side) + i]
    copies[2].wait()
    offset_masks(offset_ref, msk, lmsk, turned)
    copies[3].wait()
    copies[4].wait()


def pack(slc_real, slc_imag, offsets, pair_weight):
    dates, rows, columns = slc_real.shape
    pairs, R, _ = pair_weight.shape
    inputs = [pltpu.with_memory_space_constraint(x, pltpu.HBM) for x in (slc_real, slc_imag, offsets, pair_weight)]
    vm = pl.BlockSpec(memory_space=pltpu.VMEM)
    hbm = pl.BlockSpec(memory_space=pltpu.HBM)
    per_date, all_dates = offsets.shape
    return pl.pallas_call(
        pack_kernel,
        out_shape=(
            pltpu.VMEM((rows, 2, 2, dates, LANES), BF16),
            pltpu.VMEM((HALO, 2, 2, dates, LANES), BF16),
            pltpu.VMEM((rows // 2, 2, 2, dates, LANES), BF16),
            pltpu.VMEM((2 + per_date, all_dates, LANES), F32),
            pltpu.VMEM((2, all_dates // 2, LANES), F32),
            pltpu.VMEM((2, pairs, R, LANES), jnp.int32),
        ),
        in_specs=[hbm] * 4,
        out_specs=(vm,) * 6,
        scratch_shapes=[
            pltpu.VMEM((2, dates, rows, columns), BF16),
            pltpu.VMEM(offsets.shape, jnp.int32),
            pltpu.VMEM((2, 2, dates * (rows + 1), LANES), F32),
            pltpu.VMEM((SUB, LANES), F32),
            pltpu.VMEM((columns, columns), BF16),
            pltpu.SemaphoreType.DMA((5,)),
        ],
        name="pack",
        compiler_params=pltpu.CompilerParams(vmem_limit_bytes=12 * 1024 * 1024),
    )(*inputs)


def edge_kernel(own_ref, near_ref, sent_ref):
    side = lax.axis_index("date")
    first = (own_ref.shape[0] - HALO) * side
    for i in range(HALO):
        sent_ref[0, i] = own_ref[first + i]
        sent_ref[1, i] = near_ref[i]


def edges(own, near):
    vm = pl.BlockSpec(memory_space=pltpu.VMEM)
    return pl.pallas_call(
        edge_kernel,
        out_shape=pltpu.VMEM((2, HALO, *own.shape[1:]), own.dtype),
        in_specs=[vm, vm],
        out_specs=vm,
        name="edges",
        compiler_params=pltpu.CompilerParams(vmem_limit_bytes=4 * 1024 * 1024),
    )(own, near)


def gix(row, k, cls):
    return al(((row * K + k) * CLASSES + cls) * SUB)


def roll_right(x):
    return pltpu.roll(x, 1, 1)


def roll_left(x):
    return pltpu.roll(x, LANES - 1, 1)


def swap_halves(x):
    return pltpu.roll(x, GROUPS, 1)


def run(count, unroll, step):
    def body(i, c):
        for u in range(unroll):
            step(i * unroll + u)
        return c

    whole = count // unroll
    lax.fori_loop(0, whole, body, 0)
    for n in range(whole * unroll, count):
        step(n)


def lane_masks():
    lane = lax.broadcasted_iota(jnp.int32, (SUB, LANES), 1)
    return lane < GROUPS, lane % GROUPS == 0, lane % GROUPS == GROUPS - 1


def offset_masks(offset_ref, msk, lmsk, turned):
    dates = offset_ref.shape[1]
    turned[...] = jnp.zeros(turned.shape, F32)
    turned[pl.ds(0, K), pl.ds(0, dates)] = offset_ref[...].astype(F32)
    offsets = jnp.transpose(turned[...])[:dates]
    first = lax.broadcasted_iota(jnp.int32, (dates, 1), 0).astype(F32)
    tests = [offsets[:, 1:2] == 2.0, offsets[:, 2:3] == 4.0]
    tests += [first + offsets[:, k : k + 1] < dates for k in range(K)]
    for n, test in enumerate(tests[: msk.shape[0]]):
        msk[n] = jnp.broadcast_to(jnp.where(test, 1.0, 0.0).astype(F32), (dates, LANES))
    if lmsk is not None:
        half = dates // 2
        low = lax.broadcasted_iota(jnp.int32, (half, LANES), 1) < GROUPS
        for n in range(2):
            lmsk[n] = jnp.where(low, msk[n, :half], msk[n, half:])


def place_images(img, side, row, mine_ref, mine_row, other_ref, other_row):
    half_dates = mine_ref.shape[3]
    DP = half_dates + SUB
    own = (lax.broadcasted_iota(jnp.int32, (half_dates, LANES), 1) // GROUPS) == side
    low = lane_masks()[0]
    third = 1.0 / 3.0
    for part in range(2):
        for pair in range(2):
            mine = mine_ref[mine_row, part, pair].astype(F32) * third
            other = other_ref[other_row, part, pair].astype(F32) * third
            for odd in range(2):
                if odd:
                    x = swap_halves(jnp.where(own, other, mine))
                else:
                    x = jnp.where(own, mine, other)
                base = ((row * 2 + part) * CLASSES + pair * 2 + odd) * DP
                img[pl.ds(al(base), half_dates), :] = x
                img[pl.ds(al(base + half_dates), SUB), :] = jnp.where(low, swap_halves(x[:SUB]), 0.0)


def construct(img, lmsk, count, base, outside, resume, unroll, work, outs, NZ):
    cre, cim, zre, zim, mag, hle, dh, sh = work
    rr, ss, aa, hlo = outs
    DP = lmsk.shape[1] + SUB
    NB = lmsk.shape[1] // SUB
    _, at_first, at_last = lane_masks()
    ua, ub, uc = unroll
    fix = lambda ft, row, k, cls: al((((ft * NZ + row) * K + k) * CLASSES + cls) * SUB)

    def block(ft, carry):
        f0 = al(ft * SUB)

        def form(rho):
            sel1 = vreg(lmsk.at[0], f0) > 0.5
            sel2 = vreg(lmsk.at[1], f0) > 0.5

            def image(part, cls, shift):
                return vreg(img, ((rho * 2 + part) * CLASSES + cls) * DP + f0 + shift)

            pair = {}
            for cls in range(CLASSES):
                a_re, a_im = image(0, cls, 0), image(1, cls, 0)
                second = [(image(0, cls, o), image(1, cls, o)) for o in range(1, SPAN + 1)]
                pick = lambda mask, i, j: tuple(
                    jnp.where(mask, x, y) for x, y in zip(second[i - 1], second[j - 1])
                )
                chosen = (second[0], pick(sel1, 2, 3), pick(sel2, 4, 3), second[4])
                for k in range(K):
                    b_re, b_im = chosen[k]
                    pair[0, k, cls] = a_re * b_re + a_im * b_im
                    pair[1, k, cls] = a_im * b_re - a_re * b_im
            for part, ref in enumerate((cre, cim)):
                for k in range(K):
                    x = [pair[part, k, cls] for cls in range(CLASSES)]
                    x01, x23 = x[0] + x[1], x[2] + x[3]
                    sums = (
                        x01 + jnp.where(at_first, 0.0, roll_right(x[3])),
                        x01 + x[2],
                        x[1] + x23,
                        x23 + jnp.where(at_last, 0.0, roll_left(x[0])),
                    )
                    for cls in range(CLASSES):
                        ref[pl.ds(gix(rho, k, cls), SUB), :] = sums[cls]

        run(count, ua, form)

        def edge(m, cross, scale):
            q = 1.0 / (m + 1.0)
            link = m * q
            if scale is not None:
                link = link * scale
            return link, link * (cross * q)

        def smooth(j, rows):
            for k in range(K):
                sums = [{}, {}]
                for part, ref in enumerate((cre, cim)):
                    for cls in range(CLASSES):
                        c = [vreg(ref, gix(j + d, k, cls)) for d in range(rows + 2)]
                        middle = c[1] + c[2]
                        sums[part][0, cls] = c[0] + middle
                        if rows == 2:
                            sums[part][1, cls] = middle + c[3]
                for d in range(rows):
                    smooth_row(j + d, k, [[sums[part][d, cls] for cls in range(CLASSES)] for part in range(2)])

        def smooth_row(j, k, sums):
            re, im = sums
            mg = []
            for cls in range(CLASSES):
                i0 = gix(j, k, cls)
                sq = re[cls] * re[cls] + im[cls] * im[cls]
                mg.append(sq * lax.rsqrt(jnp.maximum(sq, 1e-30)))
                zre[pl.ds(i0, SUB), :] = re[cls]
                zim[pl.ds(i0, SUB), :] = im[cls]
                mag[pl.ds(i0, SUB), :] = mg[cls]
            links, flows = [], []
            for cls in range(CLASSES):
                if cls < CLASSES - 1:
                    n_re, n_im, m = re[cls + 1], im[cls + 1], mg[cls] * mg[cls + 1]
                else:
                    n_re, n_im = roll_left(re[0]), roll_left(im[0])
                    m = jnp.where(at_last, 0.0, mg[cls] * roll_left(mg[0]))
                link, flow = edge(m, im[cls] * n_re - re[cls] * n_im, column_weight)
                hle[pl.ds(gix(j, k, cls), SUB), :] = link
                links.append(link)
                flows.append(flow)
            mid = links[1] + unwrap_damping
            end = links[3] + unwrap_damping
            dens = (links[0] + roll_right(end), links[0] + mid, mid + links[2], links[2] + end)
            srcs = (
                flows[0] - roll_right(flows[3]),
                flows[1] - flows[0],
                flows[2] - flows[1],
                flows[3] - flows[2],
            )
            for cls in range(CLASSES):
                dh[pl.ds(gix(j, k, cls), SUB), :] = dens[cls]
                sh[pl.ds(gix(j, k, cls), SUB), :] = srcs[cls]

        run((count - 2) // 2, ub, lambda i: smooth(2 * i, 2))
        if count % 2:
            smooth(count - 3, 1)

        for condition, row in outside:
            @pl.when(condition)
            def _():
                for k in range(K):
                    for cls in range(CLASSES):
                        mag[pl.ds(gix(row, k, cls), SUB), :] = jnp.zeros((SUB, LANES), F32)

        def vertical(j, k, cls):
            i0, i1 = gix(j, k, cls), gix(j + 1, k, cls)
            m = vreg(mag, i0) * vreg(mag, i1)
            return edge(m, vreg(zim, i0) * vreg(zre, i1) - vreg(zre, i0) * vreg(zim, i1), None)

        def stencil(j, ks, before):
            after = []
            n = 0
            for k in ks:
                root = []
                for cls in range(CLASSES):
                    i0 = gix(j, k, cls)
                    v, f = vertical(j, k, cls)
                    vm, fm, rm = before[n : n + 3]
                    n += 3
                    den = vreg(dh, i0) + vm + v
                    src = vreg(sh, i0) + f - fm
                    r = lax.rsqrt(den)
                    place = fix(ft, base + j, k, cls)
                    rr[pl.ds(place, SUB), :] = r
                    ss[pl.ds(place, SUB), :] = src * r
                    aa[pl.ds(place, SUB), :] = vm * (r * rm)
                    root.append(r)
                    after += [v, f, r]
                for cls in range(CLASSES):
                    other = root[cls + 1] if cls < CLASSES - 1 else roll_left(root[0])
                    i0 = gix(j, k, cls)
                    hlo[pl.ds(fix(ft, base + j, k, cls), SUB), :] = vreg(hle, i0) * (root[cls] * other)
            return after

        def phase_c(k):
            start = []
            for cls in range(CLASSES):
                above = jnp.zeros((SUB, LANES), F32)
                if resume is not None:
                    above = jnp.where(resume, vreg(rr, fix(ft, base, k, cls)), above)
                start += [*vertical(0, k, cls), above]

            def body(i, c):
                for u in range(uc):
                    c = stencil(1 + i * uc + u, [k], c)
                return tuple(c)

            lax.fori_loop(0, (count - 4) // uc, body, tuple(start))

        for k in range(K):
            phase_c(k)
        return carry

    lax.fori_loop(0, NB, block, 0)


def work_scratch(count):
    group = K * CLASSES * SUB
    v2 = lambda rows: pltpu.VMEM((rows, LANES), F32)
    return [v2(count * group)] * 2 + [v2((count - 2) * group)] * 6


def weight_kernel(wraw, msk, wf, perm_ref):
    dates = msk.shape[1]
    R = wraw.shape[2]
    NF = dates // SUB
    perm_ref[...] = perm_matrix(False)
    pairs = K * dates
    WR = K * NF * 2 * SUB + 1

    def weights(i, c):
        p0 = i * UW
        rows = [
            wraw[half, pl.ds(p0, UW)].reshape(UW * R, LANES).astype(F32).astype(BF16) for half in range(2)
        ]
        out = jnp.dot(jnp.concatenate(rows, axis=1), perm_ref[...], preferred_element_type=F32)
        for n in range(UW):
            f, k = i * (UW // K) + n // K, n % K
            t, sub = f // SUB, f % SUB
            for block in range(R // SUB):
                for half in range(2):
                    x = out[n * R + block * SUB : n * R + (block + 1) * SUB, half * LANES : (half + 1) * LANES]
                    place = ((k * NF + t) * 2 + half) * SUB + sub + block * SUB * WR
                    wf[pl.ds(place, SUB, stride=WR), :] = x
        return c

    lax.fori_loop(0, pairs // UW, weights, 0)
    for row in range(R):
        for k in range(K):
            for t in range(NF):
                if (t + 1) * SUB + SPAN - 1 >= dates:
                    for half in range(2):
                        place = row * WR + ((k * NF + t) * 2 + half) * SUB
                        wf[pl.ds(place, SUB), :] = wf[pl.ds(place, SUB), :] * msk[2 + k, pl.ds(t * SUB, SUB), :]


def inner_kernel(
    own_ref, near_ref, rest_ref, lmsk, rr, ss, aa, hlo,
    img, cre, cim, zre, zim, mag, hle, dh, sh,
):
    R = own_ref.shape[0] // 2
    H = HALO
    NZ = R + 2 * H - 2
    side = lax.axis_index("date")
    row0 = (R - H) * side
    far = R * side
    run(H, UH, lambda i: place_images(img, side, far + i, own_ref, row0 + far + i, near_ref, i))
    far = H * (1 - side)
    run(R, UI, lambda i: place_images(img, side, far + i, own_ref, row0 + far + i, rest_ref, i))
    construct(
        img, lmsk, R + H, H * (1 - side), (), None, UNROLL_1,
        (cre, cim, zre, zim, mag, hle, dh, sh), (rr, ss, aa, hlo), NZ,
    )


def outer_kernel(
    own_ref, near_ref, halo_ref, msk, lmsk, rr_in, ss_in, aa_in, hlo_in, wf,
    out_hbm, rr, ss, aa, hlo,
    img, cre, cim, zre, zim, mag, hle, dh, sh, ya, yb, yc, yy,
    vv, aw, ag, wk, vfin, fbuf, obuf, perm_ref, osem,
):
    dates = 2 * own_ref.shape[3]
    R = own_ref.shape[0] // 2
    H = HALO
    NR = R + 2 * H
    NZ = NR - 2
    NF = dates // SUB
    NB = NF // 2
    side = lax.axis_index("date")
    tile = lax.axis_index("tile")
    tiles = lax.axis_size("tile")
    zero = jnp.zeros((SUB, LANES), F32)
    low = lane_masks()[0]
    WR = K * NF * 2 * SUB + 1

    count = H + MORE
    base = (NR - count) * side
    run(H, UH, lambda i: place_images(img, side, MORE * side + i, halo_ref.at[1], i, halo_ref.at[0], i))
    row0 = (2 * R - MORE) * side
    run(
        MORE, MORE,
        lambda i: place_images(
            img, side, H * (1 - side) + i, own_ref, row0 + i, near_ref, (H - MORE) * side + i
        ),
    )
    outside = (
        ((tile == 0) & (side == 0), H - 2),
        ((tile == tiles - 1) & (side == 1), H - 1 + R - (NR - count)),
    )
    construct(
        img, lmsk, count, base, outside, side == 1, UNROLL_2,
        (cre, cim, zre, zim, mag, hle, dh, sh), (rr, ss, aa, hlo), NZ,
    )

    def sweep_block(ft, carry):
        def at(ref, row, k, cls):
            if any(ref is x for x in (ya, yb, yc)):
                return gix(row, k, cls)
            return al((((ft * NZ + row) * K + k) * CLASSES + cls) * SUB)

        def sweeps(i, c):
            ks = [i * KS + u for u in range(KS)]
            steps = []
            buffers = [ya, yb, yc]
            held = ss
            power = SWEEPS // 2
            while power >= 1:
                source = held
                for n in range(power):
                    free = [x for x in buffers if x is not source and x is not held]
                    steps.append((source, held if n == power - 1 else None, free[0]))
                    source = free[0]
                held = source
                power //= 2
            for n, (source, added, target) in enumerate(steps):
                left = len(steps) - 1 - n
                classes = range(CLASSES)
                get = lambda ref, row, k: [vreg(ref, at(ref, row, k, cls)) for cls in classes]
                top = H - 1 - left
                window = [
                    ([None, get(source, top - 1, k), get(source, top, k)], [None, get(aa, top, k)]) for k in ks
                ]
                for j in range(H - 1 - left, H - 1 + R + left):
                    for u, k in enumerate(ks):
                        y, links = window[u]
                        y = [y[1], y[2], get(source, j + 1, k)]
                        links = [links[1], get(aa, j + 1, k)]
                        window[u] = y, links
                        h = get(hlo, j, k)
                        right = [h[cls] * y[1][cls + 1] for cls in range(CLASSES - 1)] + [h[3] * roll_left(y[1][0])]
                        back = [roll_right(h[3] * y[1][3])] + [h[cls] * y[1][cls] for cls in range(CLASSES - 1)]
                        new = []
                        for cls in range(CLASSES):
                            x = links[0][cls] * y[0][cls] + links[1][cls] * y[2][cls]
                            if added is not None:
                                x = x + (y[1][cls] if added is source else vreg(added, at(added, j, k, cls)))
                            if cls in (0, CLASSES - 1):
                                x = (x + right[cls]) + back[cls] if cls == 0 else (x + back[cls]) + right[cls]
                            else:
                                x = x + (right[cls] + back[cls])
                            new.append(x)
                        if left:
                            for cls in range(CLASSES):
                                target[pl.ds(gix(j, k, cls), SUB), :] = new[cls]
                        else:
                            row = j - (H - 1)
                            scaled = [
                                new[cls] * (vreg(rr, at(rr, j, k, cls)) * (1.0 / residual_scale))
                                for cls in range(CLASSES)
                            ]
                            for pair in range(2):
                                even, odd = scaled[2 * pair], scaled[2 * pair + 1]
                                crossed = swap_halves(jnp.where(low, odd, even))
                                first = jnp.where(low, even, crossed)
                                second = jnp.where(low, crossed, odd)
                                for upper, value in enumerate((first, second)):
                                    place = (((row * K + k) * NF + upper * NB + ft) * 2 + pair) * SUB
                                    yy[pl.ds(al(place), SUB), :] = value
            return c

        def two(i, c):
            sweeps(2 * i, 0)
            sweeps(2 * i + 1, 0)
            return c

        lax.fori_loop(0, K // 2, two, 0)
        return carry

    lax.fori_loop(0, NB, sweep_block, 0)

    damping = solve_damping * 255.0
    inv_span = 1.0 / SPAN
    for u in range(vv.shape[0]):
        for half in range(2):
            vv[u, half, pl.ds(dates, SUB), :] = zero
            for m in range(SPAN):
                aw[u, half, m, pl.ds(0, SUB), :] = zero
                ag[u, half, m, pl.ds(0, SUB), :] = zero

    groups = [(t, half) for t in range(NF) for half in range(2)]

    def spread(ref, u, t, half, q):
        m_1 = vreg(msk.at[0], t * SUB)
        m_2 = vreg(msk.at[1], t * SUB)
        q0, q1, q2, q3 = q
        two = q2 + q3
        a1 = two + q1
        for m, value in enumerate(
            (a1 + q0, a1, jnp.where(m_1 > 0.5, two, a1), jnp.where(m_2 > 0.5, two, q3), q3)
        ):
            ref[u, half, m, pl.ds(SUB + t * SUB, SUB), :] = value

    def collect(ref, u, t, half):
        total = ref[u, half, 0, pl.ds(SUB + t * SUB, SUB), :]
        for m in range(1, SPAN):
            total = total + ref[u, half, m, pl.ds(SUB + t * SUB - m, SUB), :]
        return total

    def residual(u, row, t, half):
        y = [vreg(yy, al((((row * K + k) * NF + t) * 2 + half) * SUB)) for k in range(K)]
        s = [vv[u, half, pl.ds(t * SUB + m, SUB), :] for m in range(SPAN)]
        for m in range(1, SPAN):
            s[m] = s[m - 1] + s[m]
        m_1 = vreg(msk.at[0], t * SUB) > 0.5
        m_2 = vreg(msk.at[1], t * SUB) > 0.5
        model = (s[0], jnp.where(m_1, s[1], s[2]), jnp.where(m_2, s[3], s[2]), s[4])
        return [a - b for a, b in zip(y, model)]

    U = vv.shape[0]

    def invert_rows(i, c):
        rows = [(u, i * U + u) for u in range(U)]
        inverse = {}
        for p in range(PASSES):
            for step in range(STEPS):
                start = p == 0 and step == 0
                for u, row in rows:
                    for t, half in groups:
                        if start:
                            res = [
                                vreg(yy, al((((row * K + k) * NF + t) * 2 + half) * SUB)) for k in range(K)
                            ]
                        else:
                            res = residual(u, row, t, half)
                        g = []
                        w_all = []
                        for k in range(K):
                            if step == 0:
                                place = row * WR + ((k * NF + t) * 2 + half) * SUB
                                w = vreg(wf, place) * (1.0 / (1.0 + res[k] * res[k]))
                                wk[u, t, half, k] = w
                                w_all.append(w)
                            else:
                                w = wk[u, t, half, k]
                            g.append(w * res[k])
                        if step == 0:
                            spread(aw, u, t, half, w_all)
                        spread(ag, u, t, half, g)
                for u, row in rows:
                    for t, half in groups:
                        if step == 0:
                            inverse[u, t, half] = inv_span / (collect(aw, u, t, half) + damping)
                        grad = collect(ag, u, t, half)
                        place = pl.ds(t * SUB, SUB)
                        if start:
                            v = grad * inverse[u, t, half]
                        else:
                            old = vv[u, half, place, :]
                            v = old + (grad - damping * old) * inverse[u, t, half]
                        if p == PASSES - 1 and step == STEPS - 1:
                            vfin[row, half, place, :] = v * residual_scale
                        else:
                            vv[u, half, place, :] = v
        return c

    perm_ref[...] = perm_matrix(True)
    unknowns = dates - 1
    OP = dates + 1

    def finish(first):
        split = [[], [], []]
        for u in range(SUB):
            rest = jnp.concatenate([vfin[first + u, 0], vfin[first + u, 1]], axis=1)
            for part in split:
                part.append(rest.astype(BF16))
                rest = rest - part[-1].astype(F32)
        out = None
        for part in split:
            x = jnp.dot(jnp.concatenate(part, axis=0), perm_ref[...], preferred_element_type=F32)
            out = x if out is None else out + x
        for u in range(SUB):
            for half in range(2):
                fbuf[half, pl.ds(u * OP, dates), :] = out[
                    u * dates : (u + 1) * dates, half * LANES : (half + 1) * LANES
                ]
        for j in range(unknowns):
            for half in range(2):
                obuf[half, j, pl.ds(first, SUB), :] = fbuf[half, pl.ds(j, SUB, stride=OP), :]

    outs = []
    for first in range(0, R, SUB):
        lax.fori_loop(first // U, (first + SUB) // U, invert_rows, 0)
        finish(first)
        for half in range(2):
            copy = pltpu.make_async_copy(
                obuf.at[half, pl.ds(0, unknowns), pl.ds(first, SUB)],
                out_hbm.at[:, pl.ds(first, SUB), pl.ds(half * LANES, LANES)],
                osem.at[first // SUB, half],
            )
            copy.start()
            outs.append(copy)
    for copy in outs:
        copy.wait()


def weigh(wraw, msk):
    _, pairs, R, _ = wraw.shape
    vm = pl.BlockSpec(memory_space=pltpu.VMEM)
    return pl.pallas_call(
        weight_kernel,
        out_shape=pltpu.VMEM((R * (2 * pairs + 1), LANES), F32),
        in_specs=[vm, vm],
        out_specs=vm,
        scratch_shapes=[pltpu.VMEM((2 * LANES, 2 * LANES), BF16)],
        name="weigh",
        compiler_params=pltpu.CompilerParams(vmem_limit_bytes=4 * 1024 * 1024),
    )(wraw, msk)


def solve(own, near, rest, halo, msk, lmsk, wf):
    tile_rows = own.shape[0]
    dates = 2 * own.shape[3]
    R = tile_rows // 2
    columns = 2 * LANES
    H = HALO
    NZ = R + 2 * H - 2
    NF = dates // SUB
    group = K * CLASSES * SUB
    image = 2 * CLASSES * (dates // 2 + SUB)
    vm = pl.BlockSpec(memory_space=pltpu.VMEM)
    hbm = pl.BlockSpec(memory_space=pl.ANY)
    U = 2
    v2 = lambda rows: pltpu.VMEM((rows, LANES), F32)
    stencil = [v2(NF // 2 * NZ * group)] * 4
    inner = pl.pallas_call(
        inner_kernel,
        out_shape=tuple(stencil),
        in_specs=[vm] * 4,
        out_specs=(vm,) * 4,
        scratch_shapes=[
            v2((R + H) * image),
            *work_scratch(R + H),
        ],
        name="inner",
        compiler_params=pltpu.CompilerParams(vmem_limit_bytes=24 * 1024 * 1024),
    )
    rr, ss, aa, hlo = inner(own, near, rest, lmsk)
    outer = pl.pallas_call(
        outer_kernel,
        out_shape=(jax.ShapeDtypeStruct((dates - 1, R, columns), F32), *stencil),
        in_specs=[vm] * 10,
        out_specs=(hbm,) + (vm,) * 4,
        input_output_aliases={5: 1, 6: 2, 7: 3, 8: 4},
        scratch_shapes=[
            v2((H + MORE) * image),
            *work_scratch(H + MORE),
            v2(NZ * group), v2(NZ * group), v2(NZ * group),
            v2(R * NF * K * 2 * SUB),
            pltpu.VMEM((U, 2, dates + SUB, LANES), F32),
            pltpu.VMEM((U, 2, SPAN, dates + SUB, LANES), F32),
            pltpu.VMEM((U, 2, SPAN, dates + SUB, LANES), F32),
            pltpu.VMEM((U, NF, 2, K, SUB, LANES), F32),
            pltpu.VMEM((R, 2, dates, LANES), F32),
            pltpu.VMEM((2, SUB * (dates + 1), LANES), F32),
            pltpu.VMEM((2, dates, R, LANES), F32),
            pltpu.VMEM((columns, columns), BF16),
            pltpu.SemaphoreType.DMA((R // SUB, 2)),
        ],
        name="outer",
        compiler_params=pltpu.CompilerParams(vmem_limit_bytes=28 * 1024 * 1024),
    )
    return outer(own, near, halo, msk, lmsk, rr, ss, aa, hlo, wf)[0]


def local(slc_real, slc_imag, pair_offset, pair_weight):
    tiles = lax.axis_size("tile")
    swap = [(0, 1), (1, 0)]
    moves = [(2 * t + 1, 2 * t + 2) for t in range(tiles - 1)] + [(2 * t + 2, 2 * t + 1) for t in range(tiles - 1)]
    own, near, rest, msk, lmsk, wraw = pack(slc_real, slc_imag, pair_offset.T, pair_weight)
    near = lax.ppermute(near, "date", swap)
    rest = lax.ppermute(rest, "date", swap)
    sent = edges(own, near)
    halo = lax.ppermute(sent, ("tile", "date"), moves)
    wf = weigh(wraw, msk)
    return solve(own, near, rest, halo, msk, lmsk, wf)


def solution(mesh):
    placed = (
        P("date", ("scene", "tile"), None),
        P("date", ("scene", "tile"), None),
        P(),
        P(None, ("scene", "tile", "date"), None),
    )
    return jax.shard_map(
        local,
        mesh=mesh,
        in_specs=placed,
        out_specs=P(None, ("scene", "tile", "date"), None),
        check_vma=False,
    )
```

```python
import jax
import jax.numpy as jnp
from jax import lax
from jax.experimental import pallas as pl
from jax.experimental.pallas import tpu as pltpu
from jax.sharding import PartitionSpec as P


K = 4
SPAN = 5
SWEEPS = 8
PASSES = 3
STEPS = 2

unwrap_damping = 0.08
column_weight = 0.15
solve_damping = 0.1
residual_scale = 0.3

LANES = 128
SUB = 8
CLASSES = 4
GROUPS = 64
UI, UH, UW, KS = 4, 3, 32, 1
UNROLL_1 = (25, 4, 7)
UNROLL_2 = (14, 3, 10)
MORE = 5
HALO = SWEEPS + 1
F32 = jnp.float32
BF16 = jnp.bfloat16


def al(x):
    return pl.multiple_of(x, SUB)


def vreg(ref, row):
    return ref[pl.ds(row, SUB), :]


def perm_matrix(transpose, swap=0):
    n = CLASSES * GROUPS
    a = lax.broadcasted_iota(jnp.int32, (n, n), 0)
    b = lax.broadcasted_iota(jnp.int32, (n, n), 1)
    col, place = (b, a) if transpose else (a, b)
    target = ((col % CLASSES) ^ swap) * GROUPS + col // CLASSES
    return jnp.where(place == target, 1.0, 0.0).astype(BF16)


def pack_kernel(
    re_hbm, im_hbm, offset_hbm, all_ref, near_ref, rest_ref, msk, lmsk,
    images, offset_ref, flat, turned, perm_ref, sems,
):
    _, dates, rows, columns = images.shape
    side = lax.axis_index("date")
    copies = [
        pltpu.make_async_copy(re_hbm, images.at[0], sems.at[0]),
        pltpu.make_async_copy(im_hbm, images.at[1], sems.at[1]),
        pltpu.make_async_copy(offset_hbm, offset_ref, sems.at[2]),
    ]
    for copy in copies:
        copy.start()
    perm_ref[...] = perm_matrix(False, side)
    CH = dates // 2
    pitch = rows + 1
    for part in range(2):
        copies[part].wait()
        for first in range(0, dates, CH):
            block = images[part, first : first + CH].reshape(CH * rows, columns)
            out = jnp.dot(block, perm_ref[...], preferred_element_type=F32)
            for n in range(CH):
                for half in range(2):
                    flat[part, half, pl.ds((first + n) * pitch, rows), :] = out[
                        n * rows : (n + 1) * rows, half * LANES : (half + 1) * LANES
                    ]
    RW = 8

    def turn(i, c):
        for u in range(RW):
            row = i * RW + u
            for part in range(2):
                for half in range(2):
                    tile = flat[part, half, pl.ds(row, dates, stride=pitch), :]
                    all_ref[row, part, half] = tile.astype(BF16)
        return c

    lax.fori_loop(0, rows // RW, turn, 0)
    near = near_ref.shape[0]
    rest = rest_ref.shape[0]
    for i in range(near):
        near_ref[i] = all_ref[(rows - near) * (1 - side) + i]
    for i in range(rest):
        rest_ref[i] = all_ref[near * side + (rows - near - rest) * (1 - side) + i]
    copies[2].wait()
    offset_masks(offset_ref, msk, lmsk, turned)


def pack(slc_real, slc_imag, offsets):
    dates, rows, columns = slc_real.shape
    inputs = [pltpu.with_memory_space_constraint(x, pltpu.HBM) for x in (slc_real, slc_imag, offsets)]
    vm = pl.BlockSpec(memory_space=pltpu.VMEM)
    hbm = pl.BlockSpec(memory_space=pltpu.HBM)
    per_date, all_dates = offsets.shape
    return pl.pallas_call(
        pack_kernel,
        out_shape=(
            pltpu.VMEM((rows, 2, 2, dates, LANES), BF16),
            pltpu.VMEM((HALO, 2, 2, dates, LANES), BF16),
            pltpu.VMEM((rows // 2, 2, 2, dates, LANES), BF16),
            pltpu.VMEM((2 + per_date, all_dates, LANES), F32),
            pltpu.VMEM((2, all_dates // 2, LANES), F32),
        ),
        in_specs=[hbm] * 3,
        out_specs=(vm,) * 5,
        scratch_shapes=[
            pltpu.VMEM((2, dates, rows, columns), BF16),
            pltpu.VMEM(offsets.shape, jnp.int32),
            pltpu.VMEM((2, 2, dates * (rows + 1), LANES), F32),
            pltpu.VMEM((SUB, LANES), F32),
            pltpu.VMEM((columns, columns), BF16),
            pltpu.SemaphoreType.DMA((3,)),
        ],
        name="pack",
        compiler_params=pltpu.CompilerParams(vmem_limit_bytes=12 * 1024 * 1024),
    )(*inputs)


def edge_kernel(own_ref, near_ref, sent_ref):
    side = lax.axis_index("date")
    first = (own_ref.shape[0] - HALO) * side
    for i in range(HALO):
        sent_ref[0, i] = own_ref[first + i]
        sent_ref[1, i] = near_ref[i]


def edges(own, near):
    vm = pl.BlockSpec(memory_space=pltpu.VMEM)
    return pl.pallas_call(
        edge_kernel,
        out_shape=pltpu.VMEM((2, HALO, *own.shape[1:]), own.dtype),
        in_specs=[vm, vm],
        out_specs=vm,
        name="edges",
        compiler_params=pltpu.CompilerParams(vmem_limit_bytes=4 * 1024 * 1024),
    )(own, near)


def gix(row, k, cls):
    return al(((row * K + k) * CLASSES + cls) * SUB)


def roll_right(x):
    return pltpu.roll(x, 1, 1)


def roll_left(x):
    return pltpu.roll(x, LANES - 1, 1)


def swap_halves(x):
    return pltpu.roll(x, GROUPS, 1)


def run(count, unroll, step):
    def body(i, c):
        for u in range(unroll):
            step(i * unroll + u)
        return c

    whole = count // unroll
    lax.fori_loop(0, whole, body, 0)
    for n in range(whole * unroll, count):
        step(n)


def lane_masks():
    lane = lax.broadcasted_iota(jnp.int32, (SUB, LANES), 1)
    return lane < GROUPS, lane % GROUPS == 0, lane % GROUPS == GROUPS - 1


def offset_masks(offset_ref, msk, lmsk, turned):
    dates = offset_ref.shape[1]
    turned[...] = jnp.zeros(turned.shape, F32)
    turned[pl.ds(0, K), pl.ds(0, dates)] = offset_ref[...].astype(F32)
    offsets = jnp.transpose(turned[...])[:dates]
    first = lax.broadcasted_iota(jnp.int32, (dates, 1), 0).astype(F32)
    tests = [offsets[:, 1:2] == 2.0, offsets[:, 2:3] == 4.0]
    tests += [first + offsets[:, k : k + 1] < dates for k in range(K)]
    for n, test in enumerate(tests[: msk.shape[0]]):
        msk[n] = jnp.broadcast_to(jnp.where(test, 1.0, 0.0).astype(F32), (dates, LANES))
    if lmsk is not None:
        half = dates // 2
        low = lax.broadcasted_iota(jnp.int32, (half, LANES), 1) < GROUPS
        for n in range(2):
            lmsk[n] = jnp.where(low, msk[n, :half], msk[n, half:])


def place_images(img, side, row, mine_ref, mine_row, other_ref, other_row):
    half_dates = mine_ref.shape[3]
    DP = half_dates + SUB
    own = (lax.broadcasted_iota(jnp.int32, (half_dates, LANES), 1) // GROUPS) == side
    low = lane_masks()[0]
    third = 1.0 / 3.0
    for part in range(2):
        for pair in range(2):
            mine = mine_ref[mine_row, part, pair].astype(F32) * third
            other = other_ref[other_row, part, pair].astype(F32) * third
            for odd in range(2):
                if odd:
                    x = swap_halves(jnp.where(own, other, mine))
                else:
                    x = jnp.where(own, mine, other)
                base = ((row * 2 + part) * CLASSES + pair * 2 + odd) * DP
                img[pl.ds(al(base), half_dates), :] = x
                img[pl.ds(al(base + half_dates), SUB), :] = jnp.where(low, swap_halves(x[:SUB]), 0.0)


def construct(img, lmsk, count, base, outside, resume, unroll, work, outs, NZ):
    cre, cim, zre, zim, mag, hle, dh, sh = work
    rr, ss, aa, hlo = outs
    DP = lmsk.shape[1] + SUB
    NB = lmsk.shape[1] // SUB
    _, at_first, at_last = lane_masks()
    ua, ub, uc = unroll
    fix = lambda ft, row, k, cls: al((((ft * NZ + row) * K + k) * CLASSES + cls) * SUB)

    def block(ft, carry):
        f0 = al(ft * SUB)

        def form(rho):
            sel1 = vreg(lmsk.at[0], f0) > 0.5
            sel2 = vreg(lmsk.at[1], f0) > 0.5

            def image(part, cls, shift):
                return vreg(img, ((rho * 2 + part) * CLASSES + cls) * DP + f0 + shift)

            pair = {}
            for cls in range(CLASSES):
                a_re, a_im = image(0, cls, 0), image(1, cls, 0)
                second = [(image(0, cls, o), image(1, cls, o)) for o in range(1, SPAN + 1)]
                pick = lambda mask, i, j: tuple(
                    jnp.where(mask, x, y) for x, y in zip(second[i - 1], second[j - 1])
                )
                chosen = (second[0], pick(sel1, 2, 3), pick(sel2, 4, 3), second[4])
                for k in range(K):
                    b_re, b_im = chosen[k]
                    pair[0, k, cls] = a_re * b_re + a_im * b_im
                    pair[1, k, cls] = a_im * b_re - a_re * b_im
            for part, ref in enumerate((cre, cim)):
                for k in range(K):
                    x = [pair[part, k, cls] for cls in range(CLASSES)]
                    x01, x23 = x[0] + x[1], x[2] + x[3]
                    sums = (
                        x01 + jnp.where(at_first, 0.0, roll_right(x[3])),
                        x01 + x[2],
                        x[1] + x23,
                        x23 + jnp.where(at_last, 0.0, roll_left(x[0])),
                    )
                    for cls in range(CLASSES):
                        ref[pl.ds(gix(rho, k, cls), SUB), :] = sums[cls]

        run(count, ua, form)

        def edge(m, cross, scale):
            q = 1.0 / (m + 1.0)
            link = m * q
            if scale is not None:
                link = link * scale
            return link, link * (cross * q)

        def smooth(j, rows):
            for k in range(K):
                sums = [{}, {}]
                for part, ref in enumerate((cre, cim)):
                    for cls in range(CLASSES):
                        c = [vreg(ref, gix(j + d, k, cls)) for d in range(rows + 2)]
                        middle = c[1] + c[2]
                        sums[part][0, cls] = c[0] + middle
                        if rows == 2:
                            sums[part][1, cls] = middle + c[3]
                for d in range(rows):
                    smooth_row(j + d, k, [[sums[part][d, cls] for cls in range(CLASSES)] for part in range(2)])

        def smooth_row(j, k, sums):
            re, im = sums
            mg = []
            for cls in range(CLASSES):
                i0 = gix(j, k, cls)
                sq = re[cls] * re[cls] + im[cls] * im[cls]
                mg.append(sq * lax.rsqrt(jnp.maximum(sq, 1e-30)))
                zre[pl.ds(i0, SUB), :] = re[cls]
                zim[pl.ds(i0, SUB), :] = im[cls]
                mag[pl.ds(i0, SUB), :] = mg[cls]
            links, flows = [], []
            for cls in range(CLASSES):
                if cls < CLASSES - 1:
                    n_re, n_im, m = re[cls + 1], im[cls + 1], mg[cls] * mg[cls + 1]
                else:
                    n_re, n_im = roll_left(re[0]), roll_left(im[0])
                    m = jnp.where(at_last, 0.0, mg[cls] * roll_left(mg[0]))
                link, flow = edge(m, im[cls] * n_re - re[cls] * n_im, column_weight)
                hle[pl.ds(gix(j, k, cls), SUB), :] = link
                links.append(link)
                flows.append(flow)
            mid = links[1] + unwrap_damping
            end = links[3] + unwrap_damping
            dens = (links[0] + roll_right(end), links[0] + mid, mid + links[2], links[2] + end)
            srcs = (
                flows[0] - roll_right(flows[3]),
                flows[1] - flows[0],
                flows[2] - flows[1],
                flows[3] - flows[2],
            )
            for cls in range(CLASSES):
                dh[pl.ds(gix(j, k, cls), SUB), :] = dens[cls]
                sh[pl.ds(gix(j, k, cls), SUB), :] = srcs[cls]

        run((count - 2) // 2, ub, lambda i: smooth(2 * i, 2))
        if count % 2:
            smooth(count - 3, 1)

        for condition, row in outside:
            @pl.when(condition)
            def _():
                for k in range(K):
                    for cls in range(CLASSES):
                        mag[pl.ds(gix(row, k, cls), SUB), :] = jnp.zeros((SUB, LANES), F32)

        def vertical(j, k, cls):
            i0, i1 = gix(j, k, cls), gix(j + 1, k, cls)
            m = vreg(mag, i0) * vreg(mag, i1)
            return edge(m, vreg(zim, i0) * vreg(zre, i1) - vreg(zre, i0) * vreg(zim, i1), None)

        def stencil(j, ks, before):
            after = []
            n = 0
            for k in ks:
                root = []
                for cls in range(CLASSES):
                    i0 = gix(j, k, cls)
                    v, f = vertical(j, k, cls)
                    vm, fm, rm = before[n : n + 3]
                    n += 3
                    den = vreg(dh, i0) + vm + v
                    src = vreg(sh, i0) + f - fm
                    r = lax.rsqrt(den)
                    place = fix(ft, base + j, k, cls)
                    rr[pl.ds(place, SUB), :] = r
                    ss[pl.ds(place, SUB), :] = src * r
                    aa[pl.ds(place, SUB), :] = vm * (r * rm)
                    root.append(r)
                    after += [v, f, r]
                for cls in range(CLASSES):
                    other = root[cls + 1] if cls < CLASSES - 1 else roll_left(root[0])
                    i0 = gix(j, k, cls)
                    hlo[pl.ds(fix(ft, base + j, k, cls), SUB), :] = vreg(hle, i0) * (root[cls] * other)
            return after

        def phase_c(k):
            start = []
            for cls in range(CLASSES):
                above = jnp.zeros((SUB, LANES), F32)
                if resume is not None:
                    above = jnp.where(resume, vreg(rr, fix(ft, base, k, cls)), above)
                start += [*vertical(0, k, cls), above]

            def body(i, c):
                for u in range(uc):
                    c = stencil(1 + i * uc + u, [k], c)
                return tuple(c)

            lax.fori_loop(0, (count - 4) // uc, body, tuple(start))

        for k in range(K):
            phase_c(k)
        return carry

    lax.fori_loop(0, NB, block, 0)


def work_scratch(count):
    group = K * CLASSES * SUB
    v2 = lambda rows: pltpu.VMEM((rows, LANES), F32)
    return [v2(count * group)] * 2 + [v2((count - 2) * group)] * 6


def permute_weights(wraw, msk, wf, perm_ref):
    dates = msk.shape[1]
    R = wraw.shape[2]
    NF = dates // SUB
    perm_ref[...] = perm_matrix(False)
    pairs = K * dates
    WR = K * NF * 2 * SUB + 1

    def weights(i, c):
        p0 = i * UW
        rows = [
            wraw[half, pl.ds(p0, UW)].reshape(UW * R, LANES).astype(F32).astype(BF16) for half in range(2)
        ]
        out = jnp.dot(jnp.concatenate(rows, axis=1), perm_ref[...], preferred_element_type=F32)
        for n in range(UW):
            f, k = i * (UW // K) + n // K, n % K
            t, sub = f // SUB, f % SUB
            for block in range(R // SUB):
                for half in range(2):
                    x = out[n * R + block * SUB : n * R + (block + 1) * SUB, half * LANES : (half + 1) * LANES]
                    place = ((k * NF + t) * 2 + half) * SUB + sub + block * SUB * WR
                    wf[pl.ds(place, SUB, stride=WR), :] = x
        return c

    lax.fori_loop(0, pairs // UW, weights, 0)
    for row in range(R):
        for k in range(K):
            for t in range(NF):
                if (t + 1) * SUB + SPAN - 1 >= dates:
                    for half in range(2):
                        place = row * WR + ((k * NF + t) * 2 + half) * SUB
                        wf[pl.ds(place, SUB), :] = wf[pl.ds(place, SUB), :] * msk[2 + k, pl.ds(t * SUB, SUB), :]


def inner_kernel(
    own_ref, near_ref, rest_ref, msk, lmsk, weight_hbm, rr, ss, aa, hlo, wf,
    img, cre, cim, zre, zim, mag, hle, dh, sh, wraw, perm_ref, wsem,
):
    copies = [
        pltpu.make_async_copy(weight_hbm.at[:, :, pl.ds(half * LANES, LANES)], wraw.at[half], wsem.at[half])
        for half in range(2)
    ]
    for copy in copies:
        copy.start()
    R = own_ref.shape[0] // 2
    H = HALO
    NZ = R + 2 * H - 2
    side = lax.axis_index("date")
    row0 = (R - H) * side
    far = R * side
    run(H, UH, lambda i: place_images(img, side, far + i, own_ref, row0 + far + i, near_ref, i))
    far = H * (1 - side)
    run(R, UI, lambda i: place_images(img, side, far + i, own_ref, row0 + far + i, rest_ref, i))
    construct(
        img, lmsk, R + H, H * (1 - side), (), None, UNROLL_1,
        (cre, cim, zre, zim, mag, hle, dh, sh), (rr, ss, aa, hlo), NZ,
    )
    for copy in copies:
        copy.wait()
    permute_weights(wraw, msk, wf, perm_ref)


def outer_kernel(
    own_ref, near_ref, halo_ref, msk, lmsk, rr_in, ss_in, aa_in, hlo_in, wf,
    out_hbm, rr, ss, aa, hlo,
    img, cre, cim, zre, zim, mag, hle, dh, sh, ya, yb, yc, yy,
    vv, aw, ag, wk, vfin, fbuf, obuf, perm_ref, osem,
):
    dates = 2 * own_ref.shape[3]
    R = own_ref.shape[0] // 2
    H = HALO
    NR = R + 2 * H
    NZ = NR - 2
    NF = dates // SUB
    NB = NF // 2
    side = lax.axis_index("date")
    tile = lax.axis_index("tile")
    tiles = lax.axis_size("tile")
    zero = jnp.zeros((SUB, LANES), F32)
    low = lane_masks()[0]
    WR = K * NF * 2 * SUB + 1

    count = H + MORE
    base = (NR - count) * side
    run(H, UH, lambda i: place_images(img, side, MORE * side + i, halo_ref.at[1], i, halo_ref.at[0], i))
    row0 = (2 * R - MORE) * side
    run(
        MORE, MORE,
        lambda i: place_images(
            img, side, H * (1 - side) + i, own_ref, row0 + i, near_ref, (H - MORE) * side + i
        ),
    )
    outside = (
        ((tile == 0) & (side == 0), H - 2),
        ((tile == tiles - 1) & (side == 1), H - 1 + R - (NR - count)),
    )
    construct(
        img, lmsk, count, base, outside, side == 1, UNROLL_2,
        (cre, cim, zre, zim, mag, hle, dh, sh), (rr, ss, aa, hlo), NZ,
    )

    def sweep_block(ft, carry):
        def at(ref, row, k, cls):
            if any(ref is x for x in (ya, yb, yc)):
                return gix(row, k, cls)
            return al((((ft * NZ + row) * K + k) * CLASSES + cls) * SUB)

        def sweeps(i, c):
            ks = [i * KS + u for u in range(KS)]
            steps = []
            buffers = [ya, yb, yc]
            held = ss
            power = SWEEPS // 2
            while power >= 1:
                source = held
                for n in range(power):
                    free = [x for x in buffers if x is not source and x is not held]
                    steps.append((source, held if n == power - 1 else None, free[0]))
                    source = free[0]
                held = source
                power //= 2
            for n, (source, added, target) in enumerate(steps):
                left = len(steps) - 1 - n
                classes = range(CLASSES)
                get = lambda ref, row, k: [vreg(ref, at(ref, row, k, cls)) for cls in classes]
                top = H - 1 - left
                window = [
                    ([None, get(source, top - 1, k), get(source, top, k)], [None, get(aa, top, k)]) for k in ks
                ]
                for j in range(H - 1 - left, H - 1 + R + left):
                    for u, k in enumerate(ks):
                        y, links = window[u]
                        y = [y[1], y[2], get(source, j + 1, k)]
                        links = [links[1], get(aa, j + 1, k)]
                        window[u] = y, links
                        h = get(hlo, j, k)
                        right = [h[cls] * y[1][cls + 1] for cls in range(CLASSES - 1)] + [h[3] * roll_left(y[1][0])]
                        back = [roll_right(h[3] * y[1][3])] + [h[cls] * y[1][cls] for cls in range(CLASSES - 1)]
                        new = []
                        for cls in range(CLASSES):
                            x = links[0][cls] * y[0][cls] + links[1][cls] * y[2][cls]
                            if added is not None:
                                x = x + (y[1][cls] if added is source else vreg(added, at(added, j, k, cls)))
                            if cls in (0, CLASSES - 1):
                                x = (x + right[cls]) + back[cls] if cls == 0 else (x + back[cls]) + right[cls]
                            else:
                                x = x + (right[cls] + back[cls])
                            new.append(x)
                        if left:
                            for cls in range(CLASSES):
                                target[pl.ds(gix(j, k, cls), SUB), :] = new[cls]
                        else:
                            row = j - (H - 1)
                            scaled = [
                                new[cls] * (vreg(rr, at(rr, j, k, cls)) * (1.0 / residual_scale))
                                for cls in range(CLASSES)
                            ]
                            for pair in range(2):
                                even, odd = scaled[2 * pair], scaled[2 * pair + 1]
                                crossed = swap_halves(jnp.where(low, odd, even))
                                first = jnp.where(low, even, crossed)
                                second = jnp.where(low, crossed, odd)
                                for upper, value in enumerate((first, second)):
                                    place = (((row * K + k) * NF + upper * NB + ft) * 2 + pair) * SUB
                                    yy[pl.ds(al(place), SUB), :] = value
            return c

        def two(i, c):
            sweeps(2 * i, 0)
            sweeps(2 * i + 1, 0)
            return c

        lax.fori_loop(0, K // 2, two, 0)
        return carry

    lax.fori_loop(0, NB, sweep_block, 0)

    damping = solve_damping * 255.0
    inv_span = 1.0 / SPAN
    for u in range(vv.shape[0]):
        for half in range(2):
            vv[u, half, pl.ds(dates, SUB), :] = zero
            for m in range(SPAN):
                aw[u, half, m, pl.ds(0, SUB), :] = zero
                ag[u, half, m, pl.ds(0, SUB), :] = zero

    groups = [(t, half) for t in range(NF) for half in range(2)]

    def spread(ref, u, t, half, q):
        m_1 = vreg(msk.at[0], t * SUB)
        m_2 = vreg(msk.at[1], t * SUB)
        q0, q1, q2, q3 = q
        two = q2 + q3
        a1 = two + q1
        for m, value in enumerate(
            (a1 + q0, a1, jnp.where(m_1 > 0.5, two, a1), jnp.where(m_2 > 0.5, two, q3), q3)
        ):
            ref[u, half, m, pl.ds(SUB + t * SUB, SUB), :] = value

    def collect(ref, u, t, half):
        total = ref[u, half, 0, pl.ds(SUB + t * SUB, SUB), :]
        for m in range(1, SPAN):
            total = total + ref[u, half, m, pl.ds(SUB + t * SUB - m, SUB), :]
        return total

    def residual(u, row, t, half):
        y = [vreg(yy, al((((row * K + k) * NF + t) * 2 + half) * SUB)) for k in range(K)]
        s = [vv[u, half, pl.ds(t * SUB + m, SUB), :] for m in range(SPAN)]
        for m in range(1, SPAN):
            s[m] = s[m - 1] + s[m]
        m_1 = vreg(msk.at[0], t * SUB) > 0.5
        m_2 = vreg(msk.at[1], t * SUB) > 0.5
        model = (s[0], jnp.where(m_1, s[1], s[2]), jnp.where(m_2, s[3], s[2]), s[4])
        return [a - b for a, b in zip(y, model)]

    U = vv.shape[0]

    def invert_rows(i, c):
        rows = [(u, i * U + u) for u in range(U)]
        inverse = {}
        for p in range(PASSES):
            for step in range(STEPS):
                start = p == 0 and step == 0
                for u, row in rows:
                    for t, half in groups:
                        if start:
                            res = [
                                vreg(yy, al((((row * K + k) * NF + t) * 2 + half) * SUB)) for k in range(K)
                            ]
                        else:
                            res = residual(u, row, t, half)
                        g = []
                        w_all = []
                        for k in range(K):
                            if step == 0:
                                place = row * WR + ((k * NF + t) * 2 + half) * SUB
                                w = vreg(wf, place) * (1.0 / (1.0 + res[k] * res[k]))
                                wk[u, t, half, k] = w
                                w_all.append(w)
                            else:
                                w = wk[u, t, half, k]
                            g.append(w * res[k])
                        if step == 0:
                            spread(aw, u, t, half, w_all)
                        spread(ag, u, t, half, g)
                for u, row in rows:
                    for t, half in groups:
                        if step == 0:
                            inverse[u, t, half] = inv_span / (collect(aw, u, t, half) + damping)
                        grad = collect(ag, u, t, half)
                        place = pl.ds(t * SUB, SUB)
                        if start:
                            v = grad * inverse[u, t, half]
                        else:
                            old = vv[u, half, place, :]
                            v = old + (grad - damping * old) * inverse[u, t, half]
                        if p == PASSES - 1 and step == STEPS - 1:
                            vfin[row, half, place, :] = v * residual_scale
                        else:
                            vv[u, half, place, :] = v
        return c

    perm_ref[...] = perm_matrix(True)
    unknowns = dates - 1
    OP = dates + 1

    def finish(first):
        split = [[], [], []]
        for u in range(SUB):
            rest = jnp.concatenate([vfin[first + u, 0], vfin[first + u, 1]], axis=1)
            for part in split:
                part.append(rest.astype(BF16))
                rest = rest - part[-1].astype(F32)
        out = None
        for part in split:
            x = jnp.dot(jnp.concatenate(part, axis=0), perm_ref[...], preferred_element_type=F32)
            out = x if out is None else out + x
        for u in range(SUB):
            for half in range(2):
                fbuf[half, pl.ds(u * OP, dates), :] = out[
                    u * dates : (u + 1) * dates, half * LANES : (half + 1) * LANES
                ]
        for j in range(unknowns):
            for half in range(2):
                obuf[half, j, pl.ds(first, SUB), :] = fbuf[half, pl.ds(j, SUB, stride=OP), :]

    outs = []
    for first in range(0, R, SUB):
        lax.fori_loop(first // U, (first + SUB) // U, invert_rows, 0)
        finish(first)
        for half in range(2):
            copy = pltpu.make_async_copy(
                obuf.at[half, pl.ds(0, unknowns), pl.ds(first, SUB)],
                out_hbm.at[:, pl.ds(first, SUB), pl.ds(half * LANES, LANES)],
                osem.at[first // SUB, half],
            )
            copy.start()
            outs.append(copy)
    for copy in outs:
        copy.wait()


def solve(own, near, rest, halo, msk, lmsk, pair_weight):
    dates = 2 * own.shape[3]
    pairs, R, columns = pair_weight.shape
    H = HALO
    NZ = R + 2 * H - 2
    NF = dates // SUB
    group = K * CLASSES * SUB
    image = 2 * CLASSES * (dates // 2 + SUB)
    vm = pl.BlockSpec(memory_space=pltpu.VMEM)
    hbm = pl.BlockSpec(memory_space=pl.ANY)
    U = 2
    v2 = lambda rows: pltpu.VMEM((rows, LANES), F32)
    stencil = [v2(NF // 2 * NZ * group)] * 4
    inner = pl.pallas_call(
        inner_kernel,
        out_shape=(*stencil, v2(R * (2 * pairs + 1))),
        in_specs=[vm] * 5 + [pl.BlockSpec(memory_space=pltpu.HBM)],
        out_specs=(vm,) * 5,
        scratch_shapes=[
            v2((R + H) * image),
            *work_scratch(R + H),
            pltpu.VMEM((2, pairs, R, LANES), jnp.int32),
            pltpu.VMEM((columns, columns), BF16),
            pltpu.SemaphoreType.DMA((2,)),
        ],
        name="inner",
        compiler_params=pltpu.CompilerParams(vmem_limit_bytes=24 * 1024 * 1024),
    )
    weights = pltpu.with_memory_space_constraint(pair_weight, pltpu.HBM)
    rr, ss, aa, hlo, wf = inner(own, near, rest, msk, lmsk, weights)
    outer = pl.pallas_call(
        outer_kernel,
        out_shape=(jax.ShapeDtypeStruct((dates - 1, R, columns), F32), *stencil),
        in_specs=[vm] * 10,
        out_specs=(hbm,) + (vm,) * 4,
        input_output_aliases={5: 1, 6: 2, 7: 3, 8: 4},
        scratch_shapes=[
            v2((H + MORE) * image),
            *work_scratch(H + MORE),
            v2(NZ * group), v2(NZ * group), v2(NZ * group),
            v2(R * NF * K * 2 * SUB),
            pltpu.VMEM((U, 2, dates + SUB, LANES), F32),
            pltpu.VMEM((U, 2, SPAN, dates + SUB, LANES), F32),
            pltpu.VMEM((U, 2, SPAN, dates + SUB, LANES), F32),
            pltpu.VMEM((U, NF, 2, K, SUB, LANES), F32),
            pltpu.VMEM((R, 2, dates, LANES), F32),
            pltpu.VMEM((2, SUB * (dates + 1), LANES), F32),
            pltpu.VMEM((2, dates, R, LANES), F32),
            pltpu.VMEM((columns, columns), BF16),
            pltpu.SemaphoreType.DMA((R // SUB, 2)),
        ],
        name="outer",
        compiler_params=pltpu.CompilerParams(vmem_limit_bytes=28 * 1024 * 1024),
    )
    return outer(own, near, halo, msk, lmsk, rr, ss, aa, hlo, wf)[0]


def local(slc_real, slc_imag, pair_offset, pair_weight):
    tiles = lax.axis_size("tile")
    swap = [(0, 1), (1, 0)]
    moves = [(2 * t + 1, 2 * t + 2) for t in range(tiles - 1)] + [(2 * t + 2, 2 * t + 1) for t in range(tiles - 1)]
    own, near, rest, msk, lmsk = pack(slc_real, slc_imag, pair_offset.T)
    near = lax.ppermute(near, "date", swap)
    rest = lax.ppermute(rest, "date", swap)
    sent = edges(own, near)
    halo = lax.ppermute(sent, ("tile", "date"), moves)
    return solve(own, near, rest, halo, msk, lmsk, pair_weight)


def solution(mesh):
    placed = (
        P("date", ("scene", "tile"), None),
        P("date", ("scene", "tile"), None),
        P(),
        P(None, ("scene", "tile", "date"), None),
    )
    return jax.shard_map(
        local,
        mesh=mesh,
        in_specs=placed,
        out_specs=P(None, ("scene", "tile", "date"), None),
        check_vma=False,
    )
```
